32 devices in a mesh: dp: 8 (over z, x), tp: 4 (over y, core).
Axes of the slice: x: 2, y: 2, z: 4, core: 2. Of those that a mesh axis runs over, the one named last changes fastest.
Arguments:
- layer_input: bfloat16 [4096, 768], P('dp'), may hold values from -6 to 6
- pair_lengths: int32 [16], P('dp'), may hold values from 32 to 256, as said below
- query_weight: bfloat16 [768, 768], P('dp', 'tp'), may hold values from -0.21875 to 0.21875
- query_bias: float32 [768], P('tp'), may hold values from -3 to 3
- key_weight: bfloat16 [768, 768], P('dp', 'tp'), may hold values from -0.21875 to 0.21875
- value_weight: bfloat16 [768, 768], P('dp', 'tp'), may hold values from -0.21875 to 0.21875
- value_bias: float32 [768], P('tp'), may hold values from -3 to 3
- out_weight: bfloat16 [768, 768], P('tp', 'dp'), may hold values from -1.5 to 1.5
- out_bias: float32 [768], replicated, may hold values from -3 to 3
- first_gain: float32 [768], replicated, may hold values from 0.5 to 1.5
- first_shift: float32 [768], replicated, may hold values from -2 to 2
- up_weight: bfloat16 [768, 3072], P('dp', 'tp'), may hold values from -0.21875 to 0.21875
- up_bias: float32 [3072], P('tp'), may hold values from -3 to 3
- down_weight: bfloat16 [3072, 768], P('tp', 'dp'), may hold values from -0.21875 to 0.21875
- down_bias: float32 [768], replicated, may hold values from -3 to 3
- second_gain: float32 [768], replicated, may hold values from 0.5 to 1.5
- second_shift: float32 [768], replicated, may hold values from -2 to 2
- out_grad: bfloat16 [4096, 768], P('dp'), may hold values from -6 to 6
- query_tangent: bfloat16 [768, 768], P('dp', 'tp'), may hold values from -0.21875 to 0.21875
- key_tangent: bfloat16 [768, 768], P('dp', 'tp'), may hold values from -0.21875 to 0.21875
- value_tangent: bfloat16 [768, 768], P('dp', 'tp'), may hold values from -0.21875 to 0.21875
- out_tangent: bfloat16 [768, 768], P('tp', 'dp'), may hold values from -1.5 to 1.5
- up_tangent: bfloat16 [768, 3072], P('dp', 'tp'), may hold values from -0.21875 to 0.21875
- down_tangent: bfloat16 [3072, 768], P('tp', 'dp'), may hold values from -0.21875 to 0.21875
Outputs:
- layer_output: bfloat16 [4096, 768], P('dp')
- input_grad: bfloat16 [4096, 768], P('dp')
- layer_output_jvp: bfloat16 [4096, 768], P('dp')
- query_weight_grad: float32 [768, 768], P('dp', 'tp')
- query_bias_grad: float32 [768], P('tp')
- key_weight_grad: float32 [768, 768], P('dp', 'tp')
- value_weight_grad: float32 [768, 768], P('dp', 'tp')
- value_bias_grad: float32 [768], P('tp')
- out_weight_grad: float32 [768, 768], P('tp', 'dp')
- out_bias_grad: float32 [768], replicated
- first_gain_grad: float32 [768], replicated
- first_shift_grad: float32 [768], replicated
- up_weight_grad: float32 [768, 3072], P('dp', 'tp')
- up_bias_grad: float32 [3072], P('tp')
- down_weight_grad: float32 [3072, 768], P('tp', 'dp')
- down_bias_grad: float32 [768], replicated
- second_gain_grad: float32 [768], replicated
- second_shift_grad: float32 [768], replicated
The draws below stay inside these ranges and needn't reach their ends.
Inputs may be any that keep to these rules, and one draw needn't show every extreme that they name: Slots 0 to pair_lengths[p] - 1 of pair p hold tokens, the rest are padding; some pair has length 256.
All inputs are finite; a program needn't handle non-finite values.
Results may differ from the reference program's by a relative error of at most 0.024.
Values may be sent and summed in bfloat16 or wider, within the bound.
No kernel may reach another device: no remote copies, remote signals or barrier semaphores. Data moves between devices by JAX's collectives and lax.ppermute only.
A program may use at most 128 MiB of HBM per device.

```python
import jax
import jax.numpy as jnp
from jax import lax

D = 768
HEADS = 12
HEAD = 64
FF = 3072
SEQ = 256
PAIRS_DEV = 2
PAIRS = 16
TOKENS = 4096
N_TP = 4


def draw_pair_lengths(key, part):
    counts = jax.random.randint(key, (PAIRS,), SEQ // 8, SEQ + 1)
    chosen = jax.random.randint(jax.random.fold_in(key, 7), (), 0, PAIRS)
    return counts.at[chosen].set(SEQ).astype(jnp.int32)


def steps_of(key, shape, cuts, low, top_value):
    level, own = 1.0, jax.random.fold_in(key, 6)
    for position, blocks in cuts:
        heights = jnp.exp(jax.random.uniform(jax.random.fold_in(own, position), (blocks,), jnp.float32, low / len(cuts), top_value / len(cuts)))
        level = level * jnp.repeat(heights, shape[position] // blocks).reshape([-1 if axis == position else 1 for axis in range(len(shape))])
    return level


def scatter_about(stream_key, shape, deviation, reach, split=(), kind=jnp.bfloat16):
    values = jax.random.normal(stream_key, shape, jnp.float32) * deviation
    if len(split) > 0:
        values = steps_of(stream_key, shape, split, -0.22, 0.18) * values
    return jnp.clip(values, min=-reach, max=reach).astype(kind)


def setup_inputs(seed: int = 0) -> dict:
    streams_of = jax.random.split(jax.random.key(seed), 25)
    return {
        "layer_input": scatter_about(streams_of[0], (TOKENS, D), 1.0, 6.0, ((0, 8),)),
        "pair_lengths": draw_pair_lengths(jax.random.fold_in(streams_of[24], 71), 0),
        "query_weight": scatter_about(streams_of[2], (D, D), D ** -0.5, 0.21875, ((0, 8), (1, 4))),
        "query_bias": scatter_about(streams_of[3], (D,), 0.5, 3.0, ((0, 4),), jnp.float32),
        "key_weight": scatter_about(streams_of[4], (D, D), D ** -0.5, 0.21875, ((0, 8), (1, 4))),
        "value_weight": scatter_about(streams_of[5], (D, D), D ** -0.5, 0.21875, ((0, 8), (1, 4))),
        "value_bias": scatter_about(streams_of[6], (D,), 0.5, 3.0, ((0, 4),), jnp.float32),
        "out_weight": scatter_about(streams_of[7], (D, D), (D // 48) ** -0.5, 1.5, ((0, 4), (1, 8))),
        "out_bias": scatter_about(streams_of[8], (D,), 0.5, 3.0, (), jnp.float32),
        "first_gain": jnp.clip(1.0 + 0.1 * jax.random.normal(streams_of[9], (D,), jnp.float32), 0.5, 1.5),
        "first_shift": scatter_about(streams_of[10], (D,), 0.3, 2.0, (), jnp.float32),
        "up_weight": scatter_about(streams_of[11], (D, FF), D ** -0.5, 0.21875, ((0, 8), (1, 4))),
        "up_bias": scatter_about(streams_of[12], (FF,), 0.5, 3.0, ((0, 4),), jnp.float32),
        "down_weight": scatter_about(streams_of[13], (FF, D), (FF // 4) ** -0.5, 0.21875, ((0, 4), (1, 8))),
        "down_bias": scatter_about(streams_of[14], (D,), 0.5, 3.0, (), jnp.float32),
        "second_gain": jnp.clip(1.0 + 0.1 * jax.random.normal(streams_of[15], (D,), jnp.float32), 0.5, 1.5),
        "second_shift": scatter_about(streams_of[16], (D,), 0.3, 2.0, (), jnp.float32),
        "out_grad": scatter_about(streams_of[17], (TOKENS, D), 1.0, 6.0, ((0, 8),)),
        "query_tangent": scatter_about(streams_of[18], (D, D), D ** -0.5, 0.21875, ((0, 8), (1, 4))),
        "key_tangent": scatter_about(streams_of[19], (D, D), D ** -0.5, 0.21875, ((0, 8), (1, 4))),
        "value_tangent": scatter_about(streams_of[20], (D, D), D ** -0.5, 0.21875, ((0, 8), (1, 4))),
        "out_tangent": scatter_about(streams_of[21], (D, D), (D // 48) ** -0.5, 1.5, ((0, 4), (1, 8))),
        "up_tangent": scatter_about(streams_of[22], (D, FF), D ** -0.5, 0.21875, ((0, 8), (1, 4))),
        "down_tangent": scatter_about(streams_of[23], (FF, D), (FF // 4) ** -0.5, 0.21875, ((0, 4), (1, 8))),
    }


@jax.custom_vjp
def low(v):
    return lax.optimization_barrier(v.astype(jnp.bfloat16)).astype(jnp.float32)

@jax.custom_vjp
def low_back(v):
    return v

def low_keep(v):
    return (low(v), None)

def low_pass(kept, grad):
    return (grad,)

def back_keep(v):
    return (v, None)

def back_low(kept, grad):
    return (low(grad),)
low.defvjp(low_keep, low_pass)
low_back.defvjp(back_keep, back_low)
EPSILON = 1e-06

def round_plain(v):
    return lax.optimization_barrier(v.astype(jnp.bfloat16)).astype(jnp.float32)

def keep_value(v):
    return v

def norm_apply(resid, gain, shift):
    center = resid - lax.optimization_barrier(jnp.mean(resid, axis=-1, keepdims=True))
    spread = lax.optimization_barrier(jnp.mean(center * center, axis=-1, keepdims=True))
    return center * lax.rsqrt(spread + EPSILON) * gain + shift

def forward(params, inputs, lengths, rounder, back_rounder):
    query_weight, query_bias, key_weight, value_weight, value_bias, out_weight, out_bias, first_gain, first_shift, up_weight, up_bias, down_weight, down_bias, second_gain, second_shift = params
    highest = lax.Precision.HIGHEST
    rows = inputs.shape[0]
    groups = rows // SEQ
    shape_heads = (groups, SEQ, HEADS, HEAD)
    queries = back_rounder(rounder(jnp.dot(inputs, query_weight, precision=highest) + query_bias)).reshape(shape_heads)
    keys = back_rounder(rounder(jnp.dot(inputs, key_weight, precision=highest))).reshape(shape_heads)
    values = back_rounder(rounder(jnp.dot(inputs, value_weight, precision=highest) + value_bias)).reshape(shape_heads)
    scores = back_rounder(jnp.einsum('pqhd,pkhd->phqk', queries, keys, precision=highest) * HEAD ** (-0.5))
    valid = lax.broadcasted_iota(jnp.int32, (groups, 1, 1, SEQ), 3) < lengths[:, None, None, None]
    scores = jnp.where(valid, scores, jnp.float32(-1e+30))
    top = lax.optimization_barrier(jnp.max(scores, axis=-1, keepdims=True))
    expo = jnp.exp(scores - top)
    probs = rounder(expo / lax.optimization_barrier(jnp.sum(expo, axis=-1, keepdims=True)))
    context = back_rounder(rounder(jnp.einsum('phqk,pkhd->pqhd', probs, values, precision=highest)))
    context = context.reshape(rows, N_TP, D // N_TP)
    parts = rounder(jnp.einsum('rgc,gcd->rgd', context, out_weight.reshape(N_TP, D // N_TP, D), precision=highest))
    attended = back_rounder(lax.optimization_barrier(jnp.sum(parts, axis=1))) + out_bias
    first = norm_apply(inputs + attended, first_gain, first_shift)
    upper = back_rounder(jnp.dot(rounder(first), up_weight, precision=highest)) + up_bias
    active = rounder(jax.nn.gelu(upper, approximate=False)).reshape(rows, N_TP, FF // N_TP)
    parts_down = rounder(jnp.einsum('rgf,gfd->rgd', active, down_weight.reshape(N_TP, FF // N_TP, D), precision=highest))
    lowered = back_rounder(lax.optimization_barrier(jnp.sum(parts_down, axis=1))) + down_bias
    return norm_apply(first + lowered, second_gain, second_shift)

def reference(layer_input, pair_lengths, query_weight, query_bias, key_weight, value_weight, value_bias, out_weight, out_bias, first_gain, first_shift, up_weight, up_bias, down_weight, down_bias, second_gain, second_shift, out_grad, query_tangent, key_tangent, value_tangent, out_tangent, up_tangent, down_tangent):
    params = tuple((w.astype(jnp.float32) for w in (query_weight, query_bias, key_weight, value_weight, value_bias, out_weight, out_bias, first_gain, first_shift, up_weight, up_bias, down_weight, down_bias, second_gain, second_shift)))
    zero_d = jnp.zeros((D,), jnp.float32)
    zero_ff = jnp.zeros((FF,), jnp.float32)
    tangents = (query_tangent.astype(jnp.float32), zero_d, key_tangent.astype(jnp.float32), value_tangent.astype(jnp.float32), zero_d, out_tangent.astype(jnp.float32), zero_d, zero_d, zero_d, up_tangent.astype(jnp.float32), zero_ff, down_tangent.astype(jnp.float32), zero_d, zero_d, zero_d)
    count = PAIRS // PAIRS_DEV
    group_rows = PAIRS_DEV * SEQ
    inputs_all = layer_input.astype(jnp.float32).reshape(count, group_rows, D)
    upstream_all = out_grad.astype(jnp.float32).reshape(count, group_rows, D)
    lengths_all = pair_lengths.reshape(count, PAIRS_DEV)

    def one_group(totals, item):
        inputs, lengths, upstream = item
        result, pull = jax.vjp(lambda prm, xin: forward(prm, xin, lengths, low, low_back), params, inputs)
        grads, input_grads = pull(upstream)
        _, along = jax.jvp(lambda prm: forward(prm, inputs, lengths, round_plain, keep_value), (params,), (tangents,))
        totals = jax.tree.map(lambda a, b: a + b, totals, grads)
        return (totals, (result.astype(jnp.bfloat16), input_grads.astype(jnp.bfloat16), along.astype(jnp.bfloat16)))
    zeros = jax.tree.map(jnp.zeros_like, params)
    totals, (outputs, input_grads, alongs) = lax.scan(one_group, zeros, (inputs_all, lengths_all, upstream_all))
    return (outputs.reshape(TOKENS, D), input_grads.reshape(TOKENS, D), alongs.reshape(TOKENS, D), totals[0], totals[1], totals[2], totals[3], totals[4], totals[5], totals[6], totals[7], totals[8], totals[9], totals[10], totals[11], totals[12], totals[13], totals[14])
```

```python
import jax
import jax.numpy as jnp
from jax import lax
from jax.sharding import PartitionSpec as P

HEAD = 64
SEQ = 256
EPSILON = 1e-06
SNAKE = (0, 2, 4, 6, 7, 5, 3, 1)
BF = jnp.bfloat16
F32 = jnp.float32


def dot(left, right, dims):
    return lax.dot_general(left, right, (dims, ((), ())), preferred_element_type=F32)


NN = ((1,), (0,))
NT = ((1,), (1,))
TN = ((0,), (0,))


def xor_pairs(size, bit):
    return [(i, i ^ bit) for i in range(size)]


def gather_rows(shard, dp):
    if dp != len(SNAKE):
        return lax.all_gather(shard, "dp", axis=0, tiled=True)
    size = len(SNAKE)
    ahead = [(SNAKE[i], SNAKE[(i + 1) % size]) for i in range(size)]
    behind = [(b, a) for a, b in ahead]
    place = [0] * size
    for position, device in enumerate(SNAKE):
        place[device] = position
    me = lax.axis_index("dp")
    own_place = jnp.array(place, jnp.int32)[me]
    order = jnp.array(SNAKE, jnp.int32)
    rows = shard.shape[0]
    whole = jnp.zeros((size * rows, shard.shape[1]), shard.dtype)
    whole = lax.dynamic_update_slice(whole, shard, (me * rows, 0))
    one = two = shard
    for step in range(1, size // 2 + 1):
        one = lax.ppermute(one, "dp", ahead)
        owner = order[(own_place - step) % size]
        whole = lax.dynamic_update_slice(whole, one, (owner * rows, 0))
        if step < size // 2:
            two = lax.ppermute(two, "dp", behind)
            owner = order[(own_place + step) % size]
            whole = lax.dynamic_update_slice(whole, two, (owner * rows, 0))
    return whole


def scatter_sum(part, tp):
    count, rows, width = part.shape
    me = lax.axis_index("tp")
    rest = part.reshape(count, tp, rows // tp, width)
    size = tp
    bit = 1
    while bit < tp:
        size = size // 2
        split = rest.reshape(count, size, 2, rows // tp, width)
        mine = (me // bit) % 2
        keep = lax.dynamic_index_in_dim(split, mine, 2, keepdims=False)
        send = lax.dynamic_index_in_dim(split, 1 - mine, 2, keepdims=False)
        came = lax.ppermute(send.astype(BF), "tp", xor_pairs(tp, bit))
        rest = keep.astype(F32) + came.astype(F32)
        bit = bit * 2
        if bit < tp:
            rest = rest.astype(BF)
    return rest.reshape(count, rows // tp, width)


def norm_parts(resid):
    center = resid - jnp.mean(resid, axis=-1, keepdims=True)
    inverse = lax.rsqrt(jnp.mean(center * center, axis=-1, keepdims=True) + EPSILON)
    return center * inverse, inverse


def norm_along(unit, inverse, along):
    shifted = along - jnp.mean(along, axis=-1, keepdims=True)
    return inverse * (shifted - unit * jnp.mean(unit * shifted, axis=-1, keepdims=True))


def per_device(tp, dp, *arrays):
    (
        layer_input,
        pair_lengths,
        query_weight,
        query_bias,
        key_weight,
        value_weight,
        value_bias,
        out_weight,
        out_bias,
        first_gain,
        first_shift,
        up_weight,
        up_bias,
        down_weight,
        down_bias,
        second_gain,
        second_shift,
        out_grad,
        query_tangent,
        key_tangent,
        value_tangent,
        out_tangent,
        up_tangent,
        down_tangent,
    ) = arrays
    rows, width = layer_input.shape
    pairs = rows // SEQ
    cols = query_weight.shape[1]
    hidden = up_weight.shape[1]
    heads = cols // HEAD
    scale = HEAD ** (-0.5)
    me = lax.axis_index("tp")
    own_rows = rows // tp

    attn = gather_rows(
        jnp.concatenate(
            [query_weight, key_weight, value_weight, query_tangent, key_tangent, value_tangent], 1
        ),
        dp,
    )
    outs = gather_rows(jnp.concatenate([out_weight.T, out_tangent.T], 1), dp)
    ups = gather_rows(jnp.concatenate([up_weight, up_tangent], 1), dp)
    downs = gather_rows(jnp.concatenate([down_weight.T, down_tangent.T], 1), dp)
    out_full, tout_full = outs[:, :cols], outs[:, cols:]
    up_full, tup_full = ups[:, :hidden], ups[:, hidden:]
    down_full, tdown_full = downs[:, :hidden], downs[:, hidden:]

    rows_own = lax.dynamic_slice_in_dim(layer_input, me * own_rows, own_rows, 0).astype(F32)
    upstream = lax.dynamic_slice_in_dim(out_grad, me * own_rows, own_rows, 0).astype(F32)

    zeros = jnp.zeros((cols,), F32)
    shift_all = jnp.concatenate([query_bias, zeros, value_bias, zeros, zeros, zeros])
    mixed = (dot(layer_input, attn, NN) + shift_all).astype(BF)
    mixed = mixed.reshape(pairs, SEQ, 6, heads, HEAD)
    query, key, value, tquery, tkey, tvalue = [mixed[:, :, i] for i in range(6)]
    valid = (
        lax.broadcasted_iota(jnp.int32, (pairs, 1, 1, SEQ), 3) < pair_lengths[:, None, None, None]
    )

    def ein(text, left, right):
        return jnp.einsum(text, left, right, preferred_element_type=F32)

    scores = jnp.where(valid, ein("pqhd,pkhd->phqk", query, key) * scale, jnp.float32(-1e30))
    expo = jnp.exp(scores - jnp.max(scores, axis=-1, keepdims=True))
    probs = expo / jnp.sum(expo, axis=-1, keepdims=True)
    probs_low = probs.astype(BF)
    context = ein("phqk,pkhd->pqhd", probs_low, value).reshape(rows, cols).astype(BF)
    tscores = ein("pqhd,pkhd->phqk", tquery, key) + ein("pqhd,pkhd->phqk", query, tkey)
    tscores = jnp.where(valid, tscores * scale, jnp.float32(0.0))
    tprobs = probs * (tscores - jnp.sum(tscores * probs, axis=-1, keepdims=True))
    tcontext = ein("phqk,pkhd->pqhd", tprobs.astype(BF), value)
    tcontext = tcontext + ein("phqk,pkhd->pqhd", probs_low, tvalue)
    tcontext = tcontext.reshape(rows, cols).astype(BF)
    part = dot(context, out_full, NT).astype(BF)
    tpart = (dot(tcontext, out_full, NT) + dot(context, tout_full, NT)).astype(BF)
    attended, tattended = scatter_sum(jnp.stack([part, tpart]), tp)

    unit_one, inverse_one = norm_parts(rows_own + attended + out_bias)
    first = unit_one * first_gain + first_shift
    tfirst = norm_along(unit_one, inverse_one, tattended) * first_gain
    first_low = lax.all_gather(first.astype(BF), "tp", axis=0, tiled=True)
    tfirst_low = lax.all_gather(tfirst.astype(BF), "tp", axis=0, tiled=True)

    upper = dot(first_low, up_full, NN) + up_bias
    tupper = dot(tfirst_low, up_full, NN) + dot(first_low, tup_full, NN)
    half = 0.5 * (1.0 + lax.erf(upper * (2.0 ** -0.5)))
    active = (upper * half).astype(BF)
    slope = half + upper * (jnp.exp(-0.5 * upper * upper) * ((2.0 * jnp.pi) ** -0.5))
    tactive = (slope * tupper).astype(BF)
    part = dot(active, down_full, NT).astype(BF)
    tpart = (dot(tactive, down_full, NT) + dot(active, tdown_full, NT)).astype(BF)
    lowered, tlowered = scatter_sum(jnp.stack([part, tpart]), tp)

    unit_two, inverse_two = norm_parts(first + lowered + down_bias)
    result = (unit_two * second_gain + second_shift).astype(BF)
    tresult = (norm_along(unit_two, inverse_two, tfirst + tlowered) * second_gain).astype(BF)
    gain_two = jnp.sum(upstream * unit_two, axis=0)
    shift_two = jnp.sum(upstream, axis=0)
    grad_two = norm_along(unit_two, inverse_two, upstream * second_gain)
    bias_two = jnp.sum(grad_two, axis=0)
    grad_down = lax.all_gather(grad_two.astype(BF), "tp", axis=0, tiled=True)

    grad_active = dot(grad_down, down_full, NN)
    grad_upper = grad_active * slope
    bias_up = jnp.sum(grad_upper, axis=0)
    grad_upper_low = grad_upper.astype(BF)
    step_down = dot(grad_down, active, TN).astype(BF)
    step_up = dot(first_low, grad_upper_low, TN).astype(BF)
    part = dot(grad_upper_low, up_full, NT).astype(BF)
    (grad_first,) = scatter_sum(part[None], tp)
    grad_first = grad_first + grad_two

    gain_one = jnp.sum(grad_first * unit_one, axis=0)
    shift_one = jnp.sum(grad_first, axis=0)
    grad_one = norm_along(unit_one, inverse_one, grad_first * first_gain)
    bias_out = jnp.sum(grad_one, axis=0)
    grad_attn = lax.all_gather(grad_one.astype(BF), "tp", axis=0, tiled=True)

    step_out = dot(grad_attn, context, TN).astype(BF)
    grad_context = dot(grad_attn, out_full, NN).astype(BF).reshape(pairs, SEQ, heads, HEAD)
    grad_values = ein("phqk,pqhd->pkhd", probs_low, grad_context).astype(BF)
    grad_probs = ein("pqhd,pkhd->phqk", grad_context, value)
    grad_scores = probs * (grad_probs - jnp.sum(grad_probs * probs, axis=-1, keepdims=True))
    grad_scores = grad_scores.astype(BF)
    grad_queries = (ein("phqk,pkhd->pqhd", grad_scores, key) * scale).astype(BF)
    grad_keys = (ein("phqk,pqhd->pkhd", grad_scores, query) * scale).astype(BF)
    grad_mixed = jnp.concatenate(
        [g.reshape(rows, cols) for g in (grad_queries, grad_keys, grad_values)], 1
    )
    step_mixed = dot(layer_input, grad_mixed, TN).astype(BF)
    bias_mixed = jnp.sum(grad_mixed.astype(F32), axis=0)
    part = dot(grad_mixed, attn[:, : 3 * cols], NT).astype(BF)
    (grad_input,) = scatter_sum(part[None], tp)
    grad_input = (grad_input + grad_one).astype(BF)

    def spread(step):
        split = step.reshape(dp, step.shape[0] // dp, step.shape[1])
        came = lax.all_to_all(split, "dp", 0, 0, tiled=True)
        return jnp.sum(came.astype(F32), axis=0)

    own_down = spread(step_down).T
    own_up = spread(step_up)
    own_out = spread(step_out).T
    own_mixed = spread(step_mixed)
    small = jnp.concatenate(
        [bias_out, gain_one, shift_one, bias_two, gain_two, shift_two, bias_up, bias_mixed]
    )
    pad = -small.shape[0] % 128
    small = jnp.concatenate([small, jnp.zeros((pad,), F32)]).reshape(1, -1, 128)
    small = lax.all_to_all(jnp.broadcast_to(small, (dp,) + small.shape[1:]), "dp", 0, 0, tiled=True)
    small = jnp.sum(small, axis=0)
    shared = 6 * width // 128
    common = lax.all_gather(small[:shared], "tp", axis=0, tiled=False)
    common = jnp.sum(common, axis=0).reshape(6, width)
    small = small[shared:].reshape(-1)

    def all_rows(block):
        return lax.all_gather(block, "tp", axis=0, tiled=True)

    return (
        all_rows(result),
        all_rows(grad_input),
        all_rows(tresult),
        own_mixed[:, :cols],
        small[hidden : hidden + cols],
        own_mixed[:, cols : 2 * cols],
        own_mixed[:, 2 * cols :],
        small[hidden + 2 * cols : hidden + 3 * cols],
        own_out,
        common[0],
        common[1],
        common[2],
        own_up,
        small[:hidden],
        own_down,
        common[3],
        common[4],
        common[5],
    )


def solution(mesh):
    wide, tall, col, row, full = P("dp", "tp"), P("tp", "dp"), P("tp"), P("dp", None), P()
    placed = (
        (row, P("dp"), wide, col, wide, wide, col, tall, full, full, full, wide, col, tall)
        + (full, full, full, row, wide, wide, wide, tall, wide, tall)
    )
    results = (row, row, row, wide, col, wide, wide, col, tall, full, full, full)
    results = results + (wide, col, tall, full, full, full)
    tp, dp = mesh.shape["tp"], mesh.shape["dp"]

    def body(*arrays):
        return per_device(tp, dp, *arrays)

    return jax.shard_map(
        body, mesh=mesh, in_specs=placed, out_specs=results, check_vma=False
    )
```

```python
import functools
import math

import jax
import jax.numpy as jnp
from jax import lax
from jax.experimental import pallas as pl
from jax.experimental.pallas import tpu as pltpu
from jax.sharding import PartitionSpec as P

HEAD = 64
SEQ = 256
EPSILON = 1e-06
SCALE = HEAD ** (-0.5)
BLOCKS = (0, 2, 1, 3)
OWNERS = (0, 2, 4, 6, 1, 3, 5, 7)
SNAKE = (0, 2, 4, 6, 7, 5, 3, 1)
EXTRA = 8
BF = jnp.bfloat16
F32 = jnp.float32
VMEM_LIMIT = 16 * 1024 * 1024
TILE = 256

NN = ((1,), (0,))
NT = ((1,), (1,))
TN = ((0,), (0,))


def dot(left, right, dims):
    return lax.dot_general(left, right, (dims, ((), ())), preferred_element_type=F32)


def xor_pairs(size, bit):
    return [(i, i ^ bit) for i in range(size)]


def call(body, name, outs, near, shards=(), scratch=(), any_outs=False):
    smem = [a.dtype == jnp.int32 for a in near]
    specs = [pl.BlockSpec(memory_space=pltpu.SMEM if s else pltpu.VMEM) for s in smem]
    specs = specs + [pl.BlockSpec(memory_space=pl.ANY)] * len(shards)
    out_space = pltpu.HBM if any_outs else pltpu.VMEM
    return pl.pallas_call(
        body,
        out_shape=[jax.ShapeDtypeStruct(shape, kind) for shape, kind in outs],
        in_specs=specs,
        out_specs=[pl.BlockSpec(memory_space=out_space)] * len(outs),
        scratch_shapes=list(scratch),
        name=name,
        compiler_params=pltpu.CompilerParams(vmem_limit_bytes=VMEM_LIMIT),
        cost_estimate=pl.CostEstimate(flops=1, bytes_accessed=1, transcendentals=0),
    )(*near, *shards)


def tiles(width, body):
    step = TILE if width % TILE == 0 else width

    def one(i, carry):
        body(pl.ds(pl.multiple_of(i * step, step), step))
        return carry

    lax.fori_loop(0, width // step, one, 0)


def after(value, *others):
    return lax.optimization_barrier((value, *others))[0]


class Ring:
    def __init__(self, shard, dp):
        self.near = dp == len(SNAKE)
        self.dp = dp
        self.front = [shard, shard]
        self.parts = [shard]
        self.steps = 0

    def step(self):
        if not self.near:
            if self.steps == 0:
                self.parts = [lax.all_gather(self.parts[0], "dp", axis=0, tiled=True)]
                self.front = [self.parts[0]] * 2
            self.steps += 1
            return
        if self.steps == self.dp // 2:
            return
        ahead = [(SNAKE[i], SNAKE[(i + 1) % self.dp]) for i in range(self.dp)]
        behind = [(b, a) for a, b in ahead]
        self.steps += 1
        self.front[0] = lax.ppermute(self.front[0], "dp", ahead)
        self.parts.append(self.front[0])
        if self.steps < self.dp // 2:
            self.front[1] = lax.ppermute(self.front[1], "dp", behind)
            self.parts.append(self.front[1])


def join(rings, *values):
    fronts = [front for ring in rings for front in ring.front]
    joined = lax.optimization_barrier((*values, *fronts))
    for i, ring in enumerate(rings):
        ring.front = list(joined[len(values) + 2 * i :][:2])
    return joined[0] if len(values) == 1 else joined[: len(values)]


def ring_owner(me, index):
    size = len(SNAKE)
    place = jnp.where(me % 2 == 0, me // 2, size - 1 - me // 2)
    step = (index + 1) // 2
    place = lax.rem(place + (size - step if index % 2 else step), size)
    return jnp.where(place < size // 2, 2 * place, 2 * (size - 1 - place) + 1)


def shard_copies(where, refs, whole, sems):
    rows = whole.shape[0] // len(refs)
    made = []
    for i, ref in enumerate(refs):
        owner = ring_owner(where[1], i) if len(refs) > 1 else 0
        start = pl.multiple_of(owner * rows, rows)
        made.append(pltpu.make_async_copy(ref, whole.at[pl.ds(start, rows), :], sems.at[i]))
    return made


def start_all(copies):
    for copy in copies:
        copy.start()


def wait_all(copies):
    for copy in copies:
        copy.wait()


def swap(block, tp, bit):
    return lax.ppermute(block, "tp", xor_pairs(tp, bit))


def sum_exchange(keep, send, tp, rings=(), meanwhile=()):
    quarter = keep.shape[0] // 2
    first = swap(send, tp, 1)
    if rings or meanwhile:
        first = join(rings, first, *meanwhile)
        first = first[0] if meanwhile else first
    for ring in rings:
        ring.step()
    onward = (keep[quarter:].astype(F32) + first[quarter:].astype(F32)).astype(BF)
    second = swap(onward, tp, 2)
    if rings:
        second = join(rings, second)
    for ring in rings:
        ring.step()
    return keep, first, second


def spread_rows(own, tp, rings=()):
    across, beside = swap(own, tp, 2), swap(own, tp, 1)
    if rings:
        across = join(rings, across)
    for ring in rings:
        ring.step()
    return own, across, beside, swap(across, tp, 1)


def summed(keep, first, second):
    quarter = second.shape[0]
    near = keep[0:quarter, :].astype(F32) + first[0:quarter, :].astype(F32)
    return near + second[...].astype(F32)


def halves(array, keep, send, cols=slice(None)):
    half = array.shape[0] // 2
    keep[:, cols] = array[:half].astype(BF)
    send[:, cols] = array[half:].astype(BF)


def mean_last(value):
    return jnp.mean(value, axis=-1, keepdims=True)


def norm_along(unit, inverse, along):
    shifted = along - mean_last(along)
    return inverse * (shifted - unit * mean_last(unit * shifted))


def sum_rows(value):
    return jnp.sum(value, axis=0, keepdims=True)


def split_sums(lines):
    width = lines[0].shape[-1]
    missing = EXTRA // 2 - sum(line.shape[0] for line in lines)
    blank = [jnp.zeros((missing, width), F32)] if missing else []
    whole = jnp.concatenate([*lines, *blank]) if len(lines) + missing > 1 else lines[0]
    rounded = whole.astype(BF).astype(F32)
    return jnp.concatenate([rounded, whole - rounded]).astype(BF)


def tree_sum(four):
    return (four[0] + four[1]) + (four[2] + four[3])


def joined_sums(block):
    return block[: EXTRA // 2].astype(F32) + block[EXTRA // 2 :].astype(F32)


def pair_rows(array, pair, quarter, cols):
    near, far = pair * quarter, (pair + 2) * quarter
    return jnp.concatenate([array[near : near + quarter, cols], array[far : far + quarter, cols]])


def put_pair(ref, pair, quarter, cols, value):
    near, far = pair * quarter, (pair + 2) * quarter
    ref[near : near + quarter, cols] = value[:quarter]
    ref[far : far + quarter, cols] = value[quarter:]


def positions(me, quarter):
    local = lax.broadcasted_iota(jnp.int32, (1, SEQ), 1)
    half = jnp.where(local < quarter, me % 2, 1 - me % 2)
    return half * quarter + lax.rem(local, quarter)


def attention_forward(count, cols, where, x_ref, params, *refs):
    shards, refs = refs[:count], refs[count:]
    rel, mixed, probs, context, keep, send, whole, sems = refs
    copies = shard_copies(where, shards, whole, sems)
    start_all(copies)
    me = where[0]
    quarter = x_ref.shape[0] // 4
    for i, block in enumerate(BLOCKS):
        start = pl.multiple_of((me ^ block) * quarter, quarter)
        rel[i * quarter : (i + 1) * quarter, :] = x_ref[pl.ds(start, quarter), :]
    wait_all(copies)
    for third in range(3):
        part = slice(third * cols, (third + 1) * cols)
        mixed[:, part] = (dot(rel[...], whole[:, part], NN) + params[0:1, part]).astype(BF)
    slots = positions(me, quarter)
    heads = cols // HEAD
    for pair in range(2):
        valid = slots < where[2 + ((me // 2) ^ pair)]
        for head in range(heads):
            query, key, value = [
                pair_rows(mixed, pair, quarter, slice(at, at + HEAD))
                for at in range(head * HEAD, 3 * cols, cols)
            ]
            scores = jnp.where(valid, dot(query, key, NT) * SCALE, jnp.float32(-1e30))
            expo = jnp.exp(scores - jnp.max(scores, axis=-1, keepdims=True))
            prob = expo / jnp.sum(expo, axis=-1, keepdims=True)
            probs[pair * heads + head] = prob
            result = dot(prob.astype(BF), value, NN).astype(BF)
            put_pair(context, pair, quarter, slice(head * HEAD, (head + 1) * HEAD), result)

    def project(cut):
        halves(dot(context[...], whole[cut, 3 * cols : 4 * cols], NT), keep, send, cut)

    tiles(keep.shape[1], project)


def attention_tangent(
    count, cols, where, rel, mixed, probs, context, whole, *refs
):
    tshards, refs = refs[:count], refs[count:]
    keep, send, twhole, sems, tmixed, tcontext = refs
    copies = shard_copies(where, tshards, twhole, sems)
    start_all(copies)
    wait_all(copies)
    me = where[0]
    quarter = rel.shape[0] // 4
    for third in range(3):
        part = slice(third * cols, (third + 1) * cols)
        tmixed[:, part] = dot(rel[...], twhole[:, part], NN).astype(BF)
    slots = positions(me, quarter)
    heads = cols // HEAD
    for pair in range(2):
        valid = slots < where[2 + ((me // 2) ^ pair)]
        for head in range(heads):
            columns = [slice(at, at + HEAD) for at in range(head * HEAD, 3 * cols, cols)]
            query, key, value = [pair_rows(mixed, pair, quarter, at) for at in columns]
            tquery, tkey, tvalue = [pair_rows(tmixed, pair, quarter, at) for at in columns]
            prob = probs[pair * heads + head]
            tscores = (dot(tquery, key, NT) + dot(query, tkey, NT)) * SCALE
            tscores = jnp.where(valid, tscores, jnp.float32(0.0))
            total = jnp.sum(tscores * prob, axis=-1, keepdims=True)
            tprob = (prob * (tscores - total)).astype(BF)
            result = dot(tprob, value, NN) + dot(prob.astype(BF), tvalue, NN)
            put_pair(
                tcontext, pair, quarter, slice(head * HEAD, (head + 1) * HEAD), result.astype(BF)
            )

    def project(cut):
        part = dot(tcontext[...], whole[cut, 3 * cols : 4 * cols], NT)
        part = part + dot(context[...], twhole[cut, 3 * cols : 4 * cols], NT)
        halves(part, keep, send, cut)

    tiles(keep.shape[1], project)


def first_norm(x_rel, keep, came, second, params, first, unit, inverse, low):
    own = second.shape[0]
    resid = x_rel[0:own, :].astype(F32) + summed(keep, came, second) + params[1:2, :]
    center = resid - mean_last(resid)
    inv = lax.rsqrt(mean_last(center * center) + EPSILON)
    whitened = center * inv
    unit[...] = whitened
    inverse[...] = jnp.broadcast_to(inv, inverse.shape)
    value = whitened * params[2:3, :] + params[3:4, :]
    first[...] = value
    low[...] = value.astype(BF)


def first_norm_tangent(keep, came, second, params, unit, inverse, tfirst, low):
    along = norm_along(unit[...], inverse[:, 0:1], summed(keep, came, second)) * params[2:3, :]
    tfirst[...] = along
    low[...] = along.astype(BF)


def collect(pieces, rel):
    quarter = rel.shape[0] // 4
    for i, piece in enumerate(pieces):
        rel[i * quarter : (i + 1) * quarter, :] = piece[0:quarter, :]


def feed_forward(count, hidden, where, params, *refs):
    pieces, refs = refs[:4], refs[4:]
    shards, refs = refs[:count], refs[count:]
    rel, active, slope, keep, send, whole, sems = refs
    copies = shard_copies(where, shards, whole, sems)
    start_all(copies)
    collect(pieces, rel)
    wait_all(copies)

    def up(cut):
        upper = dot(rel[...], whole[:, cut], NN) + params[4:5, cut]
        half = 0.5 + 0.5 * lax.erf(upper * (2.0 ** -0.5))
        active[:, cut] = (upper * half).astype(BF)
        bell = jnp.exp(-0.5 * upper * upper) * 0.3989422804014327
        slope[:, cut] = half + upper * bell

    tiles(hidden, up)

    def down(cut):
        halves(dot(active[...], whole[cut, hidden:], NT), keep, send, cut)

    tiles(keep.shape[1], down)


def feed_forward_tangent(count, hidden, where, *refs):
    pieces, (rel, active, slope, whole), refs = refs[:4], refs[4:8], refs[8:]
    tshards, refs = refs[:count], refs[count:]
    keep, send, twhole, sems, trel, tactive = refs
    copies = shard_copies(where, tshards, twhole, sems)
    start_all(copies)
    collect(pieces, trel)
    wait_all(copies)

    def up(cut):
        tupper = dot(trel[...], whole[:, cut], NN) + dot(rel[...], twhole[:, cut], NN)
        tactive[:, cut] = (slope[:, cut] * tupper).astype(BF)

    tiles(hidden, up)

    def down(cut):
        part = dot(tactive[...], whole[cut, hidden:], NT)
        part = part + dot(active[...], twhole[cut, hidden:], NT)
        halves(part, keep, send, cut)

    tiles(keep.shape[1], down)


def second_norm(
    where, keep, came, second, params, first, upstream,
    result, grad, low, unit, inverse,
):
    resid = first[...] + summed(keep, came, second) + params[5:6, :]
    center = resid - mean_last(resid)
    inv = lax.rsqrt(mean_last(center * center) + EPSILON)
    whitened = center * inv
    own = second.shape[0]
    unit[...] = whitened
    inverse[...] = jnp.broadcast_to(inv, inverse.shape)
    result[...] = (whitened * params[6:7, :] + params[7:8, :]).astype(BF)
    back = upstream[pl.ds(pl.multiple_of(where[0] * own, own), own), :].astype(F32)
    value = norm_along(whitened, inv, back * params[6:7, :])
    grad[...] = value
    low[0:own, :] = value.astype(BF)
    low[own:, :] = split_sums([sum_rows(value), sum_rows(back * whitened), sum_rows(back)])


def second_norm_tangent(keep, came, second, params, tfirst, unit, inverse, result):
    along = tfirst[...] + summed(keep, came, second)
    result[...] = (norm_along(unit[...], inverse[:, 0:1], along) * params[6:7, :]).astype(BF)


def first_norm_backward(
    keep, came, second, params, grad_two, unit, inverse, grad, low
):
    back = grad_two[...] + summed(keep, came, second)
    value = norm_along(unit[...], inverse[:, 0:1], back * params[2:3, :])
    own = second.shape[0]
    grad[...] = value
    low[0:own, :] = value.astype(BF)
    low[own:, :] = split_sums([sum_rows(value), sum_rows(back * unit[...]), sum_rows(back)])


def piece_sums(pieces):
    own = pieces[0].shape[0] - EXTRA
    return tree_sum([joined_sums(piece[own:, :]) for piece in pieces])


def feed_forward_backward(hidden, *refs):
    pieces, (slope, whole) = refs[:4], refs[4:6]
    rel, grad_upper, sums, keep, send = refs[6:]
    collect(pieces, rel)
    sums[...] = piece_sums(pieces)

    def down(cut):
        there = pl.ds(pl.multiple_of(cut.start + hidden, cut.size), cut.size)
        value = dot(rel[...], whole[:, there], NN) * slope[:, cut]
        sums[3:4, cut] = sum_rows(value)
        grad_upper[:, cut] = value.astype(BF)

    tiles(hidden, down)

    def up(cut):
        halves(dot(grad_upper[...], whole[cut, :hidden], NT), keep, send, cut)

    tiles(keep.shape[1], up)


def put_owned(where, step, targets, sums=None):
    if len(targets) == 1:
        targets[0][...] = step[...]
        return
    rows = step.shape[0] // len(OWNERS)
    extra = None if sums is None else split_sums([sums])
    for i, owner in enumerate(OWNERS):
        start = pl.multiple_of((where[1] ^ owner) * rows, rows)
        target = targets[i // 4]
        target[i % 4, 0:rows, :] = step[pl.ds(start, rows), :]
        if extra is not None:
            target[i % 4, rows:, :] = extra


def weight_gradient(summing, where, *refs):
    if summing:
        left, sums, right = refs[:3]
        refs = refs[3:]
    else:
        (right, left), refs, sums = refs[:2], refs[2:], None
    targets, step = refs[:-1], refs[-1]

    def one(cut):
        step[cut, :] = dot(left[:, cut], right[...], TN).astype(BF)

    tiles(left.shape[1], one)
    put_owned(where, step, targets, None if sums is None else sums[...])


def attention_backward(cols, *refs):
    pieces, (mixed, probs, whole) = refs[:4], refs[4:7]
    rel, grad, sums, keep, send, back = refs[7:]
    collect(pieces, rel)
    sums[...] = piece_sums(pieces)
    quarter = rel.shape[0] // 4
    back[...] = dot(rel[...], whole[:, 3 * cols : 4 * cols], NN).astype(BF)
    heads = cols // HEAD
    for pair in range(2):
        for head in range(heads):
            columns = [slice(at, at + HEAD) for at in range(head * HEAD, 3 * cols, cols)]
            query, key, value = [pair_rows(mixed, pair, quarter, at) for at in columns]
            prob = probs[pair * heads + head]
            grad_context = pair_rows(back, pair, quarter, columns[0])
            grad_value = dot(prob.astype(BF), grad_context, TN)
            grad_prob = dot(grad_context, value, NT)
            total = jnp.sum(grad_prob * prob, axis=-1, keepdims=True)
            grad_score = (prob * (grad_prob - total)).astype(BF)
            put_pair(grad, pair, quarter, columns[2], grad_value.astype(BF))
            grad_query = dot(grad_score, key, NN) * SCALE
            put_pair(grad, pair, quarter, columns[0], grad_query.astype(BF))
            grad_key = dot(grad_score, query, TN) * SCALE
            put_pair(grad, pair, quarter, columns[1], grad_key.astype(BF))

    def project(cut):
        halves(dot(grad[...], whole[cut, : 3 * cols], NT), keep, send, cut)

    tiles(keep.shape[1], project)


def attention_weights(paired, cols, where, rel, grad, sums, x_rel, context, *refs):
    targets, refs = (refs[:2], refs[2:]) if paired else (refs[:1], refs[1:])
    (step,) = refs[-1:]

    def one(cut):
        step[cut, : 3 * cols] = dot(x_rel[:, cut], grad[...], TN).astype(BF)
        step[cut, 3 * cols :] = dot(rel[:, cut], context[...], TN).astype(BF)

    tiles(x_rel.shape[1], one)
    mixed = sum_rows(grad[...].astype(F32))
    mixed = jnp.concatenate([mixed, jnp.zeros((1, cols), F32)], axis=1)
    lines = jnp.concatenate([sums[0:3, :], mixed])
    put_owned(where, step, targets, lines)
    if not paired:
        refs[0][...] = lines


def fold_shards(keep, came, *outs):
    rows = outs[0].shape[0]
    for i in range(4):
        total = keep[i, 0:rows, :].astype(F32) + came[i, 0:rows, :].astype(F32)
        if i == 0:
            outs[0][...] = total
        else:
            outs[i][0:rows, :] = total.astype(BF)
    if len(outs) > 4:
        sums = joined_sums(keep[0, rows:, :]) + joined_sums(came[0, rows:, :])
        rounded = split_sums([sums])
        outs[4][...] = joined_sums(rounded)
        for i in range(1, 4):
            outs[i][rows:, :] = rounded


def last_total(refs):
    rows = refs[0].shape[0]
    total = refs[0][...]
    for ref in refs[1:4]:
        total = total + ref[0:rows, :].astype(F32)
    return total


def last_sums(refs, outs):
    rows = refs[0].shape[0]
    sums = tree_sum([refs[4][...]] + [joined_sums(ref[rows:, :]) for ref in refs[1:4]])
    for i, out in enumerate(outs):
        out[...] = sums[i]


def finish_up(*refs):
    refs[4][...] = last_total(refs)


def finish_down(*refs):
    refs[5][...] = last_total(refs)
    last_sums(refs, refs[6:])


def finish_attention(cols, *refs):
    total = last_total(refs)
    for i in range(3):
        refs[5 + i][...] = total[:, i * cols : (i + 1) * cols]
    refs[8][...] = total[:, 3 * cols :].T
    last_sums(refs, refs[9:])


def last_sum(keep, came, second, grad_one, out):
    out[...] = (grad_one[...] + summed(keep, came, second)).astype(BF)


def place_rows(count, where, *refs):
    pieces, outs, sems = refs[: 4 * count], refs[4 * count : 5 * count], refs[5 * count]
    own = pieces[0].shape[0]
    copies = []
    for i, out in enumerate(outs):
        for j, block in enumerate(BLOCKS):
            start = pl.multiple_of((where[0] ^ block) * own, own)
            copies.append(
                pltpu.make_async_copy(
                    pieces[4 * i + j], out.at[pl.ds(start, own), :], sems.at[4 * i + j]
                )
            )
    start_all(copies)
    wait_all(copies)


def per_device(tp, dp, *arrays):
    (
        layer_input,
        pair_lengths,
        query_weight,
        query_bias,
        key_weight,
        value_weight,
        value_bias,
        out_weight,
        out_bias,
        first_gain,
        first_shift,
        up_weight,
        up_bias,
        down_weight,
        down_bias,
        second_gain,
        second_shift,
        out_grad,
        query_tangent,
        key_tangent,
        value_tangent,
        out_tangent,
        up_tangent,
        down_tangent,
    ) = arrays
    rows, width = layer_input.shape
    cols = query_weight.shape[1]
    hidden = up_weight.shape[1]
    heads = cols // HEAD
    own = rows // tp
    half = rows // 2
    shard = width // dp
    paired = dp == len(SNAKE)

    place = jnp.stack([lax.axis_index("tp"), lax.axis_index("dp")]).astype(jnp.int32)
    where = jnp.concatenate([place, pair_lengths])
    zeros = jnp.zeros((cols,), F32)
    params = jnp.concatenate(
        [query_bias, zeros, value_bias, zeros, out_bias, first_gain, first_shift]
        + [up_bias, down_bias, second_gain, second_shift]
    ).reshape(8, width)
    parts = [((half, width), BF), ((half, width), BF)]
    piece = ((own + EXTRA, width), BF)
    lines = ((EXTRA // 2, width), F32)
    full_own = ((own, width), F32)
    attn_rows = ((width, 4 * cols), BF)
    ff_rows = ((width, 2 * hidden), BF)

    def pack(first_one, *blocks):
        return jnp.concatenate([first_one, *blocks], 1)

    def arriving(count):
        return pltpu.SemaphoreType.DMA((count,))

    where, out_rows, tout_rows, params = join((), where, out_weight.T, out_tangent.T, params)
    attn = Ring(pack(query_weight, key_weight, value_weight, out_rows), dp)
    attn.step()
    early = attn.parts[-1]
    ff = Ring(pack(after(up_weight, early), down_weight.T), dp)
    tattn = Ring(pack(after(query_tangent, early), key_tangent, value_tangent, tout_rows), dp)
    tff = Ring(pack(after(up_tangent, early), down_tangent.T), dp)
    attn.step()
    join([attn, ff])
    attn.step()
    ff.step()
    attn.step()
    where = join([ff], where)
    ff.step()
    count = len(attn.parts)
    x_rel, mixed, probs, context, keep, send, attn_whole = call(
        functools.partial(attention_forward, count, cols),
        "attention_forward",
        [
            ((rows, width), BF),
            ((rows, 3 * cols), BF),
            ((2 * heads, SEQ, SEQ), F32),
            ((rows, cols), BF),
            *parts,
            attn_rows,
        ],
        (where, layer_input, params),
        attn.parts,
        [arriving(count)],
    )
    first, unit_one, inverse_one, first_low = call(
        first_norm,
        "first_norm",
        [full_own, full_own, ((own, 128), F32), ((own, width), BF)],
        (x_rel, *sum_exchange(keep, send, tp, [ff]), params),
    )
    pieces = spread_rows(first_low, tp, [ff])
    tattn.front = [after(tattn.front[0], pieces[1])] * 2
    tattn.step()
    first_rel, active, slope, keep, send, ff_whole = call(
        functools.partial(feed_forward, count, hidden),
        "feed_forward",
        [((rows, width), BF), ((rows, hidden), BF), ((rows, hidden), F32), *parts, ff_rows],
        (where, params, *pieces),
        ff.parts,
        [arriving(count)],
    )
    result, grad_two, grad_two_low, unit_two, inverse_two = call(
        second_norm,
        "second_norm",
        [((own, width), BF), full_own, piece, full_own, ((own, 128), F32)],
        (where, *sum_exchange(keep, send, tp, [tattn]), params, first, out_grad),
    )
    pieces = spread_rows(grad_two_low, tp, [tattn])
    tff.front = [after(tff.front[0], pieces[1])] * 2
    tff.step()
    grad_down, grad_upper, sums_up, keep, send = call(
        functools.partial(feed_forward_backward, hidden),
        "feed_forward_backward",
        [((rows, width), BF), ((rows, hidden), BF), lines, *parts],
        (*pieces, slope, ff_whole),
    )

    def weight_outs(total, sums):
        if paired:
            return [((4, shard + (EXTRA if sums else 0), total), BF)] * 2
        return [((width, total), BF)]

    def step_of(name, near, summing):
        return call(
            functools.partial(weight_gradient, summing),
            name,
            weight_outs(hidden, summing),
            (where, *near),
            (),
            [pltpu.VMEM((width, hidden), BF)],
        )

    def swap_shards(steps):
        return lax.ppermute(steps[1], "dp", xor_pairs(dp, 1)) if paired else steps[0]

    down_steps = step_of("down_weights", (grad_down, sums_up, active), True)
    up_steps = step_of("up_weights", (grad_upper, first_rel), False)
    down_came = swap_shards(down_steps)
    exchanged = sum_exchange(keep, send, tp, [tff], (down_steps[0],))
    grad_one, grad_one_low = call(
        first_norm_backward,
        "first_norm_backward",
        [full_own, piece],
        (*exchanged, after(params, up_steps[0]), grad_two, unit_one, inverse_one),
    )
    up_came = swap_shards(up_steps)
    pieces = spread_rows(grad_one_low, tp, [tff])
    tkeep, tsend = call(
        functools.partial(attention_tangent, count, cols),
        "attention_tangent",
        parts,
        (after(where, grad_one_low), x_rel, mixed, probs, context, attn_whole),
        tattn.parts,
        [pltpu.VMEM(*attn_rows), arriving(count)]
        + [pltpu.VMEM((rows, 3 * cols), BF), pltpu.VMEM((rows, cols), BF)],
    )
    grad_attn, grad_mixed, sums_one, keep, send = call(
        functools.partial(attention_backward, cols),
        "attention_backward",
        [((rows, width), BF), ((rows, 3 * cols), BF), lines, *parts],
        (*pieces[:3], after(pieces[3], down_came, tkeep), mixed, probs, attn_whole),
        (),
        [pltpu.VMEM((rows, cols), BF)],
    )
    last_steps = call(
        functools.partial(attention_weights, paired, cols),
        "attention_weights",
        weight_outs(4 * cols, True) + ([] if paired else [lines]),
        (where, grad_attn, grad_mixed, sums_one, x_rel, context),
        (),
        [pltpu.VMEM(*attn_rows)],
    )
    last_came = swap_shards(last_steps)
    exchanged = sum_exchange(keep, send, tp, (), (last_steps[0],))
    (grad_input,) = call(
        last_sum, "last_sum", [((own, width), BF)], (*exchanged, grad_one)
    )

    tfirst, tfirst_low = call(
        first_norm_tangent,
        "first_norm_tangent",
        [full_own, ((own, width), BF)],
        (*sum_exchange(tkeep, tsend, tp), params, unit_one, inverse_one),
    )
    tkeep, tsend = call(
        functools.partial(feed_forward_tangent, count, hidden),
        "feed_forward_tangent",
        parts,
        (
            after(where, last_steps[0]),
            *spread_rows(tfirst_low, tp),
            first_rel,
            active,
            slope,
            ff_whole,
        ),
        tff.parts,
        [pltpu.VMEM(*ff_rows), arriving(count)]
        + [pltpu.VMEM((rows, width), BF), pltpu.VMEM((rows, hidden), BF)],
    )
    (tresult,) = call(
        second_norm_tangent,
        "second_norm_tangent",
        [((own, width), BF)],
        (*sum_exchange(tkeep, tsend, tp), params, tfirst, unit_two, inverse_two),
    )

    def over_dp(kept, came, sums):
        total = kept.shape[2]
        going = ((kept.shape[1], total), BF)
        outs = [((shard, total), F32), going, going, going] + ([lines] if sums else [])
        own_shard, *onward = call(fold_shards, "fold_shards", outs, (kept, came))
        there = [lax.ppermute(onward[i], "dp", xor_pairs(dp, 2 * i + 2)) for i in range(3)]
        return (own_shard, *there, *onward[3:])

    vector = ((width,), F32)
    if paired:
        own_down, *sums_two = call(
            finish_down,
            "finish_down",
            [((shard, hidden), F32)] + [vector] * 4,
            over_dp(down_steps[0], down_came, True),
        )
        (own_up,) = call(
            finish_up, "finish_up", [((shard, hidden), F32)], over_dp(up_steps[0], up_came, False)
        )
        *own_mixed, own_out, bias_out, gain_one, shift_one, mixed_line = call(
            functools.partial(finish_attention, cols),
            "finish_attention",
            [((shard, cols), F32)] * 3 + [((cols, shard), F32)] + [vector] * 4,
            over_dp(last_steps[0], last_came, True),
        )
        sums_one = [bias_out, gain_one, shift_one, mixed_line]
    else:

        def all_summed(step):
            split = step.reshape(dp, shard, -1)
            came = lax.all_to_all(split, "dp", 0, 0, tiled=True)
            return jnp.sum(came.astype(F32), axis=0)

        own_down, own_up = all_summed(down_steps[0]), all_summed(up_steps[0])
        last = all_summed(last_steps[0])
        own_mixed = [last[:, i * cols : (i + 1) * cols] for i in range(3)]
        own_out = last[:, 3 * cols :].T
        sums_two = list(lax.psum(sums_up, "dp"))
        sums_one = list(lax.psum(last_steps[1], "dp"))

    def all_rows(*blocks):
        pieces = [piece for block in blocks for piece in spread_rows(block, tp)]
        return call(
            functools.partial(place_rows, len(blocks)),
            "place_rows",
            [((rows, width), BF)] * len(blocks),
            (where, *pieces),
            scratch=[arriving(4 * len(blocks))],
            any_outs=True,
        )

    whole_result, whole_tresult = all_rows(result, tresult)
    (whole_grad,) = all_rows(grad_input)
    mixed_sums = sums_one[3]
    return (
        whole_result,
        whole_grad,
        whole_tresult,
        own_mixed[0],
        mixed_sums[:cols],
        own_mixed[1],
        own_mixed[2],
        mixed_sums[2 * cols : 3 * cols],
        own_out,
        *sums_one[:3],
        own_up,
        sums_two[3],
        own_down.T,
        *sums_two[:3],
    )


def solution(mesh):
    wide, tall, col, row, full = P("dp", "tp"), P("tp", "dp"), P("tp"), P("dp", None), P()
    placed = (
        (row, P("dp"), wide, col, wide, wide, col, tall, full, full, full, wide, col, tall)
        + (full, full, full, row, wide, wide, wide, tall, wide, tall)
    )
    results = (row, row, row, wide, col, wide, wide, col, tall, full, full, full)
    results = results + (wide, col, tall, full, full, full)
    tp, dp = mesh.shape["tp"], mesh.shape["dp"]

    def body(*arrays):
        return per_device(tp, dp, *arrays)

    return jax.shard_map(
        body, mesh=mesh, in_specs=placed, out_specs=results, check_vma=False
    )
```

```python
import functools
import math

import jax
import jax.numpy as jnp
from jax import lax
from jax.experimental import pallas as pl
from jax.experimental.pallas import tpu as pltpu
from jax.sharding import PartitionSpec as P

HEAD = 64
SEQ = 256
EPSILON = 1e-06
SCALE = HEAD ** (-0.5)
BLOCKS = (0, 2, 1, 3)
FF_GROUPS = ((2,), (3,), (1,), (0,))
LAST_GROUPS = ((2, 3), (1, 0))
SNAKE = (0, 2, 4, 6, 7, 5, 3, 1)
EXTRA = 8
BF = jnp.bfloat16
F32 = jnp.float32
VMEM_LIMIT = 16 * 1024 * 1024
TILE = 256

NN = ((1,), (0,))
NT = ((1,), (1,))
TN = ((0,), (0,))


def dot(left, right, dims):
    return lax.dot_general(left, right, (dims, ((), ())), preferred_element_type=F32)


def xor_pairs(size, bit):
    return [(i, i ^ bit) for i in range(size)]


def call(body, name, outs, near, shards=(), scratch=(), any_outs=False):
    smem = [a.dtype == jnp.int32 for a in near]
    specs = [pl.BlockSpec(memory_space=pltpu.SMEM if s else pltpu.VMEM) for s in smem]
    specs = specs + [pl.BlockSpec(memory_space=pl.ANY)] * len(shards)
    out_space = pltpu.HBM if any_outs else pltpu.VMEM
    return list(pl.pallas_call(
        body,
        out_shape=[jax.ShapeDtypeStruct(shape, kind) for shape, kind in outs],
        in_specs=specs,
        out_specs=[pl.BlockSpec(memory_space=out_space)] * len(outs),
        scratch_shapes=list(scratch),
        name=name,
        compiler_params=pltpu.CompilerParams(vmem_limit_bytes=VMEM_LIMIT),
        cost_estimate=pl.CostEstimate(flops=1, bytes_accessed=1, transcendentals=0),
    )(*near, *shards))


def tiles(width, body):
    step = TILE if width % TILE == 0 else width

    def one(i, carry):
        body(pl.ds(pl.multiple_of(i * step, step), step))
        return carry

    lax.fori_loop(0, width // step, one, 0)


def after(value, *others):
    return lax.optimization_barrier((value, *others))[0]


class Ring:
    def __init__(self, shard, dp):
        self.near = dp == len(SNAKE)
        self.dp = dp
        self.front = [shard, shard]
        self.parts = [shard]
        self.steps = 0

    def step(self):
        if not self.near:
            if self.steps == 0:
                self.parts = [lax.all_gather(self.parts[0], "dp", axis=0, tiled=True)]
                self.front = [self.parts[0]] * 2
            self.steps += 1
            return
        if self.steps == self.dp // 2:
            return
        ahead = [(SNAKE[i], SNAKE[(i + 1) % self.dp]) for i in range(self.dp)]
        behind = [(b, a) for a, b in ahead]
        self.steps += 1
        self.front[0] = lax.ppermute(self.front[0], "dp", ahead)
        self.parts.append(self.front[0])
        if self.steps < self.dp // 2:
            self.front[1] = lax.ppermute(self.front[1], "dp", behind)
            self.parts.append(self.front[1])


def join(rings, *values):
    fronts = [front for ring in rings for front in ring.front]
    joined = lax.optimization_barrier((*values, *fronts))
    for i, ring in enumerate(rings):
        ring.front = list(joined[len(values) + 2 * i :][:2])
    return joined[0] if len(values) == 1 else joined[: len(values)]


def ring_owner(me, index):
    size = len(SNAKE)
    place = jnp.where(me % 2 == 0, me // 2, size - 1 - me // 2)
    step = (index + 1) // 2
    place = lax.rem(place + (size - step if index % 2 else step), size)
    return jnp.where(place < size // 2, 2 * place, 2 * (size - 1 - place) + 1)


def join_lists(*values):
    counts = [len(value) if isinstance(value, list) else 1 for value in values]
    flat = [v for value in values for v in (value if isinstance(value, list) else [value])]
    joined = list(lax.optimization_barrier(tuple(flat)))
    results = []
    for value, count in zip(values, counts):
        taken, joined = joined[:count], joined[count:]
        results.append(taken if isinstance(value, list) else taken[0])
    return results


def shard_copies(where, refs, whole, sems):
    rows = whole.shape[0] // len(refs)
    made = []
    for i, ref in enumerate(refs):
        owner = ring_owner(where[1], i) if len(refs) > 1 else 0
        start = pl.multiple_of(owner * rows, rows)
        made.append(pltpu.make_async_copy(ref, whole.at[pl.ds(start, rows), :], sems.at[i]))
    return made


def start_all(copies):
    for copy in copies:
        copy.start()


def wait_all(copies):
    for copy in copies:
        copy.wait()


def swap(block, tp, bit):
    return lax.ppermute(block, "tp", xor_pairs(tp, bit))


def onward_sum(keep, first):
    quarter = keep.shape[0] // 2
    return (keep[quarter:].astype(F32) + first[quarter:].astype(F32)).astype(BF)


def sum_exchange(keep, send, tp):
    first = swap(send, tp, 1)
    return keep, first, swap(onward_sum(keep, first), tp, 2)


def spread_rows(own, tp, rings=()):
    across, beside = swap(own, tp, 2), swap(own, tp, 1)
    if rings:
        across = join(rings, across)
    return [own, across, beside, swap(across, tp, 1)]


def summed(keep, first, second):
    quarter = second.shape[0]
    near = keep[0:quarter, :].astype(F32) + first[0:quarter, :].astype(F32)
    return near + second[...].astype(F32)


def halves(array, keep, send, cols=slice(None)):
    half = array.shape[0] // 2
    keep[:, cols] = array[:half].astype(BF)
    send[:, cols] = array[half:].astype(BF)


def mean_last(value):
    return jnp.mean(value, axis=-1, keepdims=True)


def norm_along(unit, inverse, along):
    shifted = along - mean_last(along)
    return inverse * (shifted - unit * mean_last(unit * shifted))


def sum_rows(value):
    return jnp.sum(value, axis=0, keepdims=True)


def split_sums(lines):
    width = lines[0].shape[-1]
    missing = EXTRA // 2 - sum(line.shape[0] for line in lines)
    blank = [jnp.zeros((missing, width), F32)] if missing else []
    whole = jnp.concatenate([*lines, *blank]) if len(lines) + missing > 1 else lines[0]
    rounded = whole.astype(BF).astype(F32)
    return jnp.concatenate([rounded, whole - rounded]).astype(BF)


def tree_sum(four):
    return (four[0] + four[1]) + (four[2] + four[3])


def joined_sums(block):
    return block[: EXTRA // 2].astype(F32) + block[EXTRA // 2 :].astype(F32)


def pair_rows(array, pair, quarter, cols):
    near, far = pair * quarter, (pair + 2) * quarter
    return jnp.concatenate([array[near : near + quarter, cols], array[far : far + quarter, cols]])


def put_pair(ref, pair, quarter, cols, value):
    near, far = pair * quarter, (pair + 2) * quarter
    ref[near : near + quarter, cols] = value[:quarter]
    ref[far : far + quarter, cols] = value[quarter:]


def positions(me, quarter):
    local = lax.broadcasted_iota(jnp.int32, (1, SEQ), 1)
    half = jnp.where(local < quarter, me % 2, 1 - me % 2)
    return half * quarter + lax.rem(local, quarter)


def attention_forward(count, cols, where, x_ref, params, *refs):
    shards, refs = refs[:count], refs[count:]
    rel, mixed, probs, context, keep, send, whole, sems = refs
    copies = shard_copies(where, shards, whole, sems)
    start_all(copies)
    me = where[0]
    quarter = x_ref.shape[0] // 4
    for i, block in enumerate(BLOCKS):
        start = pl.multiple_of((me ^ block) * quarter, quarter)
        rel[i * quarter : (i + 1) * quarter, :] = x_ref[pl.ds(start, quarter), :]
    wait_all(copies)
    for third in range(3):
        part = slice(third * cols, (third + 1) * cols)
        mixed[:, part] = (dot(rel[...], whole[:, part], NN) + params[0:1, part]).astype(BF)
    slots = positions(me, quarter)
    heads = cols // HEAD
    for pair in range(2):
        valid = slots < where[2 + ((me // 2) ^ pair)]
        for head in range(heads):
            query, key, value = [
                pair_rows(mixed, pair, quarter, slice(at, at + HEAD))
                for at in range(head * HEAD, 3 * cols, cols)
            ]
            scores = jnp.where(valid, dot(query, key, NT) * SCALE, jnp.float32(-1e30))
            expo = jnp.exp(scores - jnp.max(scores, axis=-1, keepdims=True))
            prob = expo / jnp.sum(expo, axis=-1, keepdims=True)
            probs[pair * heads + head] = prob
            result = dot(prob.astype(BF), value, NN).astype(BF)
            put_pair(context, pair, quarter, slice(head * HEAD, (head + 1) * HEAD), result)

    def project(cut):
        halves(dot(context[...], whole[cut, 3 * cols : 4 * cols], NT), keep, send, cut)

    tiles(keep.shape[1], project)


def attention_tangent(
    cols, at, where, rel, mixed, probs, context, whole, along, keep, send, tmixed, tcontext
):
    me = where[0]
    quarter = rel.shape[0] // 4
    for third in range(3):
        part = slice(third * cols, (third + 1) * cols)
        there = slice(at + third * cols, at + (third + 1) * cols)
        tmixed[:, part] = dot(rel[...], along[:, there], NN).astype(BF)
    slots = positions(me, quarter)
    heads = cols // HEAD
    for pair in range(2):
        valid = slots < where[2 + ((me // 2) ^ pair)]
        for head in range(heads):
            columns = [slice(at, at + HEAD) for at in range(head * HEAD, 3 * cols, cols)]
            query, key, value = [pair_rows(mixed, pair, quarter, at) for at in columns]
            tquery, tkey, tvalue = [pair_rows(tmixed, pair, quarter, at) for at in columns]
            prob = probs[pair * heads + head]
            tscores = (dot(tquery, key, NT) + dot(query, tkey, NT)) * SCALE
            tscores = jnp.where(valid, tscores, jnp.float32(0.0))
            total = jnp.sum(tscores * prob, axis=-1, keepdims=True)
            tprob = (prob * (tscores - total)).astype(BF)
            result = dot(tprob, value, NN) + dot(prob.astype(BF), tvalue, NN)
            put_pair(
                tcontext, pair, quarter, slice(head * HEAD, (head + 1) * HEAD), result.astype(BF)
            )

    def project(cut):
        part = dot(tcontext[...], whole[cut, 3 * cols : 4 * cols], NT)
        part = part + dot(context[...], along[cut, at + 3 * cols : at + 4 * cols], NT)
        halves(part, keep, send, cut)

    tiles(keep.shape[1], project)


def first_norm(x_rel, keep, came, second, params, first, unit, inverse, low):
    own = second.shape[0]
    resid = x_rel[0:own, :].astype(F32) + summed(keep, came, second) + params[1:2, :]
    center = resid - mean_last(resid)
    inv = lax.rsqrt(mean_last(center * center) + EPSILON)
    whitened = center * inv
    unit[...] = whitened
    inverse[...] = jnp.broadcast_to(inv, inverse.shape)
    value = whitened * params[2:3, :] + params[3:4, :]
    first[...] = value
    low[...] = value.astype(BF)


def first_norm_tangent(keep, came, second, params, unit, inverse, tfirst, low):
    along = norm_along(unit[...], inverse[:, 0:1], summed(keep, came, second)) * params[2:3, :]
    tfirst[...] = along
    low[...] = along.astype(BF)


def pack_weights(*refs):
    at, out = 0, refs[-1]
    for ref in refs[:-2]:
        out[:, at : at + ref.shape[1]] = ref[...]
        at = at + ref.shape[1]
    out[:, at:] = refs[-2][...].astype(F32).T.astype(BF)


def collect(pieces, rel):
    quarter = rel.shape[0] // 4
    for i, piece in enumerate(pieces):
        rel[i * quarter : (i + 1) * quarter, :] = piece[0:quarter, :]


def feed_forward(count, hidden, where, params, *refs):
    pieces, refs = refs[:4], refs[4:]
    shards, refs = refs[:count], refs[count:]
    rel, active, slope, keep, send, whole, sems = refs
    copies = shard_copies(where, shards, whole, sems)
    start_all(copies)
    collect(pieces, rel)
    wait_all(copies)

    def up(cut):
        upper = dot(rel[...], whole[:, cut], NN) + params[4:5, cut]
        half = 0.5 + 0.5 * lax.erf(upper * (2.0 ** -0.5))
        active[:, cut] = (upper * half).astype(BF)
        bell = jnp.exp(-0.5 * upper * upper) * 0.3989422804014327
        slope[:, cut] = half + upper * bell

    tiles(hidden, up)

    def down(cut):
        halves(dot(active[...], whole[cut, hidden : 2 * hidden], NT), keep, send, cut)

    tiles(keep.shape[1], down)


def feed_forward_tangent(count, hidden, where, *refs):
    pieces, (rel, active, slope, whole), refs = refs[:4], refs[4:8], refs[8:]
    tshards, refs = refs[:count], refs[count:]
    keep, send, twhole, sems, trel, tactive = refs
    copies = shard_copies(where, tshards, twhole, sems)
    start_all(copies)
    collect(pieces, trel)
    wait_all(copies)

    def up(cut):
        tupper = dot(trel[...], whole[:, cut], NN) + dot(rel[...], twhole[:, cut], NN)
        tactive[:, cut] = (slope[:, cut] * tupper).astype(BF)

    tiles(hidden, up)

    def down(cut):
        part = dot(tactive[...], whole[cut, hidden : 2 * hidden], NT)
        part = part + dot(active[...], twhole[cut, hidden:], NT)
        halves(part, keep, send, cut)

    tiles(keep.shape[1], down)


def second_norm(
    where, keep, came, second, params, first, upstream,
    result, grad, low, unit, inverse,
):
    resid = first[...] + summed(keep, came, second) + params[5:6, :]
    center = resid - mean_last(resid)
    inv = lax.rsqrt(mean_last(center * center) + EPSILON)
    whitened = center * inv
    own = second.shape[0]
    unit[...] = whitened
    inverse[...] = jnp.broadcast_to(inv, inverse.shape)
    result[...] = (whitened * params[6:7, :] + params[7:8, :]).astype(BF)
    back = upstream[pl.ds(pl.multiple_of(where[0] * own, own), own), :].astype(F32)
    value = norm_along(whitened, inv, back * params[6:7, :])
    grad[...] = value
    low[0:own, :] = value.astype(BF)
    low[own:, :] = split_sums([sum_rows(value), sum_rows(back * whitened), sum_rows(back)])


def second_norm_tangent(keep, came, second, params, tfirst, unit, inverse, result):
    along = tfirst[...] + summed(keep, came, second)
    result[...] = (norm_along(unit[...], inverse[:, 0:1], along) * params[6:7, :]).astype(BF)


def first_norm_backward(
    keep, came, second, params, grad_two, unit, inverse, grad, low
):
    back = grad_two[...] + summed(keep, came, second)
    value = norm_along(unit[...], inverse[:, 0:1], back * params[2:3, :])
    own = second.shape[0]
    grad[...] = value
    low[0:own, :] = value.astype(BF)
    low[own:, :] = split_sums([sum_rows(value), sum_rows(back * unit[...]), sum_rows(back)])


def piece_sums(pieces):
    own = pieces[0].shape[0] - EXTRA
    return tree_sum([joined_sums(piece[own:, :]) for piece in pieces])


def feed_forward_backward(hidden, *refs):
    pieces, (slope, whole) = refs[:4], refs[4:6]
    rel, grad_upper, sums, keep, send = refs[6:]
    collect(pieces, rel)
    sums[...] = piece_sums(pieces)

    def down(cut):
        there = pl.ds(pl.multiple_of(cut.start + hidden, cut.size), cut.size)
        value = dot(rel[...], whole[:, there], NN) * slope[:, cut]
        sums[3:4, cut] = sum_rows(value)
        grad_upper[:, cut] = value.astype(BF)

    tiles(hidden, down)

    def up(cut):
        halves(dot(grad_upper[...], whole[cut, :hidden], NT), keep, send, cut)

    tiles(keep.shape[1], up)


def put_owned(groups, where, step, targets, sums):
    if len(targets) == 1:
        targets[0][...] = step[...]
        return
    rows = step.shape[0] // 8
    spare = step.shape[1] - sums.shape[1]
    if spare:
        sums = jnp.concatenate([sums, jnp.zeros((EXTRA // 2, spare), F32)], axis=1)
    extra = split_sums([sums])

    def put(target, at, owner):
        start = pl.multiple_of((where[1] ^ owner) * rows, rows)
        target[at, 0:rows, :] = step[pl.ds(start, rows), :]
        target[at, rows:, :] = extra

    for z in range(4):
        put(targets[0], z, 2 * z)
    for target, group in zip(targets[1:], groups):
        for at, z in enumerate(group):
            put(target, at, 2 * z + 1)


def feed_forward_weights(where, rel, active, first, grad_upper, sums, *refs):
    targets, step = refs[:-1], refs[-1]
    hidden = active.shape[1]

    def one(cut):
        step[cut, :hidden] = dot(rel[:, cut], active[...], TN).astype(BF)
        step[cut, hidden:] = dot(first[:, cut], grad_upper[...], TN).astype(BF)

    tiles(rel.shape[1], one)
    put_owned(FF_GROUPS, where, step, targets, sums[...])


def attention_backward(cols, *refs):
    pieces, (mixed, probs, whole) = refs[:4], refs[4:7]
    rel, grad, sums, keep, send, back = refs[7:]
    collect(pieces, rel)
    sums[...] = piece_sums(pieces)
    quarter = rel.shape[0] // 4
    back[...] = dot(rel[...], whole[:, 3 * cols : 4 * cols], NN).astype(BF)
    heads = cols // HEAD
    for pair in range(2):
        for head in range(heads):
            columns = [slice(at, at + HEAD) for at in range(head * HEAD, 3 * cols, cols)]
            query, key, value = [pair_rows(mixed, pair, quarter, at) for at in columns]
            prob = probs[pair * heads + head]
            grad_context = pair_rows(back, pair, quarter, columns[0])
            grad_value = dot(prob.astype(BF), grad_context, TN)
            grad_prob = dot(grad_context, value, NT)
            total = jnp.sum(grad_prob * prob, axis=-1, keepdims=True)
            grad_score = (prob * (grad_prob - total)).astype(BF)
            put_pair(grad, pair, quarter, columns[2], grad_value.astype(BF))
            grad_query = dot(grad_score, key, NN) * SCALE
            put_pair(grad, pair, quarter, columns[0], grad_query.astype(BF))
            grad_key = dot(grad_score, query, TN) * SCALE
            put_pair(grad, pair, quarter, columns[1], grad_key.astype(BF))

    def project(cut):
        halves(dot(grad[...], whole[cut, : 3 * cols], NT), keep, send, cut)

    tiles(keep.shape[1], project)


def attention_weights(paired, cols, where, rel, grad, sums, x_rel, context, *refs):
    count = 1 + len(LAST_GROUPS) if paired else 1
    targets, refs = refs[:count], refs[count:]
    (step,) = refs[-1:]

    def one(cut):
        step[cut, : 3 * cols] = dot(x_rel[:, cut], grad[...], TN).astype(BF)
        step[cut, 3 * cols :] = dot(rel[:, cut], context[...], TN).astype(BF)

    tiles(x_rel.shape[1], one)
    mixed = sum_rows(grad[...].astype(F32))
    mixed = jnp.concatenate([mixed, jnp.zeros((1, cols), F32)], axis=1)
    lines = jnp.concatenate([sums[0:3, :], mixed])
    put_owned(LAST_GROUPS, where, step, targets, lines)
    if not paired:
        refs[0][...] = lines


def fold_shards(group, keep, came, *outs):
    outs = list(outs)
    for at, z in enumerate(group):
        out = outs.pop(0)
        rows = keep.shape[1] - EXTRA
        total = keep[z, 0:rows, :].astype(F32) + came[at, 0:rows, :].astype(F32)
        sums = joined_sums(keep[z, rows:, :]) + joined_sums(came[at, rows:, :])
        rounded = split_sums([sums])
        if z == 0:
            out[...] = total
            outs.pop(0)[...] = joined_sums(rounded)
        else:
            out[0:rows, :] = total.astype(BF)
            out[rows:, :] = rounded


def last_total(refs):
    rows = refs[0].shape[0]
    total = refs[0][...]
    for ref in refs[1:4]:
        total = total + ref[0:rows, :].astype(F32)
    return total


def last_sums(refs, outs):
    rows = refs[0].shape[0]
    sums = tree_sum([refs[4][...]] + [joined_sums(ref[rows:, :]) for ref in refs[1:4]])
    for i, out in enumerate(outs):
        out[...] = sums[i, : out.shape[0]]


def finish_feed_forward(hidden, *refs):
    total = last_total(refs)
    refs[5][...] = total[:, :hidden]
    refs[6][...] = total[:, hidden:]
    last_sums(refs, refs[7:])


def finish_attention(cols, *refs):
    total = last_total(refs)
    for i in range(3):
        refs[5 + i][...] = total[:, i * cols : (i + 1) * cols]
    refs[8][...] = total[:, 3 * cols :].T
    last_sums(refs, refs[9:])


def last_sum(keep, came, second, grad_one, out):
    out[...] = (grad_one[...] + summed(keep, came, second)).astype(BF)


def place_rows(count, where, *refs):
    pieces, outs, sems = refs[: 4 * count], refs[4 * count : 5 * count], refs[5 * count]
    own = pieces[0].shape[0]
    copies = []
    for i, out in enumerate(outs):
        for j, block in enumerate(BLOCKS):
            start = pl.multiple_of((where[0] ^ block) * own, own)
            copies.append(
                pltpu.make_async_copy(
                    pieces[4 * i + j], out.at[pl.ds(start, own), :], sems.at[4 * i + j]
                )
            )
    start_all(copies)
    wait_all(copies)


def per_device(tp, dp, *arrays):
    (
        layer_input,
        pair_lengths,
        query_weight,
        query_bias,
        key_weight,
        value_weight,
        value_bias,
        out_weight,
        out_bias,
        first_gain,
        first_shift,
        up_weight,
        up_bias,
        down_weight,
        down_bias,
        second_gain,
        second_shift,
        out_grad,
        query_tangent,
        key_tangent,
        value_tangent,
        out_tangent,
        up_tangent,
        down_tangent,
    ) = arrays
    rows, width = layer_input.shape
    cols = query_weight.shape[1]
    hidden = up_weight.shape[1]
    heads = cols // HEAD
    own = rows // tp
    half = rows // 2
    shard = width // dp
    paired = dp == len(SNAKE)

    place = jnp.stack([lax.axis_index("tp"), lax.axis_index("dp")]).astype(jnp.int32)
    where = jnp.concatenate([place, pair_lengths])
    zeros = jnp.zeros((cols,), F32)
    params = jnp.concatenate(
        [query_bias, zeros, value_bias, zeros, out_bias, first_gain, first_shift]
        + [up_bias, down_bias, second_gain, second_shift]
    ).reshape(8, width)
    parts = [((half, width), BF), ((half, width), BF)]
    piece = ((own + EXTRA, width), BF)
    lines = ((EXTRA // 2, width), F32)
    full_own = ((own, width), F32)
    attn_rows = ((width, 4 * cols), BF)
    ff_rows = ((width, 2 * hidden + 4 * cols), BF)
    tff_rows = ((width, 2 * hidden), BF)

    def pack(first_one, *blocks):
        return jnp.concatenate([first_one, *blocks], 1)

    def arriving(count):
        return pltpu.SemaphoreType.DMA((count,))

    where, out_rows, params = join((), where, out_weight.T, params)
    attn = Ring(pack(query_weight, key_weight, value_weight, out_rows), dp)
    attn.step()
    early = attn.parts[-1]
    tangents = (query_tangent, key_tangent, value_tangent)
    group = call(
        pack_weights,
        "pack_weights",
        [((shard, 2 * hidden + 4 * cols), BF)],
        (after(up_weight, early), down_weight.T, *tangents, out_tangent),
    )
    ff = Ring(group[0], dp)
    tff = Ring(pack(after(up_tangent, early), down_tangent.T), dp)
    attn.step()
    join([attn, ff])
    attn.step()
    ff.step()
    join([attn, ff])
    attn.step()
    where, attn.parts[-1] = join([ff], where, attn.parts[-1])
    ff.step()
    count = len(attn.parts)
    x_rel, mixed, probs, context, keep, send, attn_whole = call(
        functools.partial(attention_forward, count, cols),
        "attention_forward",
        [
            ((rows, width), BF),
            ((rows, 3 * cols), BF),
            ((2 * heads, SEQ, SEQ), F32),
            ((rows, cols), BF),
            *parts,
            attn_rows,
        ],
        (where, layer_input, params),
        attn.parts,
        [arriving(count)],
    )
    keep, send = join([ff], keep, send)
    ff.step()
    first, unit_one, inverse_one, first_low = call(
        first_norm,
        "first_norm",
        [full_own, full_own, ((own, 128), F32), ((own, width), BF)],
        (x_rel, *sum_exchange(keep, send, tp), params),
    )
    first_low = join([ff], first_low)
    ff.step()
    pieces = spread_rows(first_low, tp, [ff])
    pieces[3] = join([tff], pieces[3])
    tff.step()
    first_rel, active, slope, keep, send, ff_whole = call(
        functools.partial(feed_forward, count, hidden),
        "feed_forward",
        [((rows, width), BF), ((rows, hidden), BF), ((rows, hidden), F32), *parts, ff_rows],
        (where, params, *pieces),
        ff.parts,
        [arriving(count)],
    )
    keep, send = join([tff], keep, send)
    tff.step()
    keep, first_came, second = sum_exchange(keep, send, tp)
    tkeep, tsend = call(
        functools.partial(attention_tangent, cols, 2 * hidden),
        "attention_tangent",
        parts,
        (after(where, keep), x_rel, mixed, probs, context, attn_whole, ff_whole),
        (),
        [pltpu.VMEM((rows, 3 * cols), BF), pltpu.VMEM((rows, cols), BF)],
    )
    second, tkeep, tsend = join([tff], second, tkeep, tsend)
    tff.step()
    result, grad_two, grad_two_low, unit_two, inverse_two = call(
        second_norm,
        "second_norm",
        [((own, width), BF), full_own, piece, full_own, ((own, 128), F32)],
        (where, keep, first_came, second, params, first, out_grad),
    )
    pieces = spread_rows(grad_two_low, tp)
    tfirst_came = swap(tsend, tp, 1)
    pieces[1], tfirst_came = join([], pieces[1], tfirst_came)
    tsecond = swap(onward_sum(tkeep, tfirst_came), tp, 2)
    pieces[3] = join([tff], pieces[3])
    tff.step()
    grad_down, grad_upper, sums_up, keep, send = call(
        functools.partial(feed_forward_backward, hidden),
        "feed_forward_backward",
        [((rows, width), BF), ((rows, hidden), BF), lines, *parts],
        (*pieces, slope, ff_whole),
    )
    result_pieces = spread_rows(result, tp)
    keep, send, grad_down, grad_upper, result_pieces[1] = join(
        [], keep, send, grad_down, grad_upper, result_pieces[1]
    )

    def weight_outs(total, groups):
        if paired:
            counts = [4] + [len(group) for group in groups]
            return [((count, shard + EXTRA, total), BF) for count in counts]
        return [((width, total), BF)]

    def swap_shards(steps, index):
        return lax.ppermute(steps[1 + index], "dp", xor_pairs(dp, 1)) if paired else steps[0]

    def fold(steps, came, group):
        if not paired:
            return came
        total = came.shape[2]
        outs = []
        for z in group:
            if z == 0:
                outs = outs + [((shard, total), F32), ((EXTRA // 2, total), F32)]
            else:
                outs.append(((shard + EXTRA, total), BF))
        return call(functools.partial(fold_shards, group), "fold_shards", outs, (steps[0], came))

    def send_on(folded, group):
        if not paired:
            return folded
        moved = [
            lax.ppermute(value, "dp", xor_pairs(dp, 2 * z)) for value, z in zip(folded, group) if z
        ]
        return moved + folded[len(moved) :]

    first_came = swap(send, tp, 1)
    second = swap(onward_sum(keep, first_came), tp, 2)
    ff_steps = call(
        feed_forward_weights,
        "feed_forward_weights",
        weight_outs(2 * hidden, FF_GROUPS),
        (where, grad_down, active, first_rel, after(grad_upper, first_came), sums_up),
        (),
        [pltpu.VMEM((width, 2 * hidden), BF)],
    )
    tfirst, tfirst_low = call(
        first_norm_tangent,
        "first_norm_tangent",
        [full_own, ((own, width), BF)],
        (tkeep, tfirst_came, tsecond, after(params, ff_steps[0]), unit_one, inverse_one),
    )
    second, ff_steps, tff.front, tfirst_low, result_pieces = join_lists(
        second, ff_steps, tff.front, tfirst_low, result_pieces
    )
    tff.step()
    grad_one, grad_one_low = call(
        first_norm_backward,
        "first_norm_backward",
        [full_own, piece],
        (keep, first_came, second, params, grad_two, unit_one, inverse_one),
    )
    pieces = spread_rows(grad_one_low, tp)
    tpieces = spread_rows(tfirst_low, tp)
    ff_two = swap_shards(ff_steps, 0)
    pieces[3], ff_two, ff_steps = join_lists(pieces[3], ff_two, ff_steps)
    ff_three = swap_shards(ff_steps, 1)
    ff_two = fold(ff_steps, ff_two, FF_GROUPS[0])
    pieces[3], ff_two = join_lists(pieces[3], ff_two)
    ff_two = send_on(ff_two, FF_GROUPS[0])
    grad_attn, grad_mixed, sums_one, keep, send = call(
        functools.partial(attention_backward, cols),
        "attention_backward",
        [((rows, width), BF), ((rows, 3 * cols), BF), lines, *parts],
        (*pieces, mixed, probs, attn_whole),
        (),
        [pltpu.VMEM((rows, cols), BF)],
    )
    keep, send, ff_three, tpieces[1] = join([], keep, send, ff_three, tpieces[1])
    ff_one = swap_shards(ff_steps, 2)
    first_came = swap(send, tp, 1)
    last_steps = call(
        functools.partial(attention_weights, paired, cols),
        "attention_weights",
        weight_outs(4 * cols, LAST_GROUPS) + ([] if paired else [lines]),
        (where, grad_attn, grad_mixed, sums_one, x_rel, context),
        (),
        [pltpu.VMEM(*attn_rows)],
    )
    ff_three = fold(ff_steps, ff_three, FF_GROUPS[1])
    first_came, last_steps, tpieces[3], ff_three, ff_steps = join_lists(
        first_came, last_steps, tpieces[3], ff_three, ff_steps
    )
    ff_zero = swap_shards(ff_steps, 3)
    second = swap(onward_sum(keep, first_came), tp, 2)
    last_near = swap_shards(last_steps, 0)
    ff_three = send_on(ff_three, FF_GROUPS[1])
    tkeep, tsend = call(
        functools.partial(feed_forward_tangent, count, hidden),
        "feed_forward_tangent",
        parts,
        (after(where, last_steps[0]), *tpieces, first_rel, active, slope, ff_whole),
        tff.parts,
        [pltpu.VMEM(*tff_rows), arriving(count)]
        + [pltpu.VMEM((rows, width), BF), pltpu.VMEM((rows, hidden), BF)],
    )
    second, tkeep, tsend, last_near, ff_one, ff_two, last_steps = join_lists(
        second, tkeep, tsend, last_near, ff_one, ff_two, last_steps
    )
    last_far = swap_shards(last_steps, 1)
    tfirst_came = swap(tsend, tp, 1)
    ff_one = send_on(fold(ff_steps, ff_one, FF_GROUPS[2]), FF_GROUPS[2])
    (grad_input,) = call(
        last_sum, "last_sum", [((own, width), BF)], (keep, first_came, second, grad_one)
    )
    pieces = spread_rows(grad_input, tp)
    tsecond = swap(onward_sum(tkeep, tfirst_came), tp, 2)
    last_near = send_on(fold(last_steps, last_near, LAST_GROUPS[0]), LAST_GROUPS[0])
    pieces[1], last_far, tsecond, ff_three = join_lists(pieces[1], last_far, tsecond, ff_three)
    last_far = send_on(fold(last_steps, last_far, LAST_GROUPS[1]), LAST_GROUPS[1])
    (tresult,) = call(
        second_norm_tangent,
        "second_norm_tangent",
        [((own, width), BF)],
        (tkeep, tfirst_came, tsecond, params, tfirst, unit_two, inverse_two),
    )
    tresult, last_near = join_lists(tresult, last_near)
    tresult_pieces = spread_rows(tresult, tp)
    ff_zero = fold(ff_steps, ff_zero, FF_GROUPS[3])
    if paired:
        ff_folded = [ff_zero[0], ff_one[0], ff_two[0], ff_three[0], ff_zero[1]]
        last_folded = [last_far[1], last_far[0], *last_near, last_far[2]]
    else:
        ff_folded, last_folded = [ff_zero], [last_far]

    def finish(body, name, outs, folded):
        return call(body, name, outs, folded)

    vector = ((width,), F32)
    if paired:
        own_down, own_up, *sums_two = finish(
            functools.partial(finish_feed_forward, hidden),
            "finish_feed_forward",
            [((shard, hidden), F32)] * 2 + [vector] * 4,
            ff_folded,
        )
        *own_mixed, own_out, bias_out, gain_one, shift_one, mixed_sums = finish(
            functools.partial(finish_attention, cols),
            "finish_attention",
            [((shard, cols), F32)] * 3 + [((cols, shard), F32)] + [vector] * 4,
            last_folded,
        )
        sums_one = [bias_out, gain_one, shift_one]
    else:

        def all_summed(step):
            split = step.reshape(dp, shard, -1)
            came = lax.all_to_all(split, "dp", 0, 0, tiled=True)
            return jnp.sum(came.astype(F32), axis=0)

        own_ff = all_summed(ff_folded[0])
        own_down, own_up = own_ff[:, :hidden], own_ff[:, hidden:]
        last = all_summed(last_folded[0])
        own_mixed = [last[:, i * cols : (i + 1) * cols] for i in range(3)]
        own_out = last[:, 3 * cols :].T
        sums_two = list(lax.psum(sums_up, "dp"))
        *sums_one, mixed_sums = list(lax.psum(last_steps[1], "dp"))

    def all_rows(*spread):
        return call(
            functools.partial(place_rows, len(spread)),
            "place_rows",
            [((rows, width), BF)] * len(spread),
            (where, *[piece for pieces in spread for piece in pieces]),
            scratch=[arriving(4 * len(spread))],
            any_outs=True,
        )

    whole_result, whole_grad = all_rows(result_pieces, pieces)
    (whole_tresult,) = all_rows(tresult_pieces)
    return (
        whole_result,
        whole_grad,
        whole_tresult,
        own_mixed[0],
        mixed_sums[:cols],
        own_mixed[1],
        own_mixed[2],
        mixed_sums[2 * cols : 3 * cols],
        own_out,
        *sums_one,
        own_up,
        sums_two[3],
        own_down.T,
        *sums_two[:3],
    )


def solution(mesh):
    wide, tall, col, row, full = P("dp", "tp"), P("tp", "dp"), P("tp"), P("dp", None), P()
    placed = (
        (row, P("dp"), wide, col, wide, wide, col, tall, full, full, full, wide, col, tall)
        + (full, full, full, row, wide, wide, wide, tall, wide, tall)
    )
    results = (row, row, row, wide, col, wide, wide, col, tall, full, full, full)
    results = results + (wide, col, tall, full, full, full)
    tp, dp = mesh.shape["tp"], mesh.shape["dp"]

    def body(*arrays):
        return per_device(tp, dp, *arrays)

    return jax.shard_map(
        body, mesh=mesh, in_specs=placed, out_specs=results, check_vma=False
    )
```

```python
import functools
import math

import jax
import jax.numpy as jnp
from jax import lax
from jax.experimental import pallas as pl
from jax.experimental.pallas import tpu as pltpu
from jax.sharding import PartitionSpec as P

HEAD = 64
SEQ = 256
EPSILON = 1e-06
SCALE = HEAD ** (-0.5)
BLOCKS = (0, 2, 1, 3)
FF_GROUPS = ((2,), (3,), (1,), (0,))
LAST_GROUPS = ((2, 3), (1, 0))
SNAKE = (0, 2, 4, 6, 7, 5, 3, 1)
EXTRA = 8
BF = jnp.bfloat16
F32 = jnp.float32
PLAN = {
    "xf0": ("P1", "P4"),
    "zf0": ("P4", "P7"),
    "xf1": ("P4", "P7"),
    "zf1": ("P6", "P9"),
    "xf2": ("P2", "P7"),
    "zf2": ("P7", None),
    "xf3": ("P6b", "P12"),
    "zf3": ("P11", None),
    "xl0": ("P6", "P7"),
    "zl0": ("P7", "P12"),
    "xl1": ("P8", "P9"),
    "zl1": ("P10", "P12"),
    "r2": ("P1", "P5"),
    "r3": ("P5", None),
    "a0": ("P2", "P7"),
    "a1": ("P4", "P7"),
    "n": ("P6", None),
    "h0": ("P6b", "P12"),
    "h1": ("P7", "P13"),
}
VMEM_LIMIT = 16 * 1024 * 1024
TILE = 256

NN = ((1,), (0,))
NT = ((1,), (1,))
TN = ((0,), (0,))


def dot(left, right, dims):
    return lax.dot_general(left, right, (dims, ((), ())), preferred_element_type=F32)


def xor_pairs(size, bit):
    return [(i, i ^ bit) for i in range(size)]


def call(body, name, outs, near, shards=(), scratch=(), any_outs=False):
    smem = [a.dtype == jnp.int32 for a in near]
    specs = [pl.BlockSpec(memory_space=pltpu.SMEM if s else pltpu.VMEM) for s in smem]
    specs = specs + [pl.BlockSpec(memory_space=pl.ANY)] * len(shards)
    out_space = pltpu.HBM if any_outs else pltpu.VMEM
    return list(pl.pallas_call(
        body,
        out_shape=[jax.ShapeDtypeStruct(shape, kind) for shape, kind in outs],
        in_specs=specs,
        out_specs=[pl.BlockSpec(memory_space=out_space)] * len(outs),
        scratch_shapes=list(scratch),
        name=name,
        compiler_params=pltpu.CompilerParams(vmem_limit_bytes=VMEM_LIMIT),
        cost_estimate=pl.CostEstimate(flops=1, bytes_accessed=1, transcendentals=0),
    )(*near, *shards))


def tiles(width, body):
    step = TILE if width % TILE == 0 else width

    def one(i, carry):
        body(pl.ds(pl.multiple_of(i * step, step), step))
        return carry

    lax.fori_loop(0, width // step, one, 0)


def after(value, *others):
    return lax.optimization_barrier((value, *others))[0]


class Ring:
    def __init__(self, shard, dp):
        self.near = dp == len(SNAKE)
        self.dp = dp
        self.front = [shard, shard]
        self.parts = [shard]
        self.steps = 0

    def step(self):
        if not self.near:
            if self.steps == 0:
                self.parts = [lax.all_gather(self.parts[0], "dp", axis=0, tiled=True)]
                self.front = [self.parts[0]] * 2
            self.steps += 1
            return
        if self.steps == self.dp // 2:
            return
        ahead = [(SNAKE[i], SNAKE[(i + 1) % self.dp]) for i in range(self.dp)]
        behind = [(b, a) for a, b in ahead]
        self.steps += 1
        self.front[0] = lax.ppermute(self.front[0], "dp", ahead)
        self.parts.append(self.front[0])
        if self.steps < self.dp // 2:
            self.front[1] = lax.ppermute(self.front[1], "dp", behind)
            self.parts.append(self.front[1])


def join(rings, *values):
    fronts = [front for ring in rings for front in ring.front]
    joined = lax.optimization_barrier((*values, *fronts))
    for i, ring in enumerate(rings):
        ring.front = list(joined[len(values) + 2 * i :][:2])
    return joined[0] if len(values) == 1 else joined[: len(values)]


class Flow:
    def __init__(self):
        self.makers, self.values = {}, {}

    def add(self, name, maker, needs, send):
        self.makers[name] = (maker, needs, send)

    def value_of(self, name):
        return self.values[name]

    def point(self, name, *values):
        start = [key for key in PLAN if PLAN[key][0] == name and key in self.makers]
        due = [key for key in PLAN if PLAN[key][1] == name and key in self.values]
        inputs = {}
        for key in start:
            maker, needs, _ = self.makers[key]
            inputs[key] = maker(*[self.values[need] for need in needs])
        results = join_lists(*values, *[inputs[key] for key in start], *[self.values[key] for key in due])
        count = len(values)
        for key, value in zip(due, results[count + len(start) :]):
            self.values[key] = value
        for key, value in zip(start, results[count : count + len(start)]):
            self.values[key] = self.makers[key][2](value)
        return results[0] if count == 1 else results[:count]


def ring_owner(me, index):
    size = len(SNAKE)
    place = jnp.where(me % 2 == 0, me // 2, size - 1 - me // 2)
    step = (index + 1) // 2
    place = lax.rem(place + (size - step if index % 2 else step), size)
    return jnp.where(place < size // 2, 2 * place, 2 * (size - 1 - place) + 1)


def join_lists(*values):
    counts = [len(value) if isinstance(value, list) else 1 for value in values]
    flat = [v for value in values for v in (value if isinstance(value, list) else [value])]
    joined = list(lax.optimization_barrier(tuple(flat)))
    results = []
    for value, count in zip(values, counts):
        taken, joined = joined[:count], joined[count:]
        results.append(taken if isinstance(value, list) else taken[0])
    return results


def shard_copies(where, refs, whole, sems):
    rows = whole.shape[0] // len(refs)
    made = []
    for i, ref in enumerate(refs):
        owner = ring_owner(where[1], i) if len(refs) > 1 else 0
        start = pl.multiple_of(owner * rows, rows)
        made.append(pltpu.make_async_copy(ref, whole.at[pl.ds(start, rows), :], sems.at[i]))
    return made


def start_all(copies):
    for copy in copies:
        copy.start()


def wait_all(copies):
    for copy in copies:
        copy.wait()


def swap(block, tp, bit):
    return lax.ppermute(block, "tp", xor_pairs(tp, bit))


def onward_sum(keep, first):
    quarter = keep.shape[0] // 2
    return (keep[quarter:].astype(F32) + first[quarter:].astype(F32)).astype(BF)


def sum_exchange(keep, send, tp):
    first = swap(send, tp, 1)
    return keep, first, swap(onward_sum(keep, first), tp, 2)


def spread_rows(own, tp, rings=()):
    across, beside = swap(own, tp, 2), swap(own, tp, 1)
    if rings:
        across = join(rings, across)
    return [own, across, beside, swap(across, tp, 1)]


def summed(keep, first, second):
    quarter = second.shape[0]
    near = keep[0:quarter, :].astype(F32) + first[0:quarter, :].astype(F32)
    return near + second[...].astype(F32)


def halves(array, keep, send, cols=slice(None)):
    half = array.shape[0] // 2
    keep[:, cols] = array[:half].astype(BF)
    send[:, cols] = array[half:].astype(BF)


def mean_last(value):
    return jnp.mean(value, axis=-1, keepdims=True)


def norm_along(unit, inverse, along):
    shifted = along - mean_last(along)
    return inverse * (shifted - unit * mean_last(unit * shifted))


def sum_rows(value):
    return jnp.sum(value, axis=0, keepdims=True)


def split_sums(lines):
    width = lines[0].shape[-1]
    missing = EXTRA // 2 - sum(line.shape[0] for line in lines)
    blank = [jnp.zeros((missing, width), F32)] if missing else []
    whole = jnp.concatenate([*lines, *blank]) if len(lines) + missing > 1 else lines[0]
    rounded = whole.astype(BF).astype(F32)
    return jnp.concatenate([rounded, whole - rounded]).astype(BF)


def tree_sum(four):
    return (four[0] + four[1]) + (four[2] + four[3])


def joined_sums(block):
    return block[: EXTRA // 2].astype(F32) + block[EXTRA // 2 :].astype(F32)


def pair_rows(array, pair, quarter, cols):
    near, far = pair * quarter, (pair + 2) * quarter
    return jnp.concatenate([array[near : near + quarter, cols], array[far : far + quarter, cols]])


def put_pair(ref, pair, quarter, cols, value):
    near, far = pair * quarter, (pair + 2) * quarter
    ref[near : near + quarter, cols] = value[:quarter]
    ref[far : far + quarter, cols] = value[quarter:]


def positions(me, quarter):
    local = lax.broadcasted_iota(jnp.int32, (1, SEQ), 1)
    half = jnp.where(local < quarter, me % 2, 1 - me % 2)
    return half * quarter + lax.rem(local, quarter)


def attention_forward(count, cols, where, x_ref, params, *refs):
    shards, refs = refs[:count], refs[count:]
    rel, mixed, probs, context, keep, send, whole, sems = refs
    copies = shard_copies(where, shards, whole, sems)
    start_all(copies)
    me = where[0]
    quarter = x_ref.shape[0] // 4
    for i, block in enumerate(BLOCKS):
        start = pl.multiple_of((me ^ block) * quarter, quarter)
        rel[i * quarter : (i + 1) * quarter, :] = x_ref[pl.ds(start, quarter), :]
    wait_all(copies)
    for third in range(3):
        part = slice(third * cols, (third + 1) * cols)
        mixed[:, part] = (dot(rel[...], whole[:, part], NN) + params[0:1, part]).astype(BF)
    slots = positions(me, quarter)
    heads = cols // HEAD
    for pair in range(2):
        valid = slots < where[2 + ((me // 2) ^ pair)]
        for head in range(heads):
            query, key, value = [
                pair_rows(mixed, pair, quarter, slice(at, at + HEAD))
                for at in range(head * HEAD, 3 * cols, cols)
            ]
            scores = jnp.where(valid, dot(query, key, NT) * SCALE, jnp.float32(-1e30))
            expo = jnp.exp(scores - jnp.max(scores, axis=-1, keepdims=True))
            prob = expo / jnp.sum(expo, axis=-1, keepdims=True)
            probs[pair * heads + head] = prob
            result = dot(prob.astype(BF), value, NN).astype(BF)
            put_pair(context, pair, quarter, slice(head * HEAD, (head + 1) * HEAD), result)

    def project(cut):
        halves(dot(context[...], whole[cut, 3 * cols : 4 * cols], NT), keep, send, cut)

    tiles(keep.shape[1], project)


def attention_tangent(
    count, cols, where, rel, mixed, probs, context, whole, *refs
):
    tshards, refs = refs[:count], refs[count:]
    keep, send, twhole, sems, tmixed, tcontext = refs
    copies = shard_copies(where, tshards, twhole, sems)
    start_all(copies)
    wait_all(copies)
    me = where[0]
    quarter = rel.shape[0] // 4
    for third in range(3):
        part = slice(third * cols, (third + 1) * cols)
        tmixed[:, part] = dot(rel[...], twhole[:, part], NN).astype(BF)
    slots = positions(me, quarter)
    heads = cols // HEAD
    for pair in range(2):
        valid = slots < where[2 + ((me // 2) ^ pair)]
        for head in range(heads):
            columns = [slice(at, at + HEAD) for at in range(head * HEAD, 3 * cols, cols)]
            query, key, value = [pair_rows(mixed, pair, quarter, at) for at in columns]
            tquery, tkey, tvalue = [pair_rows(tmixed, pair, quarter, at) for at in columns]
            prob = probs[pair * heads + head]
            tscores = (dot(tquery, key, NT) + dot(query, tkey, NT)) * SCALE
            tscores = jnp.where(valid, tscores, jnp.float32(0.0))
            total = jnp.sum(tscores * prob, axis=-1, keepdims=True)
            tprob = (prob * (tscores - total)).astype(BF)
            result = dot(tprob, value, NN) + dot(prob.astype(BF), tvalue, NN)
            put_pair(
                tcontext, pair, quarter, slice(head * HEAD, (head + 1) * HEAD), result.astype(BF)
            )

    def project(cut):
        part = dot(tcontext[...], whole[cut, 3 * cols : 4 * cols], NT)
        part = part + dot(context[...], twhole[cut, 3 * cols : 4 * cols], NT)
        halves(part, keep, send, cut)

    tiles(keep.shape[1], project)


def first_norm(x_rel, keep, came, second, params, first, unit, inverse, low):
    own = second.shape[0]
    resid = x_rel[0:own, :].astype(F32) + summed(keep, came, second) + params[1:2, :]
    center = resid - mean_last(resid)
    inv = lax.rsqrt(mean_last(center * center) + EPSILON)
    whitened = center * inv
    unit[...] = whitened
    inverse[...] = jnp.broadcast_to(inv, inverse.shape)
    value = whitened * params[2:3, :] + params[3:4, :]
    first[...] = value
    low[...] = value.astype(BF)


def first_norm_tangent(keep, came, second, params, unit, inverse, tfirst, low):
    along = norm_along(unit[...], inverse[:, 0:1], summed(keep, came, second)) * params[2:3, :]
    tfirst[...] = along
    low[...] = along.astype(BF)


def pack_weights(*refs):
    at, out = 0, refs[-1]
    for ref in refs[:-2]:
        out[:, at : at + ref.shape[1]] = ref[...]
        at = at + ref.shape[1]
    out[:, at:] = refs[-2][...].astype(F32).T.astype(BF)


def collect(pieces, rel):
    quarter = rel.shape[0] // 4
    for i, piece in enumerate(pieces):
        rel[i * quarter : (i + 1) * quarter, :] = piece[0:quarter, :]


def feed_forward(count, hidden, where, params, *refs):
    pieces, refs = refs[:4], refs[4:]
    shards, refs = refs[:count], refs[count:]
    rel, active, slope, keep, send, whole, sems = refs
    copies = shard_copies(where, shards, whole, sems)
    start_all(copies)
    collect(pieces, rel)
    wait_all(copies)

    def up(cut):
        upper = dot(rel[...], whole[:, cut], NN) + params[4:5, cut]
        half = 0.5 + 0.5 * lax.erf(upper * (2.0 ** -0.5))
        active[:, cut] = (upper * half).astype(BF)
        bell = jnp.exp(-0.5 * upper * upper) * 0.3989422804014327
        slope[:, cut] = half + upper * bell

    tiles(hidden, up)

    def down(cut):
        halves(dot(active[...], whole[cut, hidden : 2 * hidden], NT), keep, send, cut)

    tiles(keep.shape[1], down)


def feed_forward_tangent(count, hidden, where, *refs):
    pieces, (rel, active, slope, whole), refs = refs[:4], refs[4:8], refs[8:]
    tshards, refs = refs[:count], refs[count:]
    keep, send, twhole, sems, trel, tactive = refs
    copies = shard_copies(where, tshards, twhole, sems)
    start_all(copies)
    collect(pieces, trel)
    wait_all(copies)

    def up(cut):
        tupper = dot(trel[...], whole[:, cut], NN) + dot(rel[...], twhole[:, cut], NN)
        tactive[:, cut] = (slope[:, cut] * tupper).astype(BF)

    tiles(hidden, up)

    def down(cut):
        part = dot(tactive[...], whole[cut, hidden : 2 * hidden], NT)
        part = part + dot(active[...], twhole[cut, hidden:], NT)
        halves(part, keep, send, cut)

    tiles(keep.shape[1], down)


def second_norm(
    where, keep, came, second, params, first, upstream,
    result, grad, low, unit, inverse,
):
    resid = first[...] + summed(keep, came, second) + params[5:6, :]
    center = resid - mean_last(resid)
    inv = lax.rsqrt(mean_last(center * center) + EPSILON)
    whitened = center * inv
    own = second.shape[0]
    unit[...] = whitened
    inverse[...] = jnp.broadcast_to(inv, inverse.shape)
    result[...] = (whitened * params[6:7, :] + params[7:8, :]).astype(BF)
    back = upstream[pl.ds(pl.multiple_of(where[0] * own, own), own), :].astype(F32)
    value = norm_along(whitened, inv, back * params[6:7, :])
    grad[...] = value
    low[0:own, :] = value.astype(BF)
    low[own:, :] = split_sums([sum_rows(value), sum_rows(back * whitened), sum_rows(back)])


def second_norm_tangent(keep, came, second, params, tfirst, unit, inverse, result):
    along = tfirst[...] + summed(keep, came, second)
    result[...] = (norm_along(unit[...], inverse[:, 0:1], along) * params[6:7, :]).astype(BF)


def first_norm_backward(
    keep, came, second, params, grad_two, unit, inverse, grad, low
):
    back = grad_two[...] + summed(keep, came, second)
    value = norm_along(unit[...], inverse[:, 0:1], back * params[2:3, :])
    own = second.shape[0]
    grad[...] = value
    low[0:own, :] = value.astype(BF)
    low[own:, :] = split_sums([sum_rows(value), sum_rows(back * unit[...]), sum_rows(back)])


def piece_sums(pieces):
    own = pieces[0].shape[0] - EXTRA
    return tree_sum([joined_sums(piece[own:, :]) for piece in pieces])


def feed_forward_backward(hidden, *refs):
    pieces, (slope, whole) = refs[:4], refs[4:6]
    rel, grad_upper, sums, keep, send = refs[6:]
    collect(pieces, rel)
    sums[...] = piece_sums(pieces)

    def down(cut):
        there = pl.ds(pl.multiple_of(cut.start + hidden, cut.size), cut.size)
        value = dot(rel[...], whole[:, there], NN) * slope[:, cut]
        sums[3:4, cut] = sum_rows(value)
        grad_upper[:, cut] = value.astype(BF)

    tiles(hidden, down)

    def up(cut):
        halves(dot(grad_upper[...], whole[cut, :hidden], NT), keep, send, cut)

    tiles(keep.shape[1], up)


def put_owned(groups, where, step, targets, sums):
    if len(targets) == 1:
        targets[0][...] = step[...]
        return
    rows = step.shape[0] // 8
    spare = step.shape[1] - sums.shape[1]
    if spare:
        sums = jnp.concatenate([sums, jnp.zeros((EXTRA // 2, spare), F32)], axis=1)
    extra = split_sums([sums])

    def put(target, at, owner):
        start = pl.multiple_of((where[1] ^ owner) * rows, rows)
        target[at, 0:rows, :] = step[pl.ds(start, rows), :]
        target[at, rows:, :] = extra

    for z in range(4):
        put(targets[0], z, 2 * z)
    for target, group in zip(targets[1:], groups):
        for at, z in enumerate(group):
            put(target, at, 2 * z + 1)


def feed_forward_weights(where, rel, active, first, grad_upper, sums, *refs):
    targets, step = refs[:-1], refs[-1]
    hidden = active.shape[1]

    def one(cut):
        step[cut, :hidden] = dot(rel[:, cut], active[...], TN).astype(BF)
        step[cut, hidden:] = dot(first[:, cut], grad_upper[...], TN).astype(BF)

    tiles(rel.shape[1], one)
    put_owned(FF_GROUPS, where, step, targets, sums[...])


def attention_backward(cols, *refs):
    pieces, (mixed, probs, whole) = refs[:4], refs[4:7]
    rel, grad, sums, keep, send, back = refs[7:]
    collect(pieces, rel)
    sums[...] = piece_sums(pieces)
    quarter = rel.shape[0] // 4
    back[...] = dot(rel[...], whole[:, 3 * cols : 4 * cols], NN).astype(BF)
    heads = cols // HEAD
    for pair in range(2):
        for head in range(heads):
            columns = [slice(at, at + HEAD) for at in range(head * HEAD, 3 * cols, cols)]
            query, key, value = [pair_rows(mixed, pair, quarter, at) for at in columns]
            prob = probs[pair * heads + head]
            grad_context = pair_rows(back, pair, quarter, columns[0])
            grad_value = dot(prob.astype(BF), grad_context, TN)
            grad_prob = dot(grad_context, value, NT)
            total = jnp.sum(grad_prob * prob, axis=-1, keepdims=True)
            grad_score = (prob * (grad_prob - total)).astype(BF)
            put_pair(grad, pair, quarter, columns[2], grad_value.astype(BF))
            grad_query = dot(grad_score, key, NN) * SCALE
            put_pair(grad, pair, quarter, columns[0], grad_query.astype(BF))
            grad_key = dot(grad_score, query, TN) * SCALE
            put_pair(grad, pair, quarter, columns[1], grad_key.astype(BF))

    def project(cut):
        halves(dot(grad[...], whole[cut, : 3 * cols], NT), keep, send, cut)

    tiles(keep.shape[1], project)


def attention_weights(paired, cols, where, rel, grad, sums, x_rel, context, *refs):
    count = 1 + len(LAST_GROUPS) if paired else 1
    targets, refs = refs[:count], refs[count:]
    (step,) = refs[-1:]

    def one(cut):
        step[cut, : 3 * cols] = dot(x_rel[:, cut], grad[...], TN).astype(BF)
        step[cut, 3 * cols :] = dot(rel[:, cut], context[...], TN).astype(BF)

    tiles(x_rel.shape[1], one)
    mixed = sum_rows(grad[...].astype(F32))
    mixed = jnp.concatenate([mixed, jnp.zeros((1, cols), F32)], axis=1)
    lines = jnp.concatenate([sums[0:3, :], mixed])
    put_owned(LAST_GROUPS, where, step, targets, lines)
    if not paired:
        refs[0][...] = lines


def fold_shards(group, keep, came, *outs):
    outs = list(outs)
    for at, z in enumerate(group):
        out = outs.pop(0)
        rows = keep.shape[1] - EXTRA
        total = keep[z, 0:rows, :].astype(F32) + came[at, 0:rows, :].astype(F32)
        sums = joined_sums(keep[z, rows:, :]) + joined_sums(came[at, rows:, :])
        rounded = split_sums([sums])
        if z == 0:
            out[...] = total
            outs.pop(0)[...] = joined_sums(rounded)
        else:
            out[0:rows, :] = total.astype(BF)
            out[rows:, :] = rounded


def last_total(refs):
    rows = refs[0].shape[0]
    total = refs[0][...]
    for ref in refs[1:4]:
        total = total + ref[0:rows, :].astype(F32)
    return total


def last_sums(refs, outs, places):
    rows = refs[0].shape[0]
    sums = tree_sum([refs[4][...]] + [joined_sums(ref[rows:, :]) for ref in refs[1:4]])
    for out, (line, start) in zip(outs, places):
        out[...] = sums[line, start : start + out.shape[0]]


def finish_feed_forward(hidden, *refs):
    total = last_total(refs)
    refs[5][...] = total[:, :hidden]
    refs[6][...] = total[:, hidden:]
    last_sums(refs, refs[7:], [(i, 0) for i in range(4)])


def finish_attention(cols, *refs):
    total = last_total(refs)
    for i in range(3):
        refs[5 + i][...] = total[:, i * cols : (i + 1) * cols]
    refs[8][...] = total[:, 3 * cols :].T
    last_sums(refs, refs[9:], [(0, 0), (1, 0), (2, 0), (3, 0), (3, 2 * cols)])


def last_sum(keep, came, second, grad_one, out):
    out[...] = (grad_one[...] + summed(keep, came, second)).astype(BF)


def place_rows(count, where, *refs):
    pieces, outs, sems = refs[: 4 * count], refs[4 * count : 5 * count], refs[5 * count]
    own = pieces[0].shape[0]
    copies = []
    for i, out in enumerate(outs):
        for j, block in enumerate(BLOCKS):
            start = pl.multiple_of((where[0] ^ block) * own, own)
            copies.append(
                pltpu.make_async_copy(
                    pieces[4 * i + j], out.at[pl.ds(start, own), :], sems.at[4 * i + j]
                )
            )
    start_all(copies)
    wait_all(copies)


def per_device(tp, dp, *arrays):
    (
        layer_input,
        pair_lengths,
        query_weight,
        query_bias,
        key_weight,
        value_weight,
        value_bias,
        out_weight,
        out_bias,
        first_gain,
        first_shift,
        up_weight,
        up_bias,
        down_weight,
        down_bias,
        second_gain,
        second_shift,
        out_grad,
        query_tangent,
        key_tangent,
        value_tangent,
        out_tangent,
        up_tangent,
        down_tangent,
    ) = arrays
    rows, width = layer_input.shape
    cols = query_weight.shape[1]
    hidden = up_weight.shape[1]
    heads = cols // HEAD
    own = rows // tp
    half = rows // 2
    shard = width // dp
    paired = dp == len(SNAKE)

    place = jnp.stack([lax.axis_index("tp"), lax.axis_index("dp")]).astype(jnp.int32)
    where = jnp.concatenate([place, pair_lengths])
    zeros = jnp.zeros((cols,), F32)
    params = jnp.concatenate(
        [query_bias, zeros, value_bias, zeros, out_bias, first_gain, first_shift]
        + [up_bias, down_bias, second_gain, second_shift]
    ).reshape(8, width)
    parts = [((half, width), BF), ((half, width), BF)]
    piece = ((own + EXTRA, width), BF)
    lines = ((EXTRA // 2, width), F32)
    full_own = ((own, width), F32)
    attn_rows = ((width, 4 * cols), BF)
    ff_rows = ((width, 2 * hidden), BF)
    tff_rows = ff_rows

    def pack(first_one, *blocks):
        return jnp.concatenate([first_one, *blocks], 1)

    def arriving(count):
        return pltpu.SemaphoreType.DMA((count,))

    where, out_rows, params = join((), where, out_weight.T, params)
    attn = Ring(pack(query_weight, key_weight, value_weight, out_rows), dp)
    attn.step()
    early = attn.parts[-1]
    ff = Ring(pack(after(up_weight, early), down_weight.T), dp)
    group = call(
        pack_weights,
        "pack_weights",
        [((shard, 4 * cols), BF)],
        (after(query_tangent, early), key_tangent, value_tangent, out_tangent),
    )
    tattn = Ring(group[0], dp)
    tff = Ring(pack(after(up_tangent, early), down_tangent.T), dp)
    attn.step()
    join([attn, ff])
    attn.step()
    ff.step()
    join([attn, ff])
    attn.step()
    where, attn.parts[-1] = join([ff], where, attn.parts[-1])
    ff.step()
    count = len(attn.parts)
    x_rel, mixed, probs, context, keep, send, attn_whole = call(
        functools.partial(attention_forward, count, cols),
        "attention_forward",
        [
            ((rows, width), BF),
            ((rows, 3 * cols), BF),
            ((2 * heads, SEQ, SEQ), F32),
            ((rows, cols), BF),
            *parts,
            attn_rows,
        ],
        (where, layer_input, params),
        attn.parts,
        [arriving(count)],
    )
    keep, send = join([ff], keep, send)
    ff.step()
    first, unit_one, inverse_one, first_low = call(
        first_norm,
        "first_norm",
        [full_own, full_own, ((own, 128), F32), ((own, width), BF)],
        (x_rel, *sum_exchange(keep, send, tp), params),
    )
    first_low = join([ff], first_low)
    ff.step()
    pieces = spread_rows(first_low, tp, [ff, tattn])
    tattn.step()
    first_rel, active, slope, keep, send, ff_whole = call(
        functools.partial(feed_forward, count, hidden),
        "feed_forward",
        [((rows, width), BF), ((rows, hidden), BF), ((rows, hidden), F32), *parts, ff_rows],
        (where, params, *pieces),
        ff.parts,
        [arriving(count)],
    )
    keep, send = join([tattn], keep, send)
    tattn.step()
    keep, first_came, second = sum_exchange(keep, send, tp)
    second = join([tattn], second)
    tattn.step()
    result, grad_two, grad_two_low, unit_two, inverse_two = call(
        second_norm,
        "second_norm",
        [((own, width), BF), full_own, piece, full_own, ((own, 128), F32)],
        (where, keep, first_came, second, params, first, out_grad),
    )
    grad_two_low = join([tff], grad_two_low)
    tff.step()
    pieces = spread_rows(grad_two_low, tp, [tattn])
    tattn.step()
    grad_down, grad_upper, sums_up, keep, send = call(
        functools.partial(feed_forward_backward, hidden),
        "feed_forward_backward",
        [((rows, width), BF), ((rows, hidden), BF), lines, *parts],
        (*pieces, slope, ff_whole),
    )
    result_pieces = spread_rows(result, tp)
    keep, send, grad_down, grad_upper, result_pieces[1] = join(
        [tff, tattn], keep, send, grad_down, grad_upper, result_pieces[1]
    )
    tff.step()

    def weight_outs(total, groups):
        if paired:
            counts = [4] + [len(group) for group in groups]
            return [((count, shard + EXTRA, total), BF) for count in counts]
        return [((width, total), BF)]

    def fold(steps, came, group):
        if not paired:
            return came
        total = came.shape[2]
        outs = []
        for z in group:
            if z == 0:
                outs = outs + [((shard, total), F32), ((EXTRA // 2, total), F32)]
            else:
                outs.append(((shard + EXTRA, total), BF))
        return call(functools.partial(fold_shards, group), "fold_shards", outs, (steps[0], came))

    flow = Flow()

    def x_swap(value):
        return lax.ppermute(value, "dp", xor_pairs(dp, 1)) if paired else value

    def z_moves(group):
        def move(values):
            if not paired:
                return values
            moved = [
                lax.ppermute(value, "dp", xor_pairs(dp, 2 * z)) for value, z in zip(values, group) if z
            ]
            return moved + values[len(moved) :]

        return move

    def add_shards(prefix, steps, groups):
        for index, group in enumerate(groups):
            key = prefix + str(index)
            source = steps[1 + index] if paired else steps[0]
            flow.add("x" + key, lambda source=source: source, (), x_swap)

            def folded(came, group=group):
                return fold(steps, came, group)

            flow.add("z" + key, folded, ("x" + key,), z_moves(group))

    def ring_step(values):
        tff.front = values
        tff.step()
        return tff.front

    flow.values["r1"] = tff.front
    for index in (2, 3):
        flow.add(f"r{index}", lambda front: front, (f"r{index - 1}",), ring_step)
    flow.add("a0", lambda: tsend, (), lambda value: swap(value, tp, 1))
    flow.add("a1", lambda came: onward_sum(tkeep, came), ("a0",), lambda value: swap(value, tp, 2))

    def norm_tangent(*_):
        return call(
            first_norm_tangent,
            "first_norm_tangent",
            [full_own, ((own, width), BF)],
            (tkeep, flow.values["a0"], flow.values["a1"], params, unit_one, inverse_one),
        )

    flow.add("n", norm_tangent, ("a1",), lambda values: values)

    first_came = swap(send, tp, 1)
    second = swap(onward_sum(keep, first_came), tp, 2)
    ff_steps = call(
        feed_forward_weights,
        "feed_forward_weights",
        weight_outs(2 * hidden, FF_GROUPS),
        (where, grad_down, active, first_rel, after(grad_upper, first_came), sums_up),
        (),
        [pltpu.VMEM((width, 2 * hidden), BF)],
    )
    add_shards("f", ff_steps, FF_GROUPS)
    flow.point("P0", ff_steps[0])
    tkeep, tsend = call(
        functools.partial(attention_tangent, count, cols),
        "attention_tangent",
        parts,
        (after(where, ff_steps[0]), x_rel, mixed, probs, context, attn_whole),
        tattn.parts,
        [pltpu.VMEM(*attn_rows), arriving(count)]
        + [pltpu.VMEM((rows, 3 * cols), BF), pltpu.VMEM((rows, cols), BF)],
    )
    second, tkeep, tsend, result_pieces = flow.point("P1", second, tkeep, tsend, result_pieces)
    grad_one, grad_one_low = call(
        first_norm_backward,
        "first_norm_backward",
        [full_own, piece],
        (keep, first_came, second, params, grad_two, unit_one, inverse_one),
    )
    grad_one_low = flow.point("P2", grad_one_low)
    across, beside = swap(grad_one_low, tp, 2), swap(grad_one_low, tp, 1)
    across = flow.point("P3", across)
    pieces = [grad_one_low, across, beside, swap(across, tp, 1)]
    pieces[3] = flow.point("P4", pieces[3])
    grad_attn, grad_mixed, sums_one, keep, send = call(
        functools.partial(attention_backward, cols),
        "attention_backward",
        [((rows, width), BF), ((rows, 3 * cols), BF), lines, *parts],
        (*pieces, mixed, probs, attn_whole),
        (),
        [pltpu.VMEM((rows, cols), BF)],
    )
    keep, send = flow.point("P5", keep, send)
    first_came = swap(send, tp, 1)
    last_steps = call(
        functools.partial(attention_weights, paired, cols),
        "attention_weights",
        weight_outs(4 * cols, LAST_GROUPS) + ([] if paired else [lines]),
        (where, grad_attn, grad_mixed, sums_one, x_rel, context),
        (),
        [pltpu.VMEM(*attn_rows)],
    )
    add_shards("l", last_steps, LAST_GROUPS)
    first_came = flow.point("P6", first_came)
    tfirst, tfirst_low = flow.value_of("n")
    flow.add("h0", lambda: tfirst_low, (), lambda value: [swap(value, tp, 2), swap(value, tp, 1)])
    flow.add("h1", lambda both: both[0], ("h0",), lambda value: swap(value, tp, 1))
    first_came = flow.point("P6b", first_came)
    second = swap(onward_sum(keep, first_came), tp, 2)
    second = flow.point("P7", second)
    (grad_input,) = call(
        last_sum, "last_sum", [((own, width), BF)], (keep, first_came, second, grad_one)
    )
    grad_input = flow.point("P8", grad_input)
    across, beside = swap(grad_input, tp, 2), swap(grad_input, tp, 1)
    tkeep, tsend = call(
        functools.partial(feed_forward_tangent, count, hidden),
        "feed_forward_tangent",
        parts,
        (where, tfirst_low, *flow.value_of("h0"), flow.value_of("h1"), first_rel, active, slope, ff_whole),
        tff.parts,
        [pltpu.VMEM(*tff_rows), arriving(count)]
        + [pltpu.VMEM((rows, width), BF), pltpu.VMEM((rows, hidden), BF)],
    )
    across, tkeep, tsend = flow.point("P9", across, tkeep, tsend)
    pieces = [grad_input, across, beside, swap(across, tp, 1)]
    tfirst_came = swap(tsend, tp, 1)
    tfirst_came = flow.point("P10", tfirst_came)
    tsecond = swap(onward_sum(tkeep, tfirst_came), tp, 2)
    tsecond = flow.point("P11", tsecond)
    (tresult,) = call(
        second_norm_tangent,
        "second_norm_tangent",
        [((own, width), BF)],
        (tkeep, tfirst_came, tsecond, params, tfirst, unit_two, inverse_two),
    )
    tresult = flow.point("P12", tresult)
    across, beside = swap(tresult, tp, 2), swap(tresult, tp, 1)
    across = flow.point("P13", across)
    tresult_pieces = [tresult, across, beside, swap(across, tp, 1)]

    def gathered(prefix, groups):
        found = {}
        for index, group in enumerate(groups):
            values = flow.value_of("z" + prefix + str(index))
            if not paired:
                return [values]
            at = 0
            for z in [z for z in group if z]:
                found[z], at = values[at], at + 1
            if 0 in group:
                found[0], found[4] = values[at], values[at + 1]
        return [found[i] for i in range(5)]

    ff_folded, last_folded = gathered("f", FF_GROUPS), gathered("l", LAST_GROUPS)

    def finish(body, name, outs, folded):
        return call(body, name, outs, folded)

    vector = ((width,), F32)
    if paired:
        own_down, own_up, *sums_two = finish(
            functools.partial(finish_feed_forward, hidden),
            "finish_feed_forward",
            [((shard, hidden), F32)] * 2 + [vector] * 4,
            ff_folded,
        )
        *own_mixed, own_out, bias_out, gain_one, shift_one, bias_query, bias_value = finish(
            functools.partial(finish_attention, cols),
            "finish_attention",
            [((shard, cols), F32)] * 3
            + [((cols, shard), F32)]
            + [vector] * 3
            + [((cols,), F32)] * 2,
            last_folded,
        )
        sums_one = [bias_out, gain_one, shift_one]
    else:

        def all_summed(step):
            split = step.reshape(dp, shard, -1)
            came = lax.all_to_all(split, "dp", 0, 0, tiled=True)
            return jnp.sum(came.astype(F32), axis=0)

        own_ff = all_summed(ff_folded[0])
        own_down, own_up = own_ff[:, :hidden], own_ff[:, hidden:]
        last = all_summed(last_folded[0])
        own_mixed = [last[:, i * cols : (i + 1) * cols] for i in range(3)]
        own_out = last[:, 3 * cols :].T
        sums_two = list(lax.psum(sums_up, "dp"))
        *sums_one, mixed_sums = list(lax.psum(last_steps[1], "dp"))
        bias_query, bias_value = mixed_sums[:cols], mixed_sums[2 * cols : 3 * cols]

    def all_rows(*spread):
        return call(
            functools.partial(place_rows, len(spread)),
            "place_rows",
            [((rows, width), BF)] * len(spread),
            (where, *[piece for pieces in spread for piece in pieces]),
            scratch=[arriving(4 * len(spread))],
            any_outs=True,
        )

    whole_result, whole_grad = all_rows(result_pieces, pieces)
    (whole_tresult,) = all_rows(tresult_pieces)
    return (
        whole_result,
        whole_grad,
        whole_tresult,
        own_mixed[0],
        bias_query,
        own_mixed[1],
        own_mixed[2],
        bias_value,
        own_out,
        *sums_one,
        own_up,
        sums_two[3],
        own_down.T,
        *sums_two[:3],
    )


def solution(mesh):
    wide, tall, col, row, full = P("dp", "tp"), P("tp", "dp"), P("tp"), P("dp", None), P()
    placed = (
        (row, P("dp"), wide, col, wide, wide, col, tall, full, full, full, wide, col, tall)
        + (full, full, full, row, wide, wide, wide, tall, wide, tall)
    )
    results = (row, row, row, wide, col, wide, wide, col, tall, full, full, full)
    results = results + (wide, col, tall, full, full, full)
    tp, dp = mesh.shape["tp"], mesh.shape["dp"]

    def body(*arrays):
        return per_device(tp, dp, *arrays)

    return jax.shard_map(
        body, mesh=mesh, in_specs=placed, out_specs=results, check_vma=False
    )
```

```python
import functools
import math

import jax
import jax.numpy as jnp
from jax import lax
from jax.experimental import pallas as pl
from jax.experimental.pallas import tpu as pltpu
from jax.sharding import PartitionSpec as P

HEAD = 64
SEQ = 256
EPSILON = 1e-06
SCALE = HEAD ** (-0.5)
BLOCKS = (0, 2, 1, 3)
FF_GROUPS = ((2,), (3,), (1,), (0,))
LAST_GROUPS = ((2, 3), (1, 0))
SNAKE = (0, 2, 4, 6, 7, 5, 3, 1)
EXTRA = 8
BF = jnp.bfloat16
F32 = jnp.float32
PLAN = {
    "xf0": ("P1", "P4"),
    "zf0": ("P4", "P7"),
    "xf1": ("P4", "P7"),
    "zf1": ("P6b", "P9"),
    "xf2": ("P2", "P7"),
    "zf2": ("P7", None),
    "xf3": ("P6b", "P12"),
    "zf3": ("P11", None),
    "xl0": ("P6", "P7"),
    "zl0": ("P7", "P12"),
    "xl1": ("P8", "P9"),
    "zl1": ("P10", "P12"),
    "r2": ("P1", "P5"),
    "r3": ("P5", None),
    "a0": ("P2", "P7"),
    "a1": ("P4", "P7"),
    "n": ("P6", None),
    "h0": ("P6b", "P12"),
    "h1": ("P7", "P13"),
    "_c": ("f", "l"),
}
VMEM_LIMIT = 16 * 1024 * 1024
TILE = 768

NN = ((1,), (0,))
NT = ((1,), (1,))
TN = ((0,), (0,))


def dot(left, right, dims):
    return lax.dot_general(left, right, (dims, ((), ())), preferred_element_type=F32)


def xor_pairs(size, bit):
    return [(i, i ^ bit) for i in range(size)]


def call(body, name, outs, near, shards=(), scratch=(), any_outs=False):
    smem = [a.dtype == jnp.int32 for a in near]
    specs = [pl.BlockSpec(memory_space=pltpu.SMEM if s else pltpu.VMEM) for s in smem]
    specs = specs + [pl.BlockSpec(memory_space=pl.ANY)] * len(shards)
    out_space = pltpu.HBM if any_outs else pltpu.VMEM
    return list(pl.pallas_call(
        body,
        out_shape=[jax.ShapeDtypeStruct(shape, kind) for shape, kind in outs],
        in_specs=specs,
        out_specs=[pl.BlockSpec(memory_space=out_space)] * len(outs),
        scratch_shapes=list(scratch),
        name=name,
        compiler_params=pltpu.CompilerParams(vmem_limit_bytes=VMEM_LIMIT),
        cost_estimate=pl.CostEstimate(flops=1, bytes_accessed=1, transcendentals=0),
    )(*near, *shards))


def tiles(width, body):
    step = TILE if width % TILE == 0 else width

    def one(i, carry):
        body(pl.ds(pl.multiple_of(i * step, step), step))
        return carry

    lax.fori_loop(0, width // step, one, 0)


def after(value, *others):
    return lax.optimization_barrier((value, *others))[0]


class Ring:
    def __init__(self, shard, dp):
        self.near = dp == len(SNAKE)
        self.dp = dp
        self.front = [shard, shard]
        self.parts = [shard]
        self.steps = 0

    def step(self):
        if not self.near:
            if self.steps == 0:
                self.parts = [lax.all_gather(self.parts[0], "dp", axis=0, tiled=True)]
                self.front = [self.parts[0]] * 2
            self.steps += 1
            return
        if self.steps == self.dp // 2:
            return
        ahead = [(SNAKE[i], SNAKE[(i + 1) % self.dp]) for i in range(self.dp)]
        behind = [(b, a) for a, b in ahead]
        self.steps += 1
        self.front[0] = lax.ppermute(self.front[0], "dp", ahead)
        self.parts.append(self.front[0])
        if self.steps < self.dp // 2:
            self.front[1] = lax.ppermute(self.front[1], "dp", behind)
            self.parts.append(self.front[1])


def join(rings, *values):
    fronts = [front for ring in rings for front in ring.front]
    joined = lax.optimization_barrier((*values, *fronts))
    for i, ring in enumerate(rings):
        ring.front = list(joined[len(values) + 2 * i :][:2])
    return joined[0] if len(values) == 1 else joined[: len(values)]


class Flow:
    def __init__(self):
        self.makers, self.values = {}, {}

    def add(self, name, maker, needs, send):
        self.makers[name] = (maker, needs, send)

    def value_of(self, name):
        return self.values[name]

    def point(self, name, *values):
        start = [key for key in PLAN if PLAN[key][0] == name and key in self.makers]
        due = [key for key in PLAN if PLAN[key][1] == name and key in self.values]
        inputs = {}
        for key in start:
            maker, needs, _ = self.makers[key]
            inputs[key] = maker(*[self.values[need] for need in needs])
        results = join_lists(*values, *[inputs[key] for key in start], *[self.values[key] for key in due])
        count = len(values)
        for key, value in zip(due, results[count + len(start) :]):
            self.values[key] = value
        for key, value in zip(start, results[count : count + len(start)]):
            self.values[key] = self.makers[key][2](value)
        return results[0] if count == 1 else results[:count]


def ring_owner(me, index):
    size = len(SNAKE)
    place = jnp.where(me % 2 == 0, me // 2, size - 1 - me // 2)
    step = (index + 1) // 2
    place = lax.rem(place + (size - step if index % 2 else step), size)
    return jnp.where(place < size // 2, 2 * place, 2 * (size - 1 - place) + 1)


def join_lists(*values):
    counts = [len(value) if isinstance(value, list) else 1 for value in values]
    flat = [v for value in values for v in (value if isinstance(value, list) else [value])]
    joined = list(lax.optimization_barrier(tuple(flat)))
    results = []
    for value, count in zip(values, counts):
        taken, joined = joined[:count], joined[count:]
        results.append(taken if isinstance(value, list) else taken[0])
    return results


def shard_copies(where, refs, whole, sems):
    rows = whole.shape[0] // len(refs)
    made = []
    for i, ref in enumerate(refs):
        owner = ring_owner(where[1], i) if len(refs) > 1 else 0
        start = pl.multiple_of(owner * rows, rows)
        made.append(pltpu.make_async_copy(ref, whole.at[pl.ds(start, rows), :], sems.at[i]))
    return made


def start_all(copies):
    for copy in copies:
        copy.start()


def wait_all(copies):
    for copy in copies:
        copy.wait()


def swap(block, tp, bit):
    return lax.ppermute(block, "tp", xor_pairs(tp, bit))


def onward_sum(keep, first):
    quarter = keep.shape[0] // 2
    return (keep[quarter:].astype(F32) + first[quarter:].astype(F32)).astype(BF)


def sum_exchange(keep, send, tp):
    first = swap(send, tp, 1)
    return keep, first, swap(onward_sum(keep, first), tp, 2)


def spread_rows(own, tp, rings=()):
    across, beside = swap(own, tp, 2), swap(own, tp, 1)
    if rings:
        across = join(rings, across)
    return [own, across, beside, swap(across, tp, 1)]


def summed(keep, first, second):
    quarter = second.shape[0]
    near = keep[0:quarter, :].astype(F32) + first[0:quarter, :].astype(F32)
    return near + second[...].astype(F32)


def halves(array, keep, send, cols=slice(None)):
    half = array.shape[0] // 2
    keep[:, cols] = array[:half].astype(BF)
    send[:, cols] = array[half:].astype(BF)


def mean_last(value):
    return jnp.mean(value, axis=-1, keepdims=True)


def norm_along(unit, inverse, along):
    shifted = along - mean_last(along)
    return inverse * (shifted - unit * mean_last(unit * shifted))


def sum_rows(value):
    return jnp.sum(value, axis=0, keepdims=True)


def split_sums(lines):
    width = lines[0].shape[-1]
    missing = EXTRA // 2 - sum(line.shape[0] for line in lines)
    blank = [jnp.zeros((missing, width), F32)] if missing else []
    whole = jnp.concatenate([*lines, *blank]) if len(lines) + missing > 1 else lines[0]
    rounded = whole.astype(BF).astype(F32)
    return jnp.concatenate([rounded, whole - rounded]).astype(BF)


def tree_sum(four):
    return (four[0] + four[1]) + (four[2] + four[3])


def joined_sums(block):
    return block[: EXTRA // 2].astype(F32) + block[EXTRA // 2 :].astype(F32)


def pair_rows(array, pair, quarter, cols):
    near, far = pair * quarter, (pair + 2) * quarter
    return jnp.concatenate([array[near : near + quarter, cols], array[far : far + quarter, cols]])


def put_pair(ref, pair, quarter, cols, value):
    near, far = pair * quarter, (pair + 2) * quarter
    ref[near : near + quarter, cols] = value[:quarter]
    ref[far : far + quarter, cols] = value[quarter:]


def positions(me, quarter):
    local = lax.broadcasted_iota(jnp.int32, (1, SEQ), 1)
    half = jnp.where(local < quarter, me % 2, 1 - me % 2)
    return half * quarter + lax.rem(local, quarter)


def attention_forward(count, cols, where, x_ref, params, *refs):
    shards, refs = refs[:count], refs[count:]
    rel, mixed, probs, context, keep, send, whole, sems = refs
    copies = shard_copies(where, shards, whole, sems)
    start_all(copies)
    me = where[0]
    quarter = x_ref.shape[0] // 4
    for i, block in enumerate(BLOCKS):
        start = pl.multiple_of((me ^ block) * quarter, quarter)
        rel[i * quarter : (i + 1) * quarter, :] = x_ref[pl.ds(start, quarter), :]
    wait_all(copies)
    for third in range(3):
        part = slice(third * cols, (third + 1) * cols)
        mixed[:, part] = (dot(rel[...], whole[:, part], NN) + params[0:1, part]).astype(BF)
    slots = positions(me, quarter)
    heads = cols // HEAD
    for pair in range(2):
        valid = slots < where[2 + ((me // 2) ^ pair)]
        for head in range(heads):
            query, key, value = [
                pair_rows(mixed, pair, quarter, slice(at, at + HEAD))
                for at in range(head * HEAD, 3 * cols, cols)
            ]
            scores = jnp.where(valid, dot(query, key, NT) * SCALE, jnp.float32(-1e30))
            expo = jnp.exp(scores - jnp.max(scores, axis=-1, keepdims=True))
            prob = expo / jnp.sum(expo, axis=-1, keepdims=True)
            probs[pair * heads + head] = prob
            result = dot(prob.astype(BF), value, NN).astype(BF)
            put_pair(context, pair, quarter, slice(head * HEAD, (head + 1) * HEAD), result)

    def project(cut):
        halves(dot(context[...], whole[cut, 3 * cols : 4 * cols], NT), keep, send, cut)

    tiles(keep.shape[1], project)


def attention_tangent(
    count, cols, where, rel, mixed, probs, context, whole, *refs
):
    tshards, refs = refs[:count], refs[count:]
    keep, send, twhole, sems, tmixed, tcontext = refs
    copies = shard_copies(where, tshards, twhole, sems)
    start_all(copies)
    wait_all(copies)
    me = where[0]
    quarter = rel.shape[0] // 4
    for third in range(3):
        part = slice(third * cols, (third + 1) * cols)
        tmixed[:, part] = dot(rel[...], twhole[:, part], NN).astype(BF)
    slots = positions(me, quarter)
    heads = cols // HEAD
    for pair in range(2):
        valid = slots < where[2 + ((me // 2) ^ pair)]
        for head in range(heads):
            columns = [slice(at, at + HEAD) for at in range(head * HEAD, 3 * cols, cols)]
            query, key, value = [pair_rows(mixed, pair, quarter, at) for at in columns]
            tquery, tkey, tvalue = [pair_rows(tmixed, pair, quarter, at) for at in columns]
            prob = probs[pair * heads + head]
            tscores = (dot(tquery, key, NT) + dot(query, tkey, NT)) * SCALE
            tscores = jnp.where(valid, tscores, jnp.float32(0.0))
            total = jnp.sum(tscores * prob, axis=-1, keepdims=True)
            tprob = (prob * (tscores - total)).astype(BF)
            result = dot(tprob, value, NN) + dot(prob.astype(BF), tvalue, NN)
            put_pair(
                tcontext, pair, quarter, slice(head * HEAD, (head + 1) * HEAD), result.astype(BF)
            )

    def project(cut):
        part = dot(tcontext[...], whole[cut, 3 * cols : 4 * cols], NT)
        part = part + dot(context[...], twhole[cut, 3 * cols : 4 * cols], NT)
        halves(part, keep, send, cut)

    tiles(keep.shape[1], project)


def first_norm(x_rel, keep, came, second, params, first, unit, inverse, low):
    own = second.shape[0]
    resid = x_rel[0:own, :].astype(F32) + summed(keep, came, second) + params[1:2, :]
    center = resid - mean_last(resid)
    inv = lax.rsqrt(mean_last(center * center) + EPSILON)
    whitened = center * inv
    unit[...] = whitened
    inverse[...] = jnp.broadcast_to(inv, inverse.shape)
    value = whitened * params[2:3, :] + params[3:4, :]
    first[...] = value
    low[...] = value.astype(BF)


def first_norm_tangent(keep, came, second, params, unit, inverse, tfirst, low):
    along = norm_along(unit[...], inverse[:, 0:1], summed(keep, came, second)) * params[2:3, :]
    tfirst[...] = along
    low[...] = along.astype(BF)


def pack_weights(*refs):
    at, out = 0, refs[-1]
    for ref in refs[:-2]:
        out[:, at : at + ref.shape[1]] = ref[...]
        at = at + ref.shape[1]
    out[:, at:] = refs[-2][...].astype(F32).T.astype(BF)


def collect(pieces, rel):
    quarter = rel.shape[0] // 4
    for i, piece in enumerate(pieces):
        rel[i * quarter : (i + 1) * quarter, :] = piece[0:quarter, :]


def feed_forward(count, hidden, where, params, *refs):
    pieces, refs = refs[:4], refs[4:]
    shards, refs = refs[:count], refs[count:]
    rel, active, slope, keep, send, whole, sems = refs
    copies = shard_copies(where, shards, whole, sems)
    start_all(copies)
    collect(pieces, rel)
    wait_all(copies)

    def up(cut):
        upper = dot(rel[...], whole[:, cut], NN) + params[4:5, cut]
        half = 0.5 + 0.5 * lax.erf(upper * (2.0 ** -0.5))
        active[:, cut] = (upper * half).astype(BF)
        bell = jnp.exp(-0.5 * upper * upper) * 0.3989422804014327
        slope[:, cut] = half + upper * bell

    tiles(hidden, up)

    def down(cut):
        halves(dot(active[...], whole[cut, hidden : 2 * hidden], NT), keep, send, cut)

    tiles(keep.shape[1], down)


def feed_forward_tangent(count, hidden, where, *refs):
    pieces, (rel, active, slope, whole), refs = refs[:4], refs[4:8], refs[8:]
    tshards, refs = refs[:count], refs[count:]
    keep, send, twhole, sems, trel, tactive = refs
    copies = shard_copies(where, tshards, twhole, sems)
    start_all(copies)
    collect(pieces, trel)
    wait_all(copies)

    def up(cut):
        tupper = dot(trel[...], whole[:, cut], NN) + dot(rel[...], twhole[:, cut], NN)
        tactive[:, cut] = (slope[:, cut] * tupper).astype(BF)

    tiles(hidden, up)

    def down(cut):
        part = dot(tactive[...], whole[cut, hidden : 2 * hidden], NT)
        part = part + dot(active[...], twhole[cut, hidden:], NT)
        halves(part, keep, send, cut)

    tiles(keep.shape[1], down)


def second_norm(
    where, keep, came, second, params, first, upstream,
    result, grad, low, unit, inverse,
):
    resid = first[...] + summed(keep, came, second) + params[5:6, :]
    center = resid - mean_last(resid)
    inv = lax.rsqrt(mean_last(center * center) + EPSILON)
    whitened = center * inv
    own = second.shape[0]
    unit[...] = whitened
    inverse[...] = jnp.broadcast_to(inv, inverse.shape)
    result[...] = (whitened * params[6:7, :] + params[7:8, :]).astype(BF)
    back = upstream[pl.ds(pl.multiple_of(where[0] * own, own), own), :].astype(F32)
    value = norm_along(whitened, inv, back * params[6:7, :])
    grad[...] = value
    low[0:own, :] = value.astype(BF)
    low[own:, :] = split_sums([sum_rows(value), sum_rows(back * whitened), sum_rows(back)])


def second_norm_tangent(keep, came, second, params, tfirst, unit, inverse, result):
    along = tfirst[...] + summed(keep, came, second)
    result[...] = (norm_along(unit[...], inverse[:, 0:1], along) * params[6:7, :]).astype(BF)


def first_norm_backward(
    keep, came, second, params, grad_two, unit, inverse, grad, low
):
    back = grad_two[...] + summed(keep, came, second)
    value = norm_along(unit[...], inverse[:, 0:1], back * params[2:3, :])
    own = second.shape[0]
    grad[...] = value
    low[0:own, :] = value.astype(BF)
    low[own:, :] = split_sums([sum_rows(value), sum_rows(back * unit[...]), sum_rows(back)])


def piece_sums(pieces):
    own = pieces[0].shape[0] - EXTRA
    return tree_sum([joined_sums(piece[own:, :]) for piece in pieces])


def feed_forward_backward(hidden, *refs):
    pieces, (slope, whole) = refs[:4], refs[4:6]
    rel, grad_upper, sums, keep, send = refs[6:]
    collect(pieces, rel)
    sums[...] = piece_sums(pieces)

    def down(cut):
        there = pl.ds(pl.multiple_of(cut.start + hidden, cut.size), cut.size)
        value = dot(rel[...], whole[:, there], NN) * slope[:, cut]
        sums[3:4, cut] = sum_rows(value)
        grad_upper[:, cut] = value.astype(BF)

    tiles(hidden, down)

    def up(cut):
        halves(dot(grad_upper[...], whole[cut, :hidden], NT), keep, send, cut)

    tiles(keep.shape[1], up)


def put_owned(groups, where, step, targets, sums):
    if len(targets) == 1:
        targets[0][...] = step[...]
        return
    rows = step.shape[0] // 8
    spare = step.shape[1] - sums.shape[1]
    if spare:
        sums = jnp.concatenate([sums, jnp.zeros((EXTRA // 2, spare), F32)], axis=1)
    extra = split_sums([sums])

    def put(target, at, owner):
        start = pl.multiple_of((where[1] ^ owner) * rows, rows)
        target[at, 0:rows, :] = step[pl.ds(start, rows), :]
        target[at, rows:, :] = extra

    for z in range(4):
        put(targets[0], z, 2 * z)
    for target, group in zip(targets[1:], groups):
        for at, z in enumerate(group):
            put(target, at, 2 * z + 1)


def feed_forward_weights(where, rel, active, first, grad_upper, sums, *refs):
    targets, step = refs[:-1], refs[-1]
    hidden = active.shape[1]

    def one(cut):
        step[cut, :hidden] = dot(rel[:, cut], active[...], TN).astype(BF)
        step[cut, hidden:] = dot(first[:, cut], grad_upper[...], TN).astype(BF)

    tiles(rel.shape[1], one)
    put_owned(FF_GROUPS, where, step, targets, sums[...])


def attention_backward(cols, *refs):
    pieces, (mixed, probs, whole) = refs[:4], refs[4:7]
    rel, grad, sums, keep, send, back = refs[7:]
    collect(pieces, rel)
    sums[...] = piece_sums(pieces)
    quarter = rel.shape[0] // 4
    back[...] = dot(rel[...], whole[:, 3 * cols : 4 * cols], NN).astype(BF)
    heads = cols // HEAD
    for pair in range(2):
        for head in range(heads):
            columns = [slice(at, at + HEAD) for at in range(head * HEAD, 3 * cols, cols)]
            query, key, value = [pair_rows(mixed, pair, quarter, at) for at in columns]
            prob = probs[pair * heads + head]
            grad_context = pair_rows(back, pair, quarter, columns[0])
            grad_value = dot(prob.astype(BF), grad_context, TN)
            grad_prob = dot(grad_context, value, NT)
            total = jnp.sum(grad_prob * prob, axis=-1, keepdims=True)
            grad_score = (prob * (grad_prob - total)).astype(BF)
            put_pair(grad, pair, quarter, columns[2], grad_value.astype(BF))
            grad_query = dot(grad_score, key, NN) * SCALE
            put_pair(grad, pair, quarter, columns[0], grad_query.astype(BF))
            grad_key = dot(grad_score, query, TN) * SCALE
            put_pair(grad, pair, quarter, columns[1], grad_key.astype(BF))

    def project(cut):
        halves(dot(grad[...], whole[cut, : 3 * cols], NT), keep, send, cut)

    tiles(keep.shape[1], project)


def attention_weights(paired, cols, where, rel, grad, sums, x_rel, context, *refs):
    count = 1 + len(LAST_GROUPS) if paired else 1
    targets, refs = refs[:count], refs[count:]
    (step,) = refs[-1:]

    def one(cut):
        step[cut, : 3 * cols] = dot(x_rel[:, cut], grad[...], TN).astype(BF)
        step[cut, 3 * cols :] = dot(rel[:, cut], context[...], TN).astype(BF)

    tiles(x_rel.shape[1], one)
    mixed = sum_rows(grad[...].astype(F32))
    mixed = jnp.concatenate([mixed, jnp.zeros((1, cols), F32)], axis=1)
    lines = jnp.concatenate([sums[0:3, :], mixed])
    put_owned(LAST_GROUPS, where, step, targets, lines)
    if not paired:
        refs[0][...] = lines


def fold_shards(group, keep, came, *outs):
    outs = list(outs)
    for at, z in enumerate(group):
        out = outs.pop(0)
        rows = keep.shape[1] - EXTRA
        total = keep[z, 0:rows, :].astype(F32) + came[at, 0:rows, :].astype(F32)
        sums = joined_sums(keep[z, rows:, :]) + joined_sums(came[at, rows:, :])
        rounded = split_sums([sums])
        if z == 0:
            out[...] = total
            outs.pop(0)[...] = joined_sums(rounded)
        else:
            out[0:rows, :] = total.astype(BF)
            out[rows:, :] = rounded


def last_total(refs):
    rows = refs[0].shape[0]
    total = refs[0][...]
    for ref in refs[1:4]:
        total = total + ref[0:rows, :].astype(F32)
    return total


def last_sums(refs, outs, places):
    rows = refs[0].shape[0]
    sums = tree_sum([refs[4][...]] + [joined_sums(ref[rows:, :]) for ref in refs[1:4]])
    for out, (line, start) in zip(outs, places):
        out[...] = sums[line, start : start + out.shape[0]]


def finish_feed_forward(hidden, *refs):
    total = last_total(refs)
    refs[5][...] = total[:, :hidden]
    refs[6][...] = total[:, hidden:]
    last_sums(refs, refs[7:], [(i, 0) for i in range(4)])


def finish_attention(cols, *refs):
    total = last_total(refs)
    for i in range(3):
        refs[5 + i][...] = total[:, i * cols : (i + 1) * cols]
    refs[8][...] = total[:, 3 * cols :].T
    last_sums(refs, refs[9:], [(0, 0), (1, 0), (2, 0), (3, 0), (3, 2 * cols)])


def last_sum(keep, came, second, grad_one, out):
    out[...] = (grad_one[...] + summed(keep, came, second)).astype(BF)


def place_rows(count, where, *refs):
    pieces, outs, sems = refs[: 4 * count], refs[4 * count : 5 * count], refs[5 * count]
    own = pieces[0].shape[0]
    copies = []
    for i, out in enumerate(outs):
        for j, block in enumerate(BLOCKS):
            start = pl.multiple_of((where[0] ^ block) * own, own)
            copies.append(
                pltpu.make_async_copy(
                    pieces[4 * i + j], out.at[pl.ds(start, own), :], sems.at[4 * i + j]
                )
            )
    start_all(copies)
    wait_all(copies)


def per_device(tp, dp, *arrays):
    (
        layer_input,
        pair_lengths,
        query_weight,
        query_bias,
        key_weight,
        value_weight,
        value_bias,
        out_weight,
        out_bias,
        first_gain,
        first_shift,
        up_weight,
        up_bias,
        down_weight,
        down_bias,
        second_gain,
        second_shift,
        out_grad,
        query_tangent,
        key_tangent,
        value_tangent,
        out_tangent,
        up_tangent,
        down_tangent,
    ) = arrays
    rows, width = layer_input.shape
    cols = query_weight.shape[1]
    hidden = up_weight.shape[1]
    heads = cols // HEAD
    own = rows // tp
    half = rows // 2
    shard = width // dp
    paired = dp == len(SNAKE)

    place = jnp.stack([lax.axis_index("tp"), lax.axis_index("dp")]).astype(jnp.int32)
    where = jnp.concatenate([place, pair_lengths])
    zeros = jnp.zeros((cols,), F32)
    params = jnp.concatenate(
        [query_bias, zeros, value_bias, zeros, out_bias, first_gain, first_shift]
        + [up_bias, down_bias, second_gain, second_shift]
    ).reshape(8, width)
    parts = [((half, width), BF), ((half, width), BF)]
    piece = ((own + EXTRA, width), BF)
    lines = ((EXTRA // 2, width), F32)
    full_own = ((own, width), F32)
    attn_rows = ((width, 4 * cols), BF)
    ff_rows = ((width, 2 * hidden), BF)
    tff_rows = ff_rows

    def pack(first_one, *blocks):
        return jnp.concatenate([first_one, *blocks], 1)

    def arriving(count):
        return pltpu.SemaphoreType.DMA((count,))

    where, out_rows = join((), where, out_weight.T)
    attn = Ring(pack(query_weight, key_weight, value_weight, out_rows), dp)
    attn.step()
    early = attn.parts[-1]
    ff = Ring(pack(after(up_weight, early), down_weight.T), dp)
    group = call(
        pack_weights,
        "pack_weights",
        [((shard, 4 * cols), BF)],
        (after(query_tangent, early), key_tangent, value_tangent, out_tangent),
    )
    tattn = Ring(group[0], dp)
    tff = Ring(pack(after(up_tangent, early), down_tangent.T), dp)
    attn.step()
    join([attn, ff])
    attn.step()
    ff.step()
    join([attn, ff])
    attn.step()
    where, attn.parts[-1] = join([ff], where, attn.parts[-1])
    ff.step()
    count = len(attn.parts)
    x_rel, mixed, probs, context, keep, send, attn_whole = call(
        functools.partial(attention_forward, count, cols),
        "attention_forward",
        [
            ((rows, width), BF),
            ((rows, 3 * cols), BF),
            ((2 * heads, SEQ, SEQ), F32),
            ((rows, cols), BF),
            *parts,
            attn_rows,
        ],
        (where, layer_input, params),
        attn.parts,
        [arriving(count)],
    )
    keep, send = join([ff], keep, send)
    ff.step()
    first, unit_one, inverse_one, first_low = call(
        first_norm,
        "first_norm",
        [full_own, full_own, ((own, 128), F32), ((own, width), BF)],
        (x_rel, *sum_exchange(keep, send, tp), params),
    )
    first_low = join([ff], first_low)
    ff.step()
    pieces = spread_rows(first_low, tp, [ff, tattn])
    tattn.step()
    first_rel, active, slope, keep, send, ff_whole = call(
        functools.partial(feed_forward, count, hidden),
        "feed_forward",
        [((rows, width), BF), ((rows, hidden), BF), ((rows, hidden), F32), *parts, ff_rows],
        (where, params, *pieces),
        ff.parts,
        [arriving(count)],
    )
    keep, send = join([tattn], keep, send)
    tattn.step()
    keep, first_came, second = sum_exchange(keep, send, tp)
    second = join([tattn], second)
    tattn.step()
    result, grad_two, grad_two_low, unit_two, inverse_two = call(
        second_norm,
        "second_norm",
        [((own, width), BF), full_own, piece, full_own, ((own, 128), F32)],
        (where, keep, first_came, second, params, first, out_grad),
    )
    grad_two_low = join([tff], grad_two_low)
    tff.step()
    pieces = spread_rows(grad_two_low, tp, [tattn])
    tattn.step()
    grad_down, grad_upper, sums_up, keep, send = call(
        functools.partial(feed_forward_backward, hidden),
        "feed_forward_backward",
        [((rows, width), BF), ((rows, hidden), BF), lines, *parts],
        (*pieces, slope, ff_whole),
    )
    result_pieces = spread_rows(result, tp)
    keep, send, grad_down, grad_upper, result_pieces[1] = join(
        [tff, tattn], keep, send, grad_down, grad_upper, result_pieces[1]
    )
    tff.step()

    def weight_outs(total, groups):
        if paired:
            counts = [4] + [len(group) for group in groups]
            return [((count, shard + EXTRA, total), BF) for count in counts]
        return [((width, total), BF)]

    def fold(steps, came, group):
        if not paired:
            return came
        total = came.shape[2]
        outs = []
        for z in group:
            if z == 0:
                outs = outs + [((shard, total), F32), ((EXTRA // 2, total), F32)]
            else:
                outs.append(((shard + EXTRA, total), BF))
        return call(functools.partial(fold_shards, group), "fold_shards", outs, (steps[0], came))

    flow = Flow()

    def x_swap(value):
        return lax.ppermute(value, "dp", xor_pairs(dp, 1)) if paired else value

    def z_moves(group):
        def move(values):
            if not paired:
                return values
            moved = [
                lax.ppermute(value, "dp", xor_pairs(dp, 2 * z)) for value, z in zip(values, group) if z
            ]
            return moved + values[len(moved) :]

        return move

    def add_shards(prefix, steps, groups):
        for index, group in enumerate(groups):
            key = prefix + str(index)
            source = steps[1 + index] if paired else steps[0]
            flow.add("x" + key, lambda source=source: source, (), x_swap)

            def folded(came, group=group):
                return fold(steps, came, group)

            flow.add("z" + key, folded, ("x" + key,), z_moves(group))

    def ring_step(values):
        tff.front = values
        tff.step()
        return tff.front

    flow.values["r1"] = tff.front
    for index in (2, 3):
        flow.add(f"r{index}", lambda front: front, (f"r{index - 1}",), ring_step)
    flow.add("a0", lambda: tsend, (), lambda value: swap(value, tp, 1))
    flow.add("a1", lambda came: onward_sum(tkeep, came), ("a0",), lambda value: swap(value, tp, 2))

    def norm_tangent(*_):
        return call(
            first_norm_tangent,
            "first_norm_tangent",
            [full_own, ((own, width), BF)],
            (tkeep, flow.values["a0"], flow.values["a1"], params, unit_one, inverse_one),
        )

    flow.add("n", norm_tangent, ("a1",), lambda values: values)

    first_came = swap(send, tp, 1)
    second = swap(onward_sum(keep, first_came), tp, 2)
    ff_steps = call(
        feed_forward_weights,
        "feed_forward_weights",
        weight_outs(2 * hidden, FF_GROUPS),
        (where, grad_down, active, first_rel, after(grad_upper, first_came), sums_up),
        (),
        [pltpu.VMEM((width, 2 * hidden), BF)],
    )
    add_shards("f", ff_steps, FF_GROUPS)
    flow.point("P0", ff_steps[0])
    tkeep, tsend = call(
        functools.partial(attention_tangent, count, cols),
        "attention_tangent",
        parts,
        (after(where, ff_steps[0]), x_rel, mixed, probs, context, attn_whole),
        tattn.parts,
        [pltpu.VMEM(*attn_rows), arriving(count)]
        + [pltpu.VMEM((rows, 3 * cols), BF), pltpu.VMEM((rows, cols), BF)],
    )
    second, tkeep, tsend, result_pieces = flow.point("P1", second, tkeep, tsend, result_pieces)
    grad_one, grad_one_low = call(
        first_norm_backward,
        "first_norm_backward",
        [full_own, piece],
        (keep, first_came, second, params, grad_two, unit_one, inverse_one),
    )
    grad_one_low = flow.point("P2", grad_one_low)
    across, beside = swap(grad_one_low, tp, 2), swap(grad_one_low, tp, 1)
    across = flow.point("P3", across)
    pieces = [grad_one_low, across, beside, swap(across, tp, 1)]
    pieces[3] = flow.point("P4", pieces[3])
    grad_attn, grad_mixed, sums_one, keep, send = call(
        functools.partial(attention_backward, cols),
        "attention_backward",
        [((rows, width), BF), ((rows, 3 * cols), BF), lines, *parts],
        (*pieces, mixed, probs, attn_whole),
        (),
        [pltpu.VMEM((rows, cols), BF)],
    )
    keep, send = flow.point("P5", keep, send)
    first_came = swap(send, tp, 1)
    last_steps = call(
        functools.partial(attention_weights, paired, cols),
        "attention_weights",
        weight_outs(4 * cols, LAST_GROUPS) + ([] if paired else [lines]),
        (where, grad_attn, grad_mixed, sums_one, x_rel, context),
        (),
        [pltpu.VMEM(*attn_rows)],
    )
    add_shards("l", last_steps, LAST_GROUPS)
    first_came = flow.point("P6", first_came)
    tfirst, tfirst_low = flow.value_of("n")
    flow.add("h0", lambda: tfirst_low, (), lambda value: [swap(value, tp, 2), swap(value, tp, 1)])
    flow.add("h1", lambda both: both[0], ("h0",), lambda value: swap(value, tp, 1))
    first_came = flow.point("P6b", first_came)
    second = swap(onward_sum(keep, first_came), tp, 2)
    second = flow.point("P7", second)
    (grad_input,) = call(
        last_sum, "last_sum", [((own, width), BF)], (keep, first_came, second, grad_one)
    )
    grad_input = flow.point("P8", grad_input)
    across, beside = swap(grad_input, tp, 2), swap(grad_input, tp, 1)
    tkeep, tsend = call(
        functools.partial(feed_forward_tangent, count, hidden),
        "feed_forward_tangent",
        parts,
        (where, tfirst_low, *flow.value_of("h0"), flow.value_of("h1"), first_rel, active, slope, ff_whole),
        tff.parts,
        [pltpu.VMEM(*tff_rows), arriving(count)]
        + [pltpu.VMEM((rows, width), BF), pltpu.VMEM((rows, hidden), BF)],
    )
    across, tkeep, tsend = flow.point("P9", across, tkeep, tsend)
    pieces = [grad_input, across, beside, swap(across, tp, 1)]
    tfirst_came = swap(tsend, tp, 1)
    tfirst_came = flow.point("P10", tfirst_came)
    tsecond = swap(onward_sum(tkeep, tfirst_came), tp, 2)
    tsecond = flow.point("P11", tsecond)
    (tresult,) = call(
        second_norm_tangent,
        "second_norm_tangent",
        [((own, width), BF)],
        (tkeep, tfirst_came, tsecond, params, tfirst, unit_two, inverse_two),
    )
    tresult = flow.point("P12", tresult)
    across, beside = swap(tresult, tp, 2), swap(tresult, tp, 1)
    across = flow.point("P13", across)
    tresult_pieces = [tresult, across, beside, swap(across, tp, 1)]

    def gathered(prefix, groups):
        found = {}
        for index, group in enumerate(groups):
            values = flow.value_of("z" + prefix + str(index))
            if not paired:
                return [values]
            at = 0
            for z in [z for z in group if z]:
                found[z], at = values[at], at + 1
            if 0 in group:
                found[0], found[4] = values[at], values[at + 1]
        return [found[i] for i in range(5)]

    ff_folded, last_folded = gathered("f", FF_GROUPS), gathered("l", LAST_GROUPS)

    def finish(body, name, outs, folded):
        return call(body, name, outs, folded)

    vector = ((width,), F32)
    if paired:
        own_down, own_up, *sums_two = finish(
            functools.partial(finish_feed_forward, hidden),
            "finish_feed_forward",
            [((shard, hidden), F32)] * 2 + [vector] * 4,
            ff_folded,
        )
        *own_mixed, own_out, bias_out, gain_one, shift_one, bias_query, bias_value = finish(
            functools.partial(finish_attention, cols),
            "finish_attention",
            [((shard, cols), F32)] * 3
            + [((cols, shard), F32)]
            + [vector] * 3
            + [((cols,), F32)] * 2,
            last_folded,
        )
        sums_one = [bias_out, gain_one, shift_one]
    else:

        def all_summed(step):
            split = step.reshape(dp, shard, -1)
            came = lax.all_to_all(split, "dp", 0, 0, tiled=True)
            return jnp.sum(came.astype(F32), axis=0)

        own_ff = all_summed(ff_folded[0])
        own_down, own_up = own_ff[:, :hidden], own_ff[:, hidden:]
        last = all_summed(last_folded[0])
        own_mixed = [last[:, i * cols : (i + 1) * cols] for i in range(3)]
        own_out = last[:, 3 * cols :].T
        sums_two = list(lax.psum(sums_up, "dp"))
        *sums_one, mixed_sums = list(lax.psum(last_steps[1], "dp"))
        bias_query, bias_value = mixed_sums[:cols], mixed_sums[2 * cols : 3 * cols]

    def all_rows(*spread):
        return call(
            functools.partial(place_rows, len(spread)),
            "place_rows",
            [((rows, width), BF)] * len(spread),
            (where, *[piece for pieces in spread for piece in pieces]),
            scratch=[arriving(4 * len(spread))],
            any_outs=True,
        )

    whole_result, whole_grad = all_rows(result_pieces, pieces)
    (whole_tresult,) = all_rows(tresult_pieces)
    return (
        whole_result,
        whole_grad,
        whole_tresult,
        own_mixed[0],
        bias_query,
        own_mixed[1],
        own_mixed[2],
        bias_value,
        own_out,
        *sums_one,
        own_up,
        sums_two[3],
        own_down.T,
        *sums_two[:3],
    )


def solution(mesh):
    wide, tall, col, row, full = P("dp", "tp"), P("tp", "dp"), P("tp"), P("dp", None), P()
    placed = (
        (row, P("dp"), wide, col, wide, wide, col, tall, full, full, full, wide, col, tall)
        + (full, full, full, row, wide, wide, wide, tall, wide, tall)
    )
    results = (row, row, row, wide, col, wide, wide, col, tall, full, full, full)
    results = results + (wide, col, tall, full, full, full)
    tp, dp = mesh.shape["tp"], mesh.shape["dp"]

    def body(*arrays):
        return per_device(tp, dp, *arrays)

    return jax.shard_map(
        body, mesh=mesh, in_specs=placed, out_specs=results, check_vma=False
    )
```

```python
import functools
import math

import jax
import jax.numpy as jnp
from jax import lax
from jax.experimental import pallas as pl
from jax.experimental.pallas import tpu as pltpu
from jax.sharding import PartitionSpec as P

HEAD = 64
SEQ = 256
EPSILON = 1e-06
SCALE = HEAD ** (-0.5)
BLOCKS = (0, 2, 1, 3)
FF_GROUPS = ((2,), (3,), (1,), (0,))
LAST_GROUPS = ((2, 3), (1, 0))
SNAKE = (0, 2, 4, 6, 7, 5, 3, 1)
EXTRA = 8
BF = jnp.bfloat16
F32 = jnp.float32
PLAN = {
    "xf0": ("P1", "P4"),
    "zf0": ("P4", "P7"),
    "xf1": ("P4", "P7"),
    "zf1": ("P6b", "P9"),
    "xf2": ("P2", "P7"),
    "zf2": ("P7", None),
    "xf3": ("P6b", "P12"),
    "zf3": ("P11", None),
    "xl0": ("P6", "P7"),
    "zl0": ("P7", "P12"),
    "xl1": ("P8", "P9"),
    "zl1": ("P10", "P12"),
    "r2": ("P1", "P5"),
    "r3": ("P5", None),
    "a0": ("P2", "P7"),
    "a1": ("P4", "P7"),
    "n": ("P6", None),
    "h0": ("P6b", "P12"),
    "h1": ("P7", "P13"),
    "_c": ("f", "l"),
}
VMEM_LIMIT = 16 * 1024 * 1024
TILE = 768

NN = ((1,), (0,))
NT = ((1,), (1,))
TN = ((0,), (0,))


def dot(left, right, dims):
    return lax.dot_general(left, right, (dims, ((), ())), preferred_element_type=F32)


def xor_pairs(size, bit):
    return [(i, i ^ bit) for i in range(size)]


def call(body, name, outs, near, shards=(), scratch=(), any_outs=False):
    smem = [a.dtype == jnp.int32 for a in near]
    specs = [pl.BlockSpec(memory_space=pltpu.SMEM if s else pltpu.VMEM) for s in smem]
    specs = specs + [pl.BlockSpec(memory_space=pl.ANY)] * len(shards)
    out_space = pltpu.HBM if any_outs else pltpu.VMEM
    return list(pl.pallas_call(
        body,
        out_shape=[jax.ShapeDtypeStruct(shape, kind) for shape, kind in outs],
        in_specs=specs,
        out_specs=[pl.BlockSpec(memory_space=out_space)] * len(outs),
        scratch_shapes=list(scratch),
        name=name,
        compiler_params=pltpu.CompilerParams(vmem_limit_bytes=VMEM_LIMIT),
        cost_estimate=pl.CostEstimate(flops=1, bytes_accessed=1, transcendentals=0),
    )(*near, *shards))


def tiles(width, body):
    step = TILE if width % TILE == 0 else width

    def one(i, carry):
        body(pl.ds(pl.multiple_of(i * step, step), step))
        return carry

    lax.fori_loop(0, width // step, one, 0)


def after(value, *others):
    return lax.optimization_barrier((value, *others))[0]


class Ring:
    def __init__(self, shard, dp):
        self.near = dp == len(SNAKE)
        self.dp = dp
        self.front = [shard, shard]
        self.parts = [shard]
        self.steps = 0

    def step(self):
        if not self.near:
            if self.steps == 0:
                self.parts = [lax.all_gather(self.parts[0], "dp", axis=0, tiled=True)]
                self.front = [self.parts[0]] * 2
            self.steps += 1
            return
        if self.steps == self.dp // 2:
            return
        ahead = [(SNAKE[i], SNAKE[(i + 1) % self.dp]) for i in range(self.dp)]
        behind = [(b, a) for a, b in ahead]
        self.steps += 1
        self.front[0] = lax.ppermute(self.front[0], "dp", ahead)
        self.parts.append(self.front[0])
        if self.steps < self.dp // 2:
            self.front[1] = lax.ppermute(self.front[1], "dp", behind)
            self.parts.append(self.front[1])


def join(rings, *values):
    fronts = [front for ring in rings for front in ring.front]
    joined = lax.optimization_barrier((*values, *fronts))
    for i, ring in enumerate(rings):
        ring.front = list(joined[len(values) + 2 * i :][:2])
    return joined[0] if len(values) == 1 else joined[: len(values)]


class Flow:
    def __init__(self):
        self.makers, self.values = {}, {}

    def add(self, name, maker, needs, send):
        self.makers[name] = (maker, needs, send)

    def value_of(self, name):
        return self.values[name]

    def point(self, name, *values):
        start = [key for key in PLAN if PLAN[key][0] == name and key in self.makers]
        due = [key for key in PLAN if PLAN[key][1] == name and key in self.values]
        inputs = {}
        for key in start:
            maker, needs, _ = self.makers[key]
            inputs[key] = maker(*[self.values[need] for need in needs])
        results = join_lists(*values, *[inputs[key] for key in start], *[self.values[key] for key in due])
        count = len(values)
        for key, value in zip(due, results[count + len(start) :]):
            self.values[key] = value
        for key, value in zip(start, results[count : count + len(start)]):
            self.values[key] = self.makers[key][2](value)
        return results[0] if count == 1 else results[:count]


def ring_owner(me, index):
    size = len(SNAKE)
    place = jnp.where(me % 2 == 0, me // 2, size - 1 - me // 2)
    step = (index + 1) // 2
    place = lax.rem(place + (size - step if index % 2 else step), size)
    return jnp.where(place < size // 2, 2 * place, 2 * (size - 1 - place) + 1)


def join_lists(*values):
    counts = [len(value) if isinstance(value, list) else 1 for value in values]
    flat = [v for value in values for v in (value if isinstance(value, list) else [value])]
    joined = list(lax.optimization_barrier(tuple(flat)))
    results = []
    for value, count in zip(values, counts):
        taken, joined = joined[:count], joined[count:]
        results.append(taken if isinstance(value, list) else taken[0])
    return results


def shard_copies(where, refs, whole, sems):
    rows = whole.shape[0] // len(refs)
    made = []
    for i, ref in enumerate(refs):
        owner = ring_owner(where[1], i) if len(refs) > 1 else 0
        start = pl.multiple_of(owner * rows, rows)
        made.append(pltpu.make_async_copy(ref, whole.at[pl.ds(start, rows), :], sems.at[i]))
    return made


def start_all(copies):
    for copy in copies:
        copy.start()


def wait_all(copies):
    for copy in copies:
        copy.wait()


def swap(block, tp, bit):
    return lax.ppermute(block, "tp", xor_pairs(tp, bit))


def onward_sum(keep, first):
    quarter = keep.shape[0] // 2
    return (keep[quarter:].astype(F32) + first[quarter:].astype(F32)).astype(BF)


def sum_exchange(keep, send, tp):
    first = swap(send, tp, 1)
    return keep, first, swap(onward_sum(keep, first), tp, 2)


def spread_rows(own, tp, rings=()):
    across, beside = swap(own, tp, 2), swap(own, tp, 1)
    if rings:
        across = join(rings, across)
    return [own, across, beside, swap(across, tp, 1)]


def summed(keep, first, second):
    quarter = second.shape[0]
    near = keep[0:quarter, :].astype(F32) + first[0:quarter, :].astype(F32)
    return near + second[...].astype(F32)


def halves(array, keep, send, cols=slice(None)):
    half = array.shape[0] // 2
    keep[:, cols] = array[:half].astype(BF)
    send[:, cols] = array[half:].astype(BF)


def mean_last(value):
    return jnp.mean(value, axis=-1, keepdims=True)


def norm_along(unit, inverse, along):
    shifted = along - mean_last(along)
    return inverse * (shifted - unit * mean_last(unit * shifted))


def sum_rows(value):
    return jnp.sum(value, axis=0, keepdims=True)


def split_sums(lines):
    width = lines[0].shape[-1]
    missing = EXTRA // 2 - sum(line.shape[0] for line in lines)
    blank = [jnp.zeros((missing, width), F32)] if missing else []
    whole = jnp.concatenate([*lines, *blank]) if len(lines) + missing > 1 else lines[0]
    rounded = whole.astype(BF).astype(F32)
    return jnp.concatenate([rounded, whole - rounded]).astype(BF)


def tree_sum(four):
    return (four[0] + four[1]) + (four[2] + four[3])


def joined_sums(block):
    return block[: EXTRA // 2].astype(F32) + block[EXTRA // 2 :].astype(F32)


def pair_rows(array, pair, quarter, cols):
    near, far = pair * quarter, (pair + 2) * quarter
    return jnp.concatenate([array[near : near + quarter, cols], array[far : far + quarter, cols]])


def put_pair(ref, pair, quarter, cols, value):
    near, far = pair * quarter, (pair + 2) * quarter
    ref[near : near + quarter, cols] = value[:quarter]
    ref[far : far + quarter, cols] = value[quarter:]


def positions(me, quarter):
    local = lax.broadcasted_iota(jnp.int32, (1, SEQ), 1)
    half = jnp.where(local < quarter, me % 2, 1 - me % 2)
    return half * quarter + lax.rem(local, quarter)


def attention_forward(count, cols, where, x_ref, params, *refs):
    shards, refs = refs[:count], refs[count:]
    rel, mixed, probs, context, keep, send, whole, sems = refs
    copies = shard_copies(where, shards, whole, sems)
    start_all(copies)
    me = where[0]
    quarter = x_ref.shape[0] // 4
    for i, block in enumerate(BLOCKS):
        start = pl.multiple_of((me ^ block) * quarter, quarter)
        rel[i * quarter : (i + 1) * quarter, :] = x_ref[pl.ds(start, quarter), :]
    wait_all(copies)
    for third in range(3):
        part = slice(third * cols, (third + 1) * cols)
        mixed[:, part] = (dot(rel[...], whole[:, part], NN) + params[0:1, part]).astype(BF)
    slots = positions(me, quarter)
    heads = cols // HEAD
    for pair in range(2):
        valid = slots < where[2 + ((me // 2) ^ pair)]
        for head in range(heads):
            query, key, value = [
                pair_rows(mixed, pair, quarter, slice(at, at + HEAD))
                for at in range(head * HEAD, 3 * cols, cols)
            ]
            scores = jnp.where(valid, dot(query, key, NT) * SCALE, jnp.float32(-1e30))
            expo = jnp.exp(scores - jnp.max(scores, axis=-1, keepdims=True))
            prob = expo * (1.0 / jnp.sum(expo, axis=-1, keepdims=True))
            probs[pair * heads + head] = prob
            result = dot(prob.astype(BF), value, NN).astype(BF)
            put_pair(context, pair, quarter, slice(head * HEAD, (head + 1) * HEAD), result)

    def project(cut):
        halves(dot(context[...], whole[cut, 3 * cols : 4 * cols], NT), keep, send, cut)

    tiles(keep.shape[1], project)


def attention_tangent(
    count, cols, where, rel, mixed, probs, context, whole, *refs
):
    tshards, refs = refs[:count], refs[count:]
    keep, send, twhole, sems, tmixed, tcontext = refs
    copies = shard_copies(where, tshards, twhole, sems)
    start_all(copies)
    wait_all(copies)
    me = where[0]
    quarter = rel.shape[0] // 4
    for third in range(3):
        part = slice(third * cols, (third + 1) * cols)
        tmixed[:, part] = dot(rel[...], twhole[:, part], NN).astype(BF)
    slots = positions(me, quarter)
    heads = cols // HEAD
    for pair in range(2):
        valid = slots < where[2 + ((me // 2) ^ pair)]
        for head in range(heads):
            columns = [slice(at, at + HEAD) for at in range(head * HEAD, 3 * cols, cols)]
            query, key, value = [pair_rows(mixed, pair, quarter, at) for at in columns]
            tquery, tkey, tvalue = [pair_rows(tmixed, pair, quarter, at) for at in columns]
            prob = probs[pair * heads + head]
            tscores = (dot(tquery, key, NT) + dot(query, tkey, NT)) * SCALE
            tscores = jnp.where(valid, tscores, jnp.float32(0.0))
            total = jnp.sum(tscores * prob, axis=-1, keepdims=True)
            tprob = (prob * (tscores - total)).astype(BF)
            result = dot(tprob, value, NN) + dot(prob.astype(BF), tvalue, NN)
            put_pair(
                tcontext, pair, quarter, slice(head * HEAD, (head + 1) * HEAD), result.astype(BF)
            )

    def project(cut):
        part = dot(tcontext[...], whole[cut, 3 * cols : 4 * cols], NT)
        part = part + dot(context[...], twhole[cut, 3 * cols : 4 * cols], NT)
        halves(part, keep, send, cut)

    tiles(keep.shape[1], project)


def first_norm(x_rel, keep, came, second, params, first, unit, inverse, low):
    own = second.shape[0]
    resid = x_rel[0:own, :].astype(F32) + summed(keep, came, second) + params[1:2, :]
    center = resid - mean_last(resid)
    inv = lax.rsqrt(mean_last(center * center) + EPSILON)
    whitened = center * inv
    unit[...] = whitened
    inverse[...] = jnp.broadcast_to(inv, inverse.shape)
    value = whitened * params[2:3, :] + params[3:4, :]
    first[...] = value
    low[...] = value.astype(BF)


def first_norm_tangent(keep, came, second, params, unit, inverse, tfirst, low):
    along = norm_along(unit[...], inverse[:, 0:1], summed(keep, came, second)) * params[2:3, :]
    tfirst[...] = along
    low[...] = along.astype(BF)


def pack_weights(*refs):
    at, out = 0, refs[-1]
    for ref in refs[:-2]:
        out[:, at : at + ref.shape[1]] = ref[...]
        at = at + ref.shape[1]
    out[:, at:] = refs[-2][...].astype(F32).T.astype(BF)


def collect(pieces, rel):
    quarter = rel.shape[0] // 4
    for i, piece in enumerate(pieces):
        rel[i * quarter : (i + 1) * quarter, :] = piece[0:quarter, :]


def feed_forward(count, hidden, where, params, *refs):
    pieces, refs = refs[:4], refs[4:]
    shards, refs = refs[:count], refs[count:]
    rel, active, slope, keep, send, whole, sems = refs
    copies = shard_copies(where, shards, whole, sems)
    start_all(copies)
    collect(pieces, rel)
    wait_all(copies)

    def up(cut):
        upper = dot(rel[...], whole[:, cut], NN) + params[4:5, cut]
        half = 0.5 + 0.5 * lax.erf(upper * (2.0 ** -0.5))
        active[:, cut] = (upper * half).astype(BF)
        bell = jnp.exp(-0.5 * upper * upper) * 0.3989422804014327
        slope[:, cut] = half + upper * bell

    tiles(hidden, up)

    def down(cut):
        halves(dot(active[...], whole[cut, hidden : 2 * hidden], NT), keep, send, cut)

    tiles(keep.shape[1], down)


def feed_forward_tangent(count, hidden, where, *refs):
    pieces, (rel, active, slope, whole), refs = refs[:4], refs[4:8], refs[8:]
    tshards, refs = refs[:count], refs[count:]
    keep, send, twhole, sems, trel, tactive = refs
    copies = shard_copies(where, tshards, twhole, sems)
    start_all(copies)
    collect(pieces, trel)
    wait_all(copies)

    def up(cut):
        tupper = dot(trel[...], whole[:, cut], NN) + dot(rel[...], twhole[:, cut], NN)
        tactive[:, cut] = (slope[:, cut] * tupper).astype(BF)

    tiles(hidden, up)

    def down(cut):
        part = dot(tactive[...], whole[cut, hidden : 2 * hidden], NT)
        part = part + dot(active[...], twhole[cut, hidden:], NT)
        halves(part, keep, send, cut)

    tiles(keep.shape[1], down)


def second_norm(
    where, keep, came, second, params, first, upstream,
    result, grad, low, unit, inverse,
):
    resid = first[...] + summed(keep, came, second) + params[5:6, :]
    center = resid - mean_last(resid)
    inv = lax.rsqrt(mean_last(center * center) + EPSILON)
    whitened = center * inv
    own = second.shape[0]
    unit[...] = whitened
    inverse[...] = jnp.broadcast_to(inv, inverse.shape)
    result[...] = (whitened * params[6:7, :] + params[7:8, :]).astype(BF)
    back = upstream[pl.ds(pl.multiple_of(where[0] * own, own), own), :].astype(F32)
    value = norm_along(whitened, inv, back * params[6:7, :])
    grad[...] = value
    low[0:own, :] = value.astype(BF)
    low[own:, :] = split_sums([sum_rows(value), sum_rows(back * whitened), sum_rows(back)])


def second_norm_tangent(keep, came, second, params, tfirst, unit, inverse, result):
    along = tfirst[...] + summed(keep, came, second)
    result[...] = (norm_along(unit[...], inverse[:, 0:1], along) * params[6:7, :]).astype(BF)


def first_norm_backward(
    keep, came, second, params, grad_two, unit, inverse, grad, low
):
    back = grad_two[...] + summed(keep, came, second)
    value = norm_along(unit[...], inverse[:, 0:1], back * params[2:3, :])
    own = second.shape[0]
    grad[...] = value
    low[0:own, :] = value.astype(BF)
    low[own:, :] = split_sums([sum_rows(value), sum_rows(back * unit[...]), sum_rows(back)])


def piece_sums(pieces):
    own = pieces[0].shape[0] - EXTRA
    return tree_sum([joined_sums(piece[own:, :]) for piece in pieces])


def feed_forward_backward(hidden, *refs):
    pieces, (slope, whole) = refs[:4], refs[4:6]
    rel, grad_upper, sums, keep, send = refs[6:]
    collect(pieces, rel)
    sums[...] = piece_sums(pieces)

    def down(cut):
        there = pl.ds(pl.multiple_of(cut.start + hidden, cut.size), cut.size)
        value = dot(rel[...], whole[:, there], NN) * slope[:, cut]
        sums[3:4, cut] = sum_rows(value)
        grad_upper[:, cut] = value.astype(BF)

    tiles(hidden, down)

    def up(cut):
        halves(dot(grad_upper[...], whole[cut, :hidden], NT), keep, send, cut)

    tiles(keep.shape[1], up)


def put_owned(groups, where, step, targets, sums):
    if len(targets) == 1:
        targets[0][...] = step[...]
        return
    rows = step.shape[0] // 8
    spare = step.shape[1] - sums.shape[1]
    if spare:
        sums = jnp.concatenate([sums, jnp.zeros((EXTRA // 2, spare), F32)], axis=1)
    extra = split_sums([sums])

    def put(target, at, owner):
        start = pl.multiple_of((where[1] ^ owner) * rows, rows)
        target[at, 0:rows, :] = step[pl.ds(start, rows), :]
        target[at, rows:, :] = extra

    for z in range(4):
        put(targets[0], z, 2 * z)
    for target, group in zip(targets[1:], groups):
        for at, z in enumerate(group):
            put(target, at, 2 * z + 1)


def feed_forward_weights(where, rel, active, first, grad_upper, sums, *refs):
    targets, step = refs[:-1], refs[-1]
    hidden = active.shape[1]

    def one(cut):
        step[cut, :hidden] = dot(rel[:, cut], active[...], TN).astype(BF)
        step[cut, hidden:] = dot(first[:, cut], grad_upper[...], TN).astype(BF)

    tiles(rel.shape[1], one)
    put_owned(FF_GROUPS, where, step, targets, sums[...])


def attention_backward(cols, *refs):
    pieces, (mixed, probs, whole) = refs[:4], refs[4:7]
    rel, grad, sums, keep, send, back = refs[7:]
    collect(pieces, rel)
    sums[...] = piece_sums(pieces)
    quarter = rel.shape[0] // 4
    back[...] = dot(rel[...], whole[:, 3 * cols : 4 * cols], NN).astype(BF)
    heads = cols // HEAD
    for pair in range(2):
        for head in range(heads):
            columns = [slice(at, at + HEAD) for at in range(head * HEAD, 3 * cols, cols)]
            query, key, value = [pair_rows(mixed, pair, quarter, at) for at in columns]
            prob = probs[pair * heads + head]
            grad_context = pair_rows(back, pair, quarter, columns[0])
            grad_value = dot(prob.astype(BF), grad_context, TN)
            grad_prob = dot(grad_context, value, NT)
            total = jnp.sum(grad_prob * prob, axis=-1, keepdims=True)
            grad_score = (prob * (grad_prob - total)).astype(BF)
            put_pair(grad, pair, quarter, columns[2], grad_value.astype(BF))
            grad_query = dot(grad_score, key, NN) * SCALE
            put_pair(grad, pair, quarter, columns[0], grad_query.astype(BF))
            grad_key = dot(grad_score, query, TN) * SCALE
            put_pair(grad, pair, quarter, columns[1], grad_key.astype(BF))

    def project(cut):
        halves(dot(grad[...], whole[cut, : 3 * cols], NT), keep, send, cut)

    tiles(keep.shape[1], project)


def attention_weights(paired, cols, where, rel, grad, sums, x_rel, context, *refs):
    count = 1 + len(LAST_GROUPS) if paired else 1
    targets, refs = refs[:count], refs[count:]
    (step,) = refs[-1:]

    def one(cut):
        step[cut, : 3 * cols] = dot(x_rel[:, cut], grad[...], TN).astype(BF)
        step[cut, 3 * cols :] = dot(rel[:, cut], context[...], TN).astype(BF)

    tiles(x_rel.shape[1], one)
    mixed = sum_rows(grad[...].astype(F32))
    mixed = jnp.concatenate([mixed, jnp.zeros((1, cols), F32)], axis=1)
    lines = jnp.concatenate([sums[0:3, :], mixed])
    put_owned(LAST_GROUPS, where, step, targets, lines)
    if not paired:
        refs[0][...] = lines


def fold_shards(group, keep, came, *outs):
    outs = list(outs)
    for at, z in enumerate(group):
        out = outs.pop(0)
        rows = keep.shape[1] - EXTRA
        total = keep[z, 0:rows, :].astype(F32) + came[at, 0:rows, :].astype(F32)
        sums = joined_sums(keep[z, rows:, :]) + joined_sums(came[at, rows:, :])
        rounded = split_sums([sums])
        if z == 0:
            out[...] = total
            outs.pop(0)[...] = joined_sums(rounded)
        else:
            out[0:rows, :] = total.astype(BF)
            out[rows:, :] = rounded


def last_total(refs):
    rows = refs[0].shape[0]
    total = refs[0][...]
    for ref in refs[1:4]:
        total = total + ref[0:rows, :].astype(F32)
    return total


def last_sums(refs, outs, places):
    rows = refs[0].shape[0]
    sums = tree_sum([refs[4][...]] + [joined_sums(ref[rows:, :]) for ref in refs[1:4]])
    for out, (line, start) in zip(outs, places):
        out[...] = sums[line, start : start + out.shape[0]]


def finish_feed_forward(hidden, *refs):
    total = last_total(refs)
    refs[5][...] = total[:, :hidden]
    refs[6][...] = total[:, hidden:]
    last_sums(refs, refs[7:], [(i, 0) for i in range(4)])


def finish_attention(cols, *refs):
    total = last_total(refs)
    for i in range(3):
        refs[5 + i][...] = total[:, i * cols : (i + 1) * cols]
    refs[8][...] = total[:, 3 * cols :].T
    last_sums(refs, refs[9:], [(0, 0), (1, 0), (2, 0), (3, 0), (3, 2 * cols)])


def last_sum(keep, came, second, grad_one, out):
    out[...] = (grad_one[...] + summed(keep, came, second)).astype(BF)


def place_rows(count, where, *refs):
    pieces, outs, sems = refs[: 4 * count], refs[4 * count : 5 * count], refs[5 * count]
    own = pieces[0].shape[0]
    copies = []
    for i, out in enumerate(outs):
        for j, block in enumerate(BLOCKS):
            start = pl.multiple_of((where[0] ^ block) * own, own)
            copies.append(
                pltpu.make_async_copy(
                    pieces[4 * i + j], out.at[pl.ds(start, own), :], sems.at[4 * i + j]
                )
            )
    start_all(copies)
    wait_all(copies)


def per_device(tp, dp, *arrays):
    (
        layer_input,
        pair_lengths,
        query_weight,
        query_bias,
        key_weight,
        value_weight,
        value_bias,
        out_weight,
        out_bias,
        first_gain,
        first_shift,
        up_weight,
        up_bias,
        down_weight,
        down_bias,
        second_gain,
        second_shift,
        out_grad,
        query_tangent,
        key_tangent,
        value_tangent,
        out_tangent,
        up_tangent,
        down_tangent,
    ) = arrays
    rows, width = layer_input.shape
    cols = query_weight.shape[1]
    hidden = up_weight.shape[1]
    heads = cols // HEAD
    own = rows // tp
    half = rows // 2
    shard = width // dp
    paired = dp == len(SNAKE)

    place = jnp.stack([lax.axis_index("tp"), lax.axis_index("dp")]).astype(jnp.int32)
    where = jnp.concatenate([place, pair_lengths])
    zeros = jnp.zeros((cols,), F32)
    params = jnp.concatenate(
        [query_bias, zeros, value_bias, zeros, out_bias, first_gain, first_shift]
        + [up_bias, down_bias, second_gain, second_shift]
    ).reshape(8, width)
    parts = [((half, width), BF), ((half, width), BF)]
    piece = ((own + EXTRA, width), BF)
    lines = ((EXTRA // 2, width), F32)
    full_own = ((own, width), F32)
    attn_rows = ((width, 4 * cols), BF)
    ff_rows = ((width, 2 * hidden), BF)
    tff_rows = ff_rows

    def pack(first_one, *blocks):
        return jnp.concatenate([first_one, *blocks], 1)

    def arriving(count):
        return pltpu.SemaphoreType.DMA((count,))

    where, out_rows = join((), where, out_weight.T)
    attn = Ring(pack(query_weight, key_weight, value_weight, out_rows), dp)
    attn.step()
    early = attn.parts[-1]
    ff = Ring(pack(after(up_weight, early), down_weight.T), dp)
    group = call(
        pack_weights,
        "pack_weights",
        [((shard, 4 * cols), BF)],
        (after(query_tangent, early), key_tangent, value_tangent, out_tangent),
    )
    tattn = Ring(group[0], dp)
    tff = Ring(pack(after(up_tangent, early), down_tangent.T), dp)
    attn.step()
    join([attn, ff])
    attn.step()
    ff.step()
    join([attn, ff])
    attn.step()
    where, attn.parts[-1] = join([ff], where, attn.parts[-1])
    ff.step()
    count = len(attn.parts)
    x_rel, mixed, probs, context, keep, send, attn_whole = call(
        functools.partial(attention_forward, count, cols),
        "attention_forward",
        [
            ((rows, width), BF),
            ((rows, 3 * cols), BF),
            ((2 * heads, SEQ, SEQ), F32),
            ((rows, cols), BF),
            *parts,
            attn_rows,
        ],
        (where, layer_input, params),
        attn.parts,
        [arriving(count)],
    )
    keep, send = join([ff], keep, send)
    ff.step()
    first, unit_one, inverse_one, first_low = call(
        first_norm,
        "first_norm",
        [full_own, full_own, ((own, 128), F32), ((own, width), BF)],
        (x_rel, *sum_exchange(keep, send, tp), params),
    )
    first_low = join([ff], first_low)
    ff.step()
    pieces = spread_rows(first_low, tp, [ff, tattn])
    tattn.step()
    first_rel, active, slope, keep, send, ff_whole = call(
        functools.partial(feed_forward, count, hidden),
        "feed_forward",
        [((rows, width), BF), ((rows, hidden), BF), ((rows, hidden), F32), *parts, ff_rows],
        (where, params, *pieces),
        ff.parts,
        [arriving(count)],
    )
    keep, send = join([tattn], keep, send)
    tattn.step()
    keep, first_came, second = sum_exchange(keep, send, tp)
    second = join([tattn], second)
    tattn.step()
    result, grad_two, grad_two_low, unit_two, inverse_two = call(
        second_norm,
        "second_norm",
        [((own, width), BF), full_own, piece, full_own, ((own, 128), F32)],
        (where, keep, first_came, second, params, first, out_grad),
    )
    grad_two_low = join([tff], grad_two_low)
    tff.step()
    pieces = spread_rows(grad_two_low, tp, [tattn])
    tattn.step()
    grad_down, grad_upper, sums_up, keep, send = call(
        functools.partial(feed_forward_backward, hidden),
        "feed_forward_backward",
        [((rows, width), BF), ((rows, hidden), BF), lines, *parts],
        (*pieces, slope, ff_whole),
    )
    result_pieces = spread_rows(result, tp)
    keep, send, grad_down, grad_upper, result_pieces[1] = join(
        [tff, tattn], keep, send, grad_down, grad_upper, result_pieces[1]
    )
    tff.step()

    def weight_outs(total, groups):
        if paired:
            counts = [4] + [len(group) for group in groups]
            return [((count, shard + EXTRA, total), BF) for count in counts]
        return [((width, total), BF)]

    def fold(steps, came, group):
        if not paired:
            return came
        total = came.shape[2]
        outs = []
        for z in group:
            if z == 0:
                outs = outs + [((shard, total), F32), ((EXTRA // 2, total), F32)]
            else:
                outs.append(((shard + EXTRA, total), BF))
        return call(functools.partial(fold_shards, group), "fold_shards", outs, (steps[0], came))

    flow = Flow()

    def x_swap(value):
        return lax.ppermute(value, "dp", xor_pairs(dp, 1)) if paired else value

    def z_moves(group):
        def move(values):
            if not paired:
                return values
            moved = [
                lax.ppermute(value, "dp", xor_pairs(dp, 2 * z)) for value, z in zip(values, group) if z
            ]
            return moved + values[len(moved) :]

        return move

    def add_shards(prefix, steps, groups):
        for index, group in enumerate(groups):
            key = prefix + str(index)
            source = steps[1 + index] if paired else steps[0]
            flow.add("x" + key, lambda source=source: source, (), x_swap)

            def folded(came, group=group):
                return fold(steps, came, group)

            flow.add("z" + key, folded, ("x" + key,), z_moves(group))

    def ring_step(values):
        tff.front = values
        tff.step()
        return tff.front

    flow.values["r1"] = tff.front
    for index in (2, 3):
        flow.add(f"r{index}", lambda front: front, (f"r{index - 1}",), ring_step)
    flow.add("a0", lambda: tsend, (), lambda value: swap(value, tp, 1))
    flow.add("a1", lambda came: onward_sum(tkeep, came), ("a0",), lambda value: swap(value, tp, 2))

    def norm_tangent(*_):
        return call(
            first_norm_tangent,
            "first_norm_tangent",
            [full_own, ((own, width), BF)],
            (tkeep, flow.values["a0"], flow.values["a1"], params, unit_one, inverse_one),
        )

    flow.add("n", norm_tangent, ("a1",), lambda values: values)

    first_came = swap(send, tp, 1)
    second = swap(onward_sum(keep, first_came), tp, 2)
    ff_steps = call(
        feed_forward_weights,
        "feed_forward_weights",
        weight_outs(2 * hidden, FF_GROUPS),
        (where, grad_down, active, first_rel, after(grad_upper, first_came), sums_up),
        (),
        [pltpu.VMEM((width, 2 * hidden), BF)],
    )
    add_shards("f", ff_steps, FF_GROUPS)
    flow.point("P0", ff_steps[0])
    tkeep, tsend = call(
        functools.partial(attention_tangent, count, cols),
        "attention_tangent",
        parts,
        (after(where, ff_steps[0]), x_rel, mixed, probs, context, attn_whole),
        tattn.parts,
        [pltpu.VMEM(*attn_rows), arriving(count)]
        + [pltpu.VMEM((rows, 3 * cols), BF), pltpu.VMEM((rows, cols), BF)],
    )
    second, tkeep, tsend, result_pieces = flow.point("P1", second, tkeep, tsend, result_pieces)
    grad_one, grad_one_low = call(
        first_norm_backward,
        "first_norm_backward",
        [full_own, piece],
        (keep, first_came, second, params, grad_two, unit_one, inverse_one),
    )
    grad_one_low = flow.point("P2", grad_one_low)
    across, beside = swap(grad_one_low, tp, 2), swap(grad_one_low, tp, 1)
    across = flow.point("P3", across)
    pieces = [grad_one_low, across, beside, swap(across, tp, 1)]
    pieces[3] = flow.point("P4", pieces[3])
    grad_attn, grad_mixed, sums_one, keep, send = call(
        functools.partial(attention_backward, cols),
        "attention_backward",
        [((rows, width), BF), ((rows, 3 * cols), BF), lines, *parts],
        (*pieces, mixed, probs, attn_whole),
        (),
        [pltpu.VMEM((rows, cols), BF)],
    )
    keep, send = flow.point("P5", keep, send)
    first_came = swap(send, tp, 1)
    last_steps = call(
        functools.partial(attention_weights, paired, cols),
        "attention_weights",
        weight_outs(4 * cols, LAST_GROUPS) + ([] if paired else [lines]),
        (where, grad_attn, grad_mixed, sums_one, x_rel, context),
        (),
        [pltpu.VMEM(*attn_rows)],
    )
    add_shards("l", last_steps, LAST_GROUPS)
    first_came = flow.point("P6", first_came)
    tfirst, tfirst_low = flow.value_of("n")
    flow.add("h0", lambda: tfirst_low, (), lambda value: [swap(value, tp, 2), swap(value, tp, 1)])
    flow.add("h1", lambda both: both[0], ("h0",), lambda value: swap(value, tp, 1))
    first_came = flow.point("P6b", first_came)
    second = swap(onward_sum(keep, first_came), tp, 2)
    second = flow.point("P7", second)
    (grad_input,) = call(
        last_sum, "last_sum", [((own, width), BF)], (keep, first_came, second, grad_one)
    )
    grad_input = flow.point("P8", grad_input)
    across, beside = swap(grad_input, tp, 2), swap(grad_input, tp, 1)
    tkeep, tsend = call(
        functools.partial(feed_forward_tangent, count, hidden),
        "feed_forward_tangent",
        parts,
        (where, tfirst_low, *flow.value_of("h0"), flow.value_of("h1"), first_rel, active, slope, ff_whole),
        tff.parts,
        [pltpu.VMEM(*tff_rows), arriving(count)]
        + [pltpu.VMEM((rows, width), BF), pltpu.VMEM((rows, hidden), BF)],
    )
    across, tkeep, tsend = flow.point("P9", across, tkeep, tsend)
    pieces = [grad_input, across, beside, swap(across, tp, 1)]
    tfirst_came = swap(tsend, tp, 1)
    tfirst_came = flow.point("P10", tfirst_came)
    tsecond = swap(onward_sum(tkeep, tfirst_came), tp, 2)
    tsecond = flow.point("P11", tsecond)
    (tresult,) = call(
        second_norm_tangent,
        "second_norm_tangent",
        [((own, width), BF)],
        (tkeep, tfirst_came, tsecond, params, tfirst, unit_two, inverse_two),
    )
    tresult = flow.point("P12", tresult)
    across, beside = swap(tresult, tp, 2), swap(tresult, tp, 1)
    across = flow.point("P13", across)
    tresult_pieces = [tresult, across, beside, swap(across, tp, 1)]

    def gathered(prefix, groups):
        found = {}
        for index, group in enumerate(groups):
            values = flow.value_of("z" + prefix + str(index))
            if not paired:
                return [values]
            at = 0
            for z in [z for z in group if z]:
                found[z], at = values[at], at + 1
            if 0 in group:
                found[0], found[4] = values[at], values[at + 1]
        return [found[i] for i in range(5)]

    ff_folded, last_folded = gathered("f", FF_GROUPS), gathered("l", LAST_GROUPS)

    def finish(body, name, outs, folded):
        return call(body, name, outs, folded)

    vector = ((width,), F32)
    if paired:
        own_down, own_up, *sums_two = finish(
            functools.partial(finish_feed_forward, hidden),
            "finish_feed_forward",
            [((shard, hidden), F32)] * 2 + [vector] * 4,
            ff_folded,
        )
        *own_mixed, own_out, bias_out, gain_one, shift_one, bias_query, bias_value = finish(
            functools.partial(finish_attention, cols),
            "finish_attention",
            [((shard, cols), F32)] * 3
            + [((cols, shard), F32)]
            + [vector] * 3
            + [((cols,), F32)] * 2,
            last_folded,
        )
        sums_one = [bias_out, gain_one, shift_one]
    else:

        def all_summed(step):
            split = step.reshape(dp, shard, -1)
            came = lax.all_to_all(split, "dp", 0, 0, tiled=True)
            return jnp.sum(came.astype(F32), axis=0)

        own_ff = all_summed(ff_folded[0])
        own_down, own_up = own_ff[:, :hidden], own_ff[:, hidden:]
        last = all_summed(last_folded[0])
        own_mixed = [last[:, i * cols : (i + 1) * cols] for i in range(3)]
        own_out = last[:, 3 * cols :].T
        sums_two = list(lax.psum(sums_up, "dp"))
        *sums_one, mixed_sums = list(lax.psum(last_steps[1], "dp"))
        bias_query, bias_value = mixed_sums[:cols], mixed_sums[2 * cols : 3 * cols]

    def all_rows(*spread):
        return call(
            functools.partial(place_rows, len(spread)),
            "place_rows",
            [((rows, width), BF)] * len(spread),
            (where, *[piece for pieces in spread for piece in pieces]),
            scratch=[arriving(4 * len(spread))],
            any_outs=True,
        )

    whole_result, whole_grad = all_rows(result_pieces, pieces)
    (whole_tresult,) = all_rows(tresult_pieces)
    return (
        whole_result,
        whole_grad,
        whole_tresult,
        own_mixed[0],
        bias_query,
        own_mixed[1],
        own_mixed[2],
        bias_value,
        own_out,
        *sums_one,
        own_up,
        sums_two[3],
        own_down.T,
        *sums_two[:3],
    )


def solution(mesh):
    wide, tall, col, row, full = P("dp", "tp"), P("tp", "dp"), P("tp"), P("dp", None), P()
    placed = (
        (row, P("dp"), wide, col, wide, wide, col, tall, full, full, full, wide, col, tall)
        + (full, full, full, row, wide, wide, wide, tall, wide, tall)
    )
    results = (row, row, row, wide, col, wide, wide, col, tall, full, full, full)
    results = results + (wide, col, tall, full, full, full)
    tp, dp = mesh.shape["tp"], mesh.shape["dp"]

    def body(*arrays):
        return per_device(tp, dp, *arrays)

    return jax.shard_map(
        body, mesh=mesh, in_specs=placed, out_specs=results, check_vma=False
    )
```
